32 devices in a mesh: fsdp: 16 (over z, y, x), tp: 2 (over core).
Axes of the slice: x: 2, y: 2, z: 4, core: 2. Of those that a mesh axis runs over, the one named last changes fastest.
Arguments:
- hidden_in: bfloat16 [8192, 2560], P(('fsdp', 'tp')), may hold values from -67 to 67
- seq_ids: int32 [16, 512], P('fsdp'), may hold values from 0 to 1, never falling along the last dimension, each value on 1 to 384 neighbouring positions
- block_ids: int32 [16, 512], P('fsdp'), may hold values from 0 to 3, never falling along the last dimension, each value on 1 to 256 neighbouring positions
- clip_limit: float32 [1], replicated, may hold values from 6 to 12
- cotangent: bfloat16 [8192, 2560], P(('fsdp', 'tp')), may hold values from -6 to 6
- q_down: bfloat16 [2560, 768], P(('fsdp', 'tp')), may hold values from -0.125 to 0.125
- kv_down: bfloat16 [2560, 288], P(('fsdp', 'tp')), may hold values from -0.125 to 0.125
- q_up: bfloat16 [768, 3840], P('fsdp', 'tp'), may hold values from -1 to 1
- kv_up: bfloat16 [256, 5120], P('fsdp', 'tp'), may hold values from -0.375 to 0.375
- out_proj: bfloat16 [2560, 2560], P('fsdp', 'tp'), may hold values from -0.5 to 0.5
- gate_proj: bfloat16 [2560, 6400], P('fsdp', 'tp'), may hold values from -0.125 to 0.125
- up_proj: bfloat16 [2560, 6400], P('fsdp', 'tp'), may hold values from -0.125 to 0.125
- down_proj: bfloat16 [2560, 6400], P('fsdp', 'tp'), may hold values from -0.15625 to 0.15625
- in_gain: bfloat16 [2560], P(('fsdp', 'tp')), may hold values from 0.5 to 1.5
- q_gain: bfloat16 [768], P(('fsdp', 'tp')), may hold values from 0.5 to 1.5
- kv_gain: bfloat16 [256], P(('fsdp', 'tp')), may hold values from 0.5 to 1.5
- post_gain: bfloat16 [2560], P(('fsdp', 'tp')), may hold values from 0.5 to 1.5
Outputs:
- layer_out: bfloat16 [8192, 2560], P(('fsdp', 'tp'))
- input_grad: float32 [8192, 2560], P(('fsdp', 'tp'))
- q_down_grad: float32 [2560, 768], P(('fsdp', 'tp'))
- kv_down_grad: float32 [2560, 288], P(('fsdp', 'tp'))
- q_up_grad: float32 [768, 3840], P('fsdp', 'tp')
- kv_up_grad: float32 [256, 5120], P('fsdp', 'tp')
- out_proj_grad: float32 [2560, 2560], P('fsdp', 'tp')
- gate_proj_grad: float32 [2560, 6400], P('fsdp', 'tp')
- up_proj_grad: float32 [2560, 6400], P('fsdp', 'tp')
- down_proj_grad: float32 [2560, 6400], P('fsdp', 'tp')
- in_gain_grad: float32 [2560], P(('fsdp', 'tp'))
- q_gain_grad: float32 [768], P(('fsdp', 'tp'))
- kv_gain_grad: float32 [256], P(('fsdp', 'tp'))
- post_gain_grad: float32 [2560], P(('fsdp', 'tp'))
- q_up_clipped: bfloat16 [768, 3840], P('fsdp', 'tp')
- kv_up_clipped: bfloat16 [256, 5120], P('fsdp', 'tp')
- maxima: float32 [40], P('tp')
- factors: float32 [40], P('tp')
The draws below stay inside these ranges and needn't reach their ends.
Inputs may be any that keep to these rules, and one draw needn't show every extreme that they name: `seq_ids`: along each row the ids never fall; each row holds two sequences, each of 128 to 384 tokens. `block_ids`: along each row the ids never fall; a block has 1 to 256 tokens and some block of each row has exactly 256.
All inputs are finite; a program needn't handle non-finite values.
Results may differ from the reference program's by a relative error of at most 0.014.
The reference program's roundings to bfloat16 on the way count: a program that leaves them out, or rounds other values in their place, can miss the bound.
Values may be sent and summed in bfloat16 or wider, within the bound.
A program may use at most 320 MiB of HBM per device.

```python
import math
import jax
import jax.numpy as jnp
import numpy as np
from jax import lax

D = 2560
H = 40
NOPE = 64
ROPE = 32
VD = 64
QR = 768
KVR = 256
FF = 6400
BLOCK = 256
GROUP = 512
GROUPS = 16
TOKENS = 8192


def draw_hidden_in(key, part):
    row_key = jax.random.fold_in(key, 11)
    col_key = jax.random.fold_in(key, 12)
    base_key = jax.random.fold_in(key, 13)
    rows = jnp.exp(jax.random.uniform(row_key, (TOKENS, 1), jnp.float32, -1.2, 1.2))
    cols = jnp.exp(jax.random.uniform(col_key, (1, D), jnp.float32, -1.2, 1.2))
    base = jnp.clip(jax.random.normal(base_key, (TOKENS, D), jnp.float32), -6.0, 6.0)
    return (base * rows * cols).astype(jnp.bfloat16)


def draw_q_up(key, part):
    head_key = jax.random.fold_in(key, 21)
    base_key = jax.random.fold_in(key, 22)
    scales = jnp.exp(jax.random.uniform(head_key, (H, 1), jnp.float32, 0.0, 1.1))
    columns = jnp.broadcast_to(scales, (H, NOPE + ROPE)).reshape(1, H * (NOPE + ROPE))
    base = jnp.clip(jax.random.normal(base_key, (QR, H * (NOPE + ROPE)), jnp.float32), -5.0, 5.0)
    return (base * columns * QR ** (-0.5)).astype(jnp.bfloat16)


def level_of(own_key, extent, cuts, least, high):
    def one(axis_at, blocks):
        steps = jax.random.uniform(jax.random.fold_in(jax.random.fold_in(own_key, 6), axis_at), (blocks,), jnp.float32, least / len(cuts), high / len(cuts))
        return jnp.repeat(jnp.exp(steps), extent[axis_at] // blocks).reshape((-1,) + (1,) * (len(extent) - axis_at - 1))

    level = one(*cuts[0])
    for cut in cuts[1:]:
        level = level * one(*cut)
    return level


def split_up(count, total, reach, lean):
    loads = [(1 << 20) // math.isqrt(standing ** lean) + 1 for standing in range(2, count + 1)]
    surplus, holding = total - reach - (count - 1), [1] * (count - 1)
    while surplus > 0:
        free = [i for i in range(count - 1) if holding[i] < reach]
        pool, budget = sum([loads[i] for i in free]), surplus
        for i in free:
            addition = min(reach - holding[i], max(1, budget * loads[i] // pool), surplus)
            holding[i] = holding[i] + addition
            surplus = surplus - addition
    return np.array([reach] + holding)


def uneven(stream_key, amount, total, most, skew):
    if amount == 2:
        one = jax.random.randint(stream_key, (), max(1, total - most), min(most, total - 1) + 1)
        return jnp.stack([one, total - one])
    lengths = jnp.asarray(split_up(amount, total, most, skew), jnp.int32)
    twos = (amount - 1) // 2
    giver, sink = lengths[1:1 + 2 * twos:2], lengths[2:2 + 2 * twos:2]
    room = jnp.minimum(giver - 1, most - sink)
    passed = jax.random.randint(jax.random.fold_in(stream_key, 1), (twos,), 0, 1 << 20) % (room + 1)
    lengths = lengths.at[1:1 + 2 * twos:2].set(giver - passed).at[2:2 + 2 * twos:2].set(sink + passed)
    return lengths[jax.random.permutation(jax.random.fold_in(stream_key, 2), amount)]


def gaussian(rng, extent, scale, most, split=(), kind=jnp.bfloat16):
    values = jax.random.normal(rng, extent, jnp.float32) * scale
    if len(split) > 0:
        values = level_of(rng, extent, split, -0.22, 0.18) * values
    return jnp.clip(values, min=-most, max=most).astype(kind)


def setup_inputs(seed: int = 0) -> dict:
    seeds = jax.random.split(jax.random.key(seed), 18)
    hidden_in = draw_hidden_in(jax.random.fold_in(seeds[17], 71), 0)
    seq_ids = jax.vmap(lambda own: jnp.searchsorted(jnp.cumsum(uneven(own, 2, GROUP, GROUP - GROUP // 4, 0)), jnp.arange(GROUP), side="right"))(jax.random.split(seeds[1], GROUPS)).reshape((GROUPS, GROUP)).astype(jnp.int32)
    block_ids = jax.vmap(lambda own: jnp.searchsorted(jnp.cumsum(uneven(own, 2 * GROUP // BLOCK, GROUP, BLOCK, 0)), jnp.arange(GROUP), side="right"))(jax.random.split(seeds[2], GROUPS)).reshape((GROUPS, GROUP)).astype(jnp.int32)
    clip_limit = jnp.clip(jax.random.uniform(seeds[3], (1,), jnp.float32, 6.0, 12.0), 6.0, 12.0)
    cotangent = gaussian(seeds[4], (TOKENS, D), 1.0, 6.0, ((0, 32),))
    q_down = gaussian(seeds[5], (D, QR), D ** -0.5, 0.125, ((0, 32),))
    kv_down = gaussian(seeds[6], (D, KVR + ROPE), D ** -0.5, 0.125, ((0, 32),))
    q_up = draw_q_up(jax.random.fold_in(seeds[17], 71), 0)
    kv_up = gaussian(seeds[8], (KVR, H * (NOPE + VD)), KVR ** -0.5, 0.375, ((0, 16), (1, 2)))
    out_proj = gaussian(seeds[9], (D, H * VD), (H * VD // 16) ** -0.5, 0.5, ((0, 16), (1, 2)))
    gate_proj = gaussian(seeds[10], (D, FF), D ** -0.5, 0.125, ((0, 16), (1, 2)))
    up_proj = gaussian(seeds[11], (D, FF), D ** -0.5, 0.125, ((0, 16), (1, 2)))
    down_proj = gaussian(seeds[12], (D, FF), (FF // 4) ** -0.5, 0.15625, ((0, 16), (1, 2)))
    in_gain = jnp.clip(1.0 + 0.1 * jax.random.normal(seeds[13], (D,), jnp.float32), 0.5, 1.5).astype(jnp.bfloat16)
    q_gain = jnp.clip(1.0 + 0.1 * jax.random.normal(seeds[14], (QR,), jnp.float32), 0.5, 1.5).astype(jnp.bfloat16)
    kv_gain = jnp.clip(1.0 + 0.1 * jax.random.normal(seeds[15], (KVR,), jnp.float32), 0.5, 1.5).astype(jnp.bfloat16)
    post_gain = jnp.clip(1.0 + 0.1 * jax.random.normal(seeds[16], (D,), jnp.float32), 0.5, 1.5).astype(jnp.bfloat16)
    return {"hidden_in": hidden_in, "seq_ids": seq_ids, "block_ids": block_ids, "clip_limit": clip_limit, "cotangent": cotangent, "q_down": q_down, "kv_down": kv_down, "q_up": q_up, "kv_up": kv_up, "out_proj": out_proj, "gate_proj": gate_proj, "up_proj": up_proj, "down_proj": down_proj, "in_gain": in_gain, "q_gain": q_gain, "kv_gain": kv_gain, "post_gain": post_gain}


@jax.custom_vjp
def low(v):
    return lax.optimization_barrier(v.astype(jnp.bfloat16)).astype(jnp.float32)

@jax.custom_vjp
def low_back(v):
    return v

def low_keep(v):
    return (low(v), None)

def low_pass(kept, grad):
    return (grad,)

def back_keep(v):
    return (v, None)

def back_low(kept, grad):
    return (low(grad),)
low.defvjp(low_keep, low_pass)
low_back.defvjp(back_keep, back_low)
eps = 1e-05
resid_scale = 1.4 / math.sqrt(62.0)
rope_base = 10000.0
highest = lax.Precision.HIGHEST

def matmul(left, right):
    return jnp.dot(left, right, precision=highest, preferred_element_type=jnp.float32)

def rms_scale(value, gain):
    return value * lax.rsqrt(lax.optimization_barrier(jnp.mean(value * value, axis=-1, keepdims=True)) + eps) * gain

def rotate(value, cosine, sine):
    half = value.shape[-1] // 2
    first = value[..., :half]
    second = value[..., half:]
    return jnp.concatenate([first * cosine - second * sine, second * cosine + first * sine], axis=-1)

def angles(seq_row):
    count = seq_row.shape[0]
    earlier = lax.optimization_barrier(jnp.sum((seq_row[None, :] < seq_row[:, None]).astype(jnp.int32), axis=1))
    place = (jnp.arange(count, dtype=jnp.int32) - earlier).astype(jnp.float32)
    freq = jnp.power(rope_base, -jnp.arange(ROPE // 2, dtype=jnp.float32) * (2.0 / ROPE))
    turn = place[:, None] * freq[None, :]
    return (jnp.cos(turn), jnp.sin(turn))

def group_forward(params, x_float, seq_row, block_row):
    q_down, kv_down, q_up, kv_up, out_proj, gate_proj, up_proj, down_proj, in_gain, q_gain, kv_gain, post_gain = params
    group = x_float.shape[0]
    score_scale = 1.0 / math.sqrt(NOPE + ROPE)
    x_normed = low(rms_scale(x_float, in_gain))
    q_pre = low_back(matmul(x_normed, q_down))
    c_pre = low_back(matmul(x_normed, kv_down))
    q_latent = low(rms_scale(q_pre, q_gain))
    kv_latent = low(rms_scale(c_pre[:, :KVR], kv_gain))
    cosine, sine = angles(seq_row)
    key_rot = low(rotate(c_pre[:, KVR:], cosine, sine))
    q_full = low_back(matmul(q_latent, q_up)).reshape(group, H, NOPE + ROPE).transpose(1, 0, 2)
    kv_full = low_back(matmul(kv_latent, kv_up)).reshape(group, H, NOPE + VD).transpose(1, 0, 2)
    queries = low(jnp.concatenate([q_full[:, :, :NOPE], rotate(q_full[:, :, NOPE:], cosine, sine)], axis=-1))
    keys = jnp.concatenate([low(kv_full[:, :, :NOPE]), jnp.broadcast_to(key_rot[None], (H, group, ROPE))], axis=-1)
    values = low(kv_full[:, :, NOPE:])
    raw = low_back(jnp.einsum('hqd,hkd->hqk', queries, keys, precision=highest))
    scores = raw * score_scale
    allowed = (seq_row[:, None] == seq_row[None, :]) & (block_row[None, :] <= block_row[:, None])
    masked = jnp.where(allowed[None], scores, -1e+30)
    top = lax.optimization_barrier(jnp.max(masked, axis=-1, keepdims=True))
    weights = jnp.exp(masked - top)
    chance = weights / lax.optimization_barrier(jnp.sum(weights, axis=-1, keepdims=True))
    mixed = low_back(jnp.einsum('hqk,hkd->hqd', low(chance), values, precision=highest))
    attn = low(mixed).transpose(1, 0, 2).reshape(group, H * VD)
    branch = low_back(matmul(attn, out_proj.T))
    mid = x_float + resid_scale * branch
    mid_normed = low(rms_scale(mid, post_gain))
    gate = low_back(matmul(mid_normed, gate_proj))
    up_value = low_back(matmul(mid_normed, up_proj))
    act = low(jax.nn.silu(gate) * up_value)
    ffn = low_back(matmul(act, down_proj.T))
    result = mid + resid_scale * ffn
    peak = lax.optimization_barrier(jnp.max(masked, axis=(1, 2)))
    return (result, peak)

def reference(hidden_in, seq_ids, block_ids, clip_limit, cotangent, q_down, kv_down, q_up, kv_up, out_proj, gate_proj, up_proj, down_proj, in_gain, q_gain, kv_gain, post_gain):
    params = tuple((w.astype(jnp.float32) for w in (q_down, kv_down, q_up, kv_up, out_proj, gate_proj, up_proj, down_proj, in_gain, q_gain, kv_gain, post_gain)))
    x_groups = hidden_in.astype(jnp.float32).reshape(GROUPS, GROUP, D)
    cot_groups = cotangent.astype(jnp.float32).reshape(GROUPS, GROUP, D)

    def visit(carry, item):
        sums, peaks = carry
        x_float, cot_float, seq_row, block_row = item

        def forward(weights, inputs):
            return group_forward(weights, inputs, seq_row, block_row)
        result, pullback, peak = jax.vjp(forward, params, x_float, has_aux=True)
        weight_grads, input_grad = pullback(cot_float)
        sums = tuple((a + b for a, b in zip(sums, weight_grads)))
        return ((sums, jnp.maximum(peaks, peak)), (result, input_grad))
    start = (tuple((jnp.zeros_like(w) for w in params)), jnp.full((H,), -1e+30, jnp.float32))
    (sums, peaks), (results, input_grads) = lax.scan(visit, start, (x_groups, cot_groups, seq_ids, block_ids))
    limit = clip_limit[0]
    factors = limit / jnp.maximum(peaks, limit)
    root = jnp.sqrt(factors)
    q_cols = jnp.concatenate([jnp.broadcast_to(root[:, None], (H, NOPE)), jnp.broadcast_to(factors[:, None], (H, ROPE))], axis=1).reshape(H * (NOPE + ROPE))
    kv_cols = jnp.concatenate([jnp.broadcast_to(root[:, None], (H, NOPE)), jnp.ones((H, VD), jnp.float32)], axis=1).reshape(H * (NOPE + VD))
    q_clipped = (params[2] * q_cols[None, :]).astype(jnp.bfloat16)
    kv_clipped = (params[3] * kv_cols[None, :]).astype(jnp.bfloat16)
    layer_out = results.reshape(TOKENS, D).astype(jnp.bfloat16)
    input_grad = input_grads.reshape(TOKENS, D)
    return (layer_out, input_grad, sums[0], sums[1], sums[2], sums[3], sums[4], sums[5], sums[6], sums[7], sums[8], sums[9], sums[10], sums[11], q_clipped, kv_clipped, peaks, factors)
```

```python
import functools
import math

import jax
import jax.numpy as jnp
from jax import lax
from jax.sharding import Mesh
from jax.sharding import PartitionSpec as P

NOPE = 64
ROPE = 32
VD = 64
KVR = 256


eps = 1e-05
resid_scale = 1.4 / math.sqrt(62.0)
rope_base = 10000.0
SWAP = [(0, 1), (1, 0)]
f32 = jnp.float32
bf16 = jnp.bfloat16


def rms_scale(value, gain):
    return value * lax.rsqrt(jnp.mean(value * value, axis=-1, keepdims=True) + eps) * gain


def rotate(value, cosine, sine):
    half = value.shape[-1] // 2
    first = value[..., :half]
    second = value[..., half:]
    return jnp.concatenate(
        [first * cosine - second * sine, second * cosine + first * sine], axis=-1
    )


def angles(seq_row, start, count):
    own_ids = lax.dynamic_slice_in_dim(seq_row, start, count)
    earlier = jnp.sum((seq_row[None, :] < own_ids[:, None]).astype(jnp.int32), axis=1)
    place = (start + jnp.arange(count, dtype=jnp.int32) - earlier).astype(f32)
    freq = jnp.power(rope_base, -jnp.arange(ROPE // 2, dtype=f32) * (2.0 / ROPE))
    turn = place[:, None] * freq[None, :]
    return (jnp.cos(turn), jnp.sin(turn))


def contract(left, right, left_dim, right_dim):
    return lax.dot_general(
        left, right, (((left_dim,), (right_dim,)), ((), ())), preferred_element_type=f32
    )


def attend(items, allowed, score_scale):
    query, key_rows, value_rows = items
    raw = jnp.einsum("hqd,hkd->hqk", query, key_rows, preferred_element_type=f32)
    masked = jnp.where(allowed[None], raw * score_scale, -1e30)
    top = jnp.max(masked, axis=-1, keepdims=True)
    weights = jnp.exp(masked - top)
    total = jnp.sum(weights, axis=-1, keepdims=True)
    mixed = jnp.einsum(
        "hqk,hkd->hqd",
        (weights / total).astype(bf16),
        value_rows,
        preferred_element_type=f32,
    )
    return (
        mixed.astype(bf16),
        top[..., 0] + jnp.log(total[..., 0]),
        jnp.max(top[..., 0], axis=-1),
    )


def attend_back(items, allowed, score_scale):
    query, key_rows, value_rows, d_mixed, log_total = items
    raw = jnp.einsum("hqd,hkd->hqk", query, key_rows, preferred_element_type=f32)
    masked = jnp.where(allowed[None], raw * score_scale, -1e30)
    chance = jnp.exp(masked - log_total[..., None])
    d_values = jnp.einsum("hqk,hqd->hkd", chance.astype(bf16), d_mixed, preferred_element_type=f32)
    d_chance = jnp.einsum("hqd,hkd->hqk", d_mixed, value_rows, preferred_element_type=f32)
    inner = jnp.sum(chance * d_chance, axis=-1, keepdims=True)
    d_raw = (chance * (d_chance - inner) * score_scale).astype(bf16)
    d_query = jnp.einsum("hqk,hkd->hqd", d_raw, key_rows, preferred_element_type=f32)
    d_key_rows = jnp.einsum("hqk,hqd->hkd", d_raw, query, preferred_element_type=f32)
    return (d_query, d_key_rows, d_values)


def swap(value, axis):
    return lax.ppermute(value, axis, SWAP)


def pick(value, at, dim):
    return lax.dynamic_index_in_dim(value, at, dim, keepdims=True)


def both(own, other, axis, dim):
    here = lax.axis_index(axis) == 0
    return jnp.concatenate([jnp.where(here, own, other), jnp.where(here, other, own)], axis=dim)


def gather(block, axes, order):
    held = block.reshape((1,) * len(axes) + block.shape)
    for axis in order:
        held = both(held, swap(held, axis), axis, axes.index(axis))
    return held.reshape((-1,) + block.shape[1:])


def scatter(total, axes, order, rows):
    held = total.reshape((2,) * len(axes) + (rows,) + total.shape[1:])
    for axis in order:
        at = lax.axis_index(axis)
        dim = axes.index(axis)
        sent = pick(held, 1 - at, dim).astype(bf16)
        held = pick(held, at, dim).astype(f32) + swap(sent, axis).astype(f32)
    return held.reshape((rows,) + total.shape[1:])


def shards(
    fsdp,
    hidden_in,
    seq_ids,
    block_ids,
    clip_limit,
    cotangent,
    q_down,
    kv_down,
    q_up,
    kv_up,
    out_proj,
    gate_proj,
    up_proj,
    down_proj,
    in_gain,
    q_gain,
    kv_gain,
    post_gain,
):
    tokens_here, width = hidden_in.shape
    seq_row = seq_ids[0]
    block_row = block_ids[0]
    group = seq_row.shape[0]
    heads = q_up.shape[1] // (NOPE + ROPE)
    stride = math.gcd(heads, 4)
    packs = heads // stride
    score_scale = 1.0 / math.sqrt(NOPE + ROPE)
    first_row = lax.axis_index("c") * tokens_here
    wide, near = fsdp[1], fsdp[-1]
    pair = (wide, near)
    spread = [axis for axis in fsdp if axis not in pair]
    at_wide, at_near = lax.axis_index(wide), lax.axis_index(near)
    diagonal = [(i, 3 - i) for i in range(4)]
    every = fsdp + ["c"]
    out_order = list(fsdp)
    back_order = list(reversed(fsdp))

    small_rows = q_down.shape[0]
    small_cols = q_down.shape[1] + kv_down.shape[1]

    def column(value):
        return jnp.pad(value, (0, small_rows - value.shape[0]))[:, None]

    small = jnp.concatenate(
        [q_down, kv_down, column(in_gain), column(post_gain), column(q_gain), column(kv_gain)],
        axis=1,
    )
    small = jnp.pad(small, ((0, 0), (0, -small.shape[1] % 128)))
    small_full = gather(small, every, every)
    devices = small_full.shape[0] // small_rows

    def gain(at, count):
        return (
            small_full[:, small_cols + at].reshape(devices, small_rows)[:, :count].reshape(-1)
        ).astype(f32)

    in_float = gain(0, in_gain.shape[0])
    post_float = gain(1, post_gain.shape[0])
    q_gain_float = gain(2, q_gain.shape[0])
    kv_gain_float = gain(3, kv_gain.shape[0])
    down_full = small_full[:, :small_cols]

    q_up_full = gather(q_up, fsdp, out_order)
    kv_up_full = gather(kv_up, fsdp, out_order)
    out_full = gather(out_proj, fsdp, out_order)

    def columns_of_chip(weight):
        rows, cols = weight.shape
        parts = weight.reshape(rows, 2, 2, cols // 4).transpose(1, 2, 0, 3)

        def part(w, n):
            return pick(pick(parts, w, 0), n, 1)

        own = part(at_wide, at_near)
        from_near = swap(part(at_wide, 1 - at_near), near)
        from_wide = swap(part(1 - at_wide, at_near), wide)
        from_far = lax.ppermute(part(1 - at_wide, 1 - at_near), pair, diagonal)
        held = both(both(own, from_near, near, 1), both(from_wide, from_far, near, 1), wide, 0)
        shape = [2 if axis in pair else 1 for axis in fsdp]
        held = held.reshape(shape + [rows, cols // 4])
        for axis in spread:
            held = both(held, swap(held, axis), axis, fsdp.index(axis))
        return held.reshape(-1, cols // 4)

    def rows_of_device(total):
        cols = total.shape[1]
        rows = total.shape[0] // 2 ** len(fsdp)
        held = total.reshape([2] * len(fsdp) + [rows, cols])
        for axis in reversed(spread):
            at = lax.axis_index(axis)
            dim = fsdp.index(axis)
            sent = pick(held, 1 - at, dim).astype(bf16)
            held = pick(held, at, dim).astype(f32) + swap(sent, axis).astype(f32)
        parts = held.reshape(2, 2, rows, cols)

        def part(w, n):
            return pick(pick(parts, w, 0), n, 1).astype(bf16)

        own = pick(pick(parts, at_wide, 0), at_near, 1)
        from_near = swap(part(at_wide, 1 - at_near), near).astype(f32)
        from_wide = swap(part(1 - at_wide, at_near), wide).astype(f32)
        from_far = lax.ppermute(part(1 - at_wide, 1 - at_near), pair, diagonal).astype(f32)
        held = both(both(own, from_near, near, 1), both(from_wide, from_far, near, 1), wide, 0)
        return held.transpose(2, 0, 1, 3).reshape(rows, 4 * cols)

    def tokens_of_chips(value):
        chips = [
            value,
            swap(value, near),
            swap(value, wide),
            lax.ppermute(value, pair, diagonal),
        ]
        return jnp.concatenate(chips + [swap(rows, "c") for rows in chips], axis=0)

    def sum_of_chips(value):
        half = value.shape[0] // 2
        other = swap(value[half:].astype(bf16), "c")
        held = (value[:half] + other.astype(f32)).reshape(4, tokens_here, -1)
        sent = held[1:].astype(bf16)
        return (
            held[0]
            + swap(sent[0], near).astype(f32)
            + swap(sent[1], wide).astype(f32)
            + lax.ppermute(sent[2], pair, diagonal).astype(f32)
        )

    def core_both(value):
        return both(value, swap(value, "c"), "c", 0)

    def core_sum(value):
        at = lax.axis_index("c")
        held = value.reshape(2, tokens_here, -1)
        return (pick(held, at, 0) + swap(pick(held, 1 - at, 0), "c"))[0]

    cot_float = cotangent.astype(f32)
    d_ffn = (resid_scale * cot_float).astype(bf16)

    gate_full = columns_of_chip(gate_proj)
    up_full = columns_of_chip(up_proj)
    down_proj_full = columns_of_chip(down_proj)
    d_ffn_all = tokens_of_chips(d_ffn)

    x_float = hidden_in.astype(f32)
    x_normed = rms_scale(x_float, in_float).astype(bf16)
    pre = jnp.dot(x_normed, down_full, preferred_element_type=f32)
    q_rank = q_down.shape[1]
    q_pre = pre[:, :q_rank]
    c_lat_pre = pre[:, q_rank : q_rank + KVR]
    c_rot_pre = pre[:, q_rank + KVR :]
    own_cos, own_sin = angles(seq_row, first_row, tokens_here)
    q_latent = rms_scale(q_pre, q_gain_float).astype(bf16)
    kv_latent = rms_scale(c_lat_pre, kv_gain_float).astype(bf16)
    key_rot = rotate(c_rot_pre, own_cos, own_sin).astype(bf16)
    latents = core_both(jnp.concatenate([q_latent, kv_latent, key_rot], axis=1))
    q_lat_all = latents[:, :q_rank]
    kv_lat_all = latents[:, q_rank : q_rank + KVR]
    key_rot_all = latents[:, q_rank + KVR :]
    all_cos, all_sin = angles(seq_row, 0, group)
    q_full = (
        jnp.dot(q_lat_all, q_up_full, preferred_element_type=f32)
        .reshape(group, heads, NOPE + ROPE)
        .transpose(1, 0, 2)
    )
    kv_full = (
        jnp.dot(kv_lat_all, kv_up_full, preferred_element_type=f32)
        .reshape(group, heads, NOPE + VD)
        .transpose(1, 0, 2)
    )
    queries = jnp.concatenate(
        [q_full[:, :, :NOPE], rotate(q_full[:, :, NOPE:], all_cos, all_sin)], axis=-1
    ).astype(bf16)
    key_rows = jnp.concatenate(
        [
            kv_full[:, :, :NOPE].astype(bf16),
            jnp.broadcast_to(key_rot_all[None], (heads, group, ROPE)),
        ],
        axis=-1,
    )
    value_rows = kv_full[:, :, NOPE:].astype(bf16)
    allowed = (seq_row[:, None] == seq_row[None, :]) & (block_row[None, :] <= block_row[:, None])
    query_packs = queries.reshape(packs, stride, group, NOPE + ROPE)
    key_packs = key_rows.reshape(packs, stride, group, NOPE + ROPE)
    value_packs = value_rows.reshape(packs, stride, group, VD)
    mixed, log_total, local_peak = lax.map(
        functools.partial(attend, allowed=allowed, score_scale=score_scale),
        (query_packs, key_packs, value_packs),
    )
    attn = mixed.reshape(heads, group, VD).transpose(1, 0, 2).reshape(group, heads * VD)
    branch = core_sum(contract(attn, out_full, 1, 1))
    mid = x_float + resid_scale * branch
    mid_normed = rms_scale(mid, post_float).astype(bf16)
    mid_all = tokens_of_chips(mid_normed)
    gate = jnp.dot(mid_all, gate_full, preferred_element_type=f32)
    up_value = jnp.dot(mid_all, up_full, preferred_element_type=f32)
    sigmoid = jax.nn.sigmoid(gate)
    silu_value = gate * sigmoid
    act = (silu_value * up_value).astype(bf16)
    ffn = sum_of_chips(contract(act, down_proj_full, 1, 1))
    layer_out = (mid + resid_scale * ffn).astype(bf16)

    peaks = local_peak.reshape(heads)
    for axis in fsdp:
        peaks = jnp.maximum(peaks, swap(peaks, axis))
    limit = clip_limit[0]
    factors = limit / jnp.maximum(peaks, limit)
    root = jnp.sqrt(factors)
    q_cols = jnp.concatenate(
        [
            jnp.broadcast_to(root[:, None], (heads, NOPE)),
            jnp.broadcast_to(factors[:, None], (heads, ROPE)),
        ],
        axis=1,
    ).reshape(heads * (NOPE + ROPE))
    kv_cols = jnp.concatenate(
        [jnp.broadcast_to(root[:, None], (heads, NOPE)), jnp.ones((heads, VD), f32)], axis=1
    ).reshape(heads * (NOPE + VD))
    q_clipped = (q_up.astype(f32) * q_cols[None, :]).astype(bf16)
    kv_clipped = (kv_up.astype(f32) * kv_cols[None, :]).astype(bf16)

    d_act = jnp.dot(d_ffn_all, down_proj_full, preferred_element_type=f32)
    d_gate = (d_act * up_value * (sigmoid * (1.0 + gate * (1.0 - sigmoid)))).astype(bf16)
    d_up = (d_act * silu_value).astype(bf16)
    d_mid_normed = sum_of_chips(contract(d_gate, gate_full, 1, 1) + contract(d_up, up_full, 1, 1))
    down_out = rows_of_device(contract(d_ffn_all, act, 0, 0))
    gate_out = rows_of_device(contract(mid_all, d_gate, 0, 0))
    up_out = rows_of_device(contract(mid_all, d_up, 0, 0))
    post_pull = jax.vjp(rms_scale, mid, post_float)[1]
    d_mid_norm, post_grad = post_pull(d_mid_normed)
    d_mid = cot_float + d_mid_norm
    d_branch = (resid_scale * d_mid).astype(bf16)
    d_branch_all = core_both(d_branch)
    out_grad = contract(d_branch_all, attn, 0, 0)
    out_out = scatter(out_grad, fsdp, back_order, out_proj.shape[0])
    d_attn = jnp.dot(d_branch_all, out_full, preferred_element_type=f32).astype(bf16)
    d_mixed = d_attn.reshape(group, heads, VD).transpose(1, 0, 2).reshape(packs, stride, group, VD)
    d_query, d_key_rows, d_values = lax.map(
        functools.partial(attend_back, allowed=allowed, score_scale=score_scale),
        (query_packs, key_packs, value_packs, d_mixed, log_total),
    )
    d_query = d_query.reshape(heads, group, NOPE + ROPE)
    d_key_rows = d_key_rows.reshape(heads, group, NOPE + ROPE)
    d_values = d_values.reshape(heads, group, VD)
    d_q_rot = rotate(d_query[:, :, NOPE:], all_cos, -all_sin)
    d_q = (
        jnp.concatenate([d_query[:, :, :NOPE], d_q_rot], axis=-1)
        .transpose(1, 0, 2)
        .reshape(group, heads * (NOPE + ROPE))
        .astype(bf16)
    )
    d_key_rot_part = jnp.sum(d_key_rows[:, :, NOPE:], axis=0)
    d_kv = (
        jnp.concatenate([d_key_rows[:, :, :NOPE], d_values], axis=-1)
        .transpose(1, 0, 2)
        .reshape(group, heads * (NOPE + VD))
        .astype(bf16)
    )
    q_up_grad = contract(q_lat_all, d_q, 0, 0)
    kv_up_grad = contract(kv_lat_all, d_kv, 0, 0)
    q_up_out = scatter(q_up_grad, fsdp, back_order, q_up.shape[0])
    kv_up_out = scatter(kv_up_grad, fsdp, back_order, kv_up.shape[0])
    d_q_lat_part = contract(d_q, q_up_full, 1, 1)
    d_kv_lat_part = contract(d_kv, kv_up_full, 1, 1)
    d_latents = core_sum(
        jnp.concatenate([d_q_lat_part, d_kv_lat_part, d_key_rot_part], axis=1)
    )
    q_pull = jax.vjp(rms_scale, q_pre, q_gain_float)[1]
    d_q_pre, q_gain_grad = q_pull(d_latents[:, :q_rank])
    kv_pull = jax.vjp(rms_scale, c_lat_pre, kv_gain_float)[1]
    d_c_lat, kv_gain_grad = kv_pull(d_latents[:, q_rank : q_rank + KVR])
    d_pre = jnp.concatenate(
        [d_q_pre, d_c_lat, rotate(d_latents[:, q_rank + KVR :], own_cos, -own_sin)], axis=-1
    ).astype(bf16)
    down_grads = contract(x_normed, d_pre, 0, 0)
    d_x_normed = contract(d_pre, down_full, 1, 1)
    in_pull = jax.vjp(rms_scale, x_float, in_float)[1]
    d_x_norm, in_grad = in_pull(d_x_normed)
    input_grad = d_mid + d_x_norm

    def spread_out(value):
        rows = value.reshape(devices, -1)
        return jnp.pad(rows, ((0, 0), (0, small_rows - rows.shape[1]))).reshape(-1, 1)

    small_grads = jnp.concatenate(
        [
            down_grads,
            spread_out(in_grad),
            spread_out(post_grad),
            spread_out(q_gain_grad),
            spread_out(kv_gain_grad),
        ],
        axis=1,
    )
    small_out = scatter(small_grads, every, ["c"] + back_order, small_rows)
    return (
        layer_out,
        input_grad,
        small_out[:, :q_rank],
        small_out[:, q_rank:small_cols],
        q_up_out,
        kv_up_out,
        out_out,
        gate_out,
        up_out,
        down_out,
        small_out[: in_gain.shape[0], small_cols],
        small_out[: q_gain.shape[0], small_cols + 2],
        small_out[: kv_gain.shape[0], small_cols + 3],
        small_out[: post_gain.shape[0], small_cols + 1],
        q_clipped,
        kv_clipped,
        peaks,
        factors,
    )


def solution(mesh):
    bits = mesh.shape["fsdp"].bit_length() - 1
    fsdp = [f"f{i}" for i in range(bits)]
    fine = Mesh(mesh.devices.reshape((2,) * (bits + 1)), tuple(fsdp) + ("c",))
    split = tuple(fsdp)
    whole = split + ("c",)
    return jax.shard_map(
        functools.partial(shards, fsdp),
        mesh=fine,
        in_specs=(
            P(whole, None),
            P(split, None),
            P(split, None),
            P(),
            P(whole, None),
            P(whole, None),
            P(whole, None),
            P(split, "c"),
            P(split, "c"),
            P(split, "c"),
            P(split, "c"),
            P(split, "c"),
            P(split, "c"),
            P(whole),
            P(whole),
            P(whole),
            P(whole),
        ),
        out_specs=(
            P(whole, None),
            P(whole, None),
            P(whole, None),
            P(whole, None),
            P(split, "c"),
            P(split, "c"),
            P(split, "c"),
            P(split, "c"),
            P(split, "c"),
            P(split, "c"),
            P(whole),
            P(whole),
            P(whole),
            P(whole),
            P(split, "c"),
            P(split, "c"),
            P("c"),
            P("c"),
        ),
        check_vma=False,
    )
```

```python
import functools
import math

import jax
import jax.numpy as jnp
from jax import lax
from jax.experimental import pallas as pl
from jax.experimental.pallas import tpu as pltpu
from jax.experimental.layout import Layout, with_layout_constraint
from jax.sharding import Mesh
from jax.sharding import PartitionSpec as P

NOPE = 64
ROPE = 32
VD = 64
KVR = 256
TILE = 128


eps = 1e-05
resid_scale = 1.4 / math.sqrt(62.0)
rope_base = 10000.0
SWAP = [(0, 1), (1, 0)]
f32 = jnp.float32
bf16 = jnp.bfloat16


def rms_scale(value, gain):
    return value * lax.rsqrt(jnp.mean(value * value, axis=-1, keepdims=True) + eps) * gain


def rotate(value, cosine, sine):
    half = value.shape[-1] // 2
    first = value[..., :half]
    second = value[..., half:]
    return jnp.concatenate(
        [first * cosine - second * sine, second * cosine + first * sine], axis=-1
    )


def angles(seq_row, start, count):
    own_ids = lax.dynamic_slice_in_dim(seq_row, start, count)
    earlier = jnp.sum((seq_row[None, :] < own_ids[:, None]).astype(jnp.int32), axis=1)
    place = (start + jnp.arange(count, dtype=jnp.int32) - earlier).astype(f32)
    freq = jnp.power(rope_base, -jnp.arange(ROPE // 2, dtype=f32) * (2.0 / ROPE))
    turn = place[:, None] * freq[None, :]
    return (jnp.cos(turn), jnp.sin(turn))


def contract(left, right, left_dim, right_dim):
    return lax.dot_general(
        left, right, (((left_dim,), (right_dim,)), ((), ())), preferred_element_type=f32
    )


def turn(value, plain, first, second):
    return (
        value * plain
        + pltpu.roll(value, TILE - ROPE // 2, 1) * first
        + pltpu.roll(value, ROPE // 2, 1) * second
    )


def tables(cosine, sine):
    rows = cosine.shape[0]
    half = ROPE // 2

    def zeros(count):
        return jnp.zeros((rows, count), f32)

    plain = jnp.concatenate([jnp.ones((rows, NOPE), f32), cosine, cosine, zeros(TILE - NOPE - ROPE)], axis=1)
    first = jnp.concatenate([zeros(NOPE), -sine, zeros(TILE - NOPE - half)], axis=1)
    second = jnp.concatenate([zeros(NOPE + half), sine, zeros(TILE - NOPE - ROPE)], axis=1)
    return plain, first, second


def attend_kernel(
    scale,
    q_ref,
    kv_ref,
    rot_ref,
    plain_ref,
    first_ref,
    second_ref,
    bias_ref,
    mixed_ref,
    query_ref,
    total_ref,
    peak_ref,
):
    step = pl.program_id(0)
    lane = lax.broadcasted_iota(jnp.int32, (q_ref.shape[0], TILE), 1)
    spot = lax.broadcasted_iota(jnp.int32, peak_ref.shape, 1)

    @pl.when(step == 0)
    def _():
        peak_ref[...] = jnp.zeros_like(peak_ref)

    outs = []
    for one in range(2):
        cols = slice(one * TILE, (one + 1) * TILE)
        query = turn(q_ref[:, cols], plain_ref[...], first_ref[...], second_ref[...]).astype(bf16)
        query_ref[:, cols] = query
        kv = kv_ref[:, cols]
        keys = jnp.where(lane < NOPE, kv, rot_ref[...])
        masked = contract(keys, query, 1, 1) * scale + bias_ref[...]
        top = jnp.max(masked, axis=0, keepdims=True)
        weights = jnp.exp(masked - top)
        total = jnp.sum(weights, axis=0, keepdims=True)
        chance = (weights * (1.0 / total)).astype(bf16)
        outs.append(contract(chance, kv, 0, 0))
        total_ref[0, one : one + 1, :] = top + jnp.log(total)
        peak_ref[...] = jnp.where(spot == step * 2 + one, jnp.max(top), peak_ref[...])
    mixed_ref[...] = jnp.where(lane < VD, pltpu.roll(outs[0], VD, 1), outs[1]).astype(bf16)


def attend(q, kv, rot, turns, bias, scale):
    group, cols = q.shape
    heads = cols // TILE
    whole = pl.BlockSpec((group, TILE), lambda i: (0, 0))
    two = pl.BlockSpec((group, 2 * TILE), lambda i: (0, i))
    return pl.pallas_call(
        functools.partial(attend_kernel, scale),
        grid=(heads // 2,),
        out_shape=(
            jax.ShapeDtypeStruct((group, heads * VD), bf16),
            jax.ShapeDtypeStruct((group, cols), bf16),
            jax.ShapeDtypeStruct((heads // 2, 2, group), f32),
            jax.ShapeDtypeStruct((8, TILE), f32),
        ),
        in_specs=[two, two, whole, whole, whole, whole, pl.BlockSpec((group, group), lambda i: (0, 0))],
        out_specs=(
            pl.BlockSpec((group, TILE), lambda i: (0, i)),
            two,
            pl.BlockSpec((1, 2, group), lambda i: (i, 0, 0)),
            pl.BlockSpec((8, TILE), lambda i: (0, 0)),
        ),
        compiler_params=pltpu.CompilerParams(
            dimension_semantics=("arbitrary",), vmem_limit_bytes=40 << 20
        ),
        cost_estimate=pl.CostEstimate(
            flops=4 * heads * group * group * TILE,
            transcendentals=heads * group * group,
            bytes_accessed=12 * group * cols,
        ),
    )(q, kv, rot, *turns, bias)


def attend_back_kernel(
    scale,
    query_ref,
    kv_ref,
    d_mixed_ref,
    total_ref,
    rot_ref,
    plain_ref,
    first_ref,
    second_ref,
    bias_ref,
    d_q_ref,
    d_kv_ref,
    d_rot_ref,
):
    step = pl.program_id(0)
    lane = lax.broadcasted_iota(jnp.int32, (query_ref.shape[0], TILE), 1)

    @pl.when(step == 0)
    def _():
        d_rot_ref[...] = jnp.zeros_like(d_rot_ref)

    pair = d_mixed_ref[...].astype(f32)
    for one in range(2):
        cols = slice(one * TILE, (one + 1) * TILE)
        query = query_ref[:, cols]
        kv = kv_ref[:, cols]
        keys = jnp.where(lane < NOPE, kv, rot_ref[...])
        own = pair if one else pltpu.roll(pair, VD, 1)
        d_mixed = jnp.where(lane < VD, 0.0, own).astype(bf16)
        masked = contract(keys, query, 1, 1) * scale + bias_ref[...]
        chance = jnp.exp(masked - total_ref[0, one : one + 1, :])
        d_values = contract(chance.astype(bf16), d_mixed, 1, 0)
        d_chance = contract(kv, d_mixed, 1, 1)
        inner = jnp.sum(chance * d_chance, axis=0, keepdims=True)
        d_raw = (chance * (d_chance - inner) * scale).astype(bf16)
        d_keys = contract(d_raw, query, 1, 0)
        d_query = contract(d_raw, keys, 0, 0)
        d_q_ref[:, cols] = turn(
            d_query, plain_ref[...], first_ref[...], second_ref[...]
        ).astype(bf16)
        d_kv_ref[:, cols] = jnp.where(lane < NOPE, d_keys, d_values).astype(bf16)
        d_rot_ref[...] += d_keys


def attend_back(query, kv, d_mixed, total, rot, turns, bias, scale):
    group, cols = query.shape
    heads = cols // TILE
    whole = pl.BlockSpec((group, TILE), lambda i: (0, 0))
    two = pl.BlockSpec((group, 2 * TILE), lambda i: (0, i))
    return pl.pallas_call(
        functools.partial(attend_back_kernel, scale),
        grid=(heads // 2,),
        out_shape=(
            jax.ShapeDtypeStruct((group, cols), bf16),
            jax.ShapeDtypeStruct((group, cols), bf16),
            jax.ShapeDtypeStruct((group, TILE), f32),
        ),
        in_specs=[
            two,
            two,
            pl.BlockSpec((group, TILE), lambda i: (0, i)),
            pl.BlockSpec((1, 2, group), lambda i: (i, 0, 0)),
            whole,
            whole,
            whole,
            whole,
            pl.BlockSpec((group, group), lambda i: (0, 0)),
        ],
        out_specs=(two, two, whole),
        compiler_params=pltpu.CompilerParams(
            dimension_semantics=("arbitrary",), vmem_limit_bytes=40 << 20
        ),
        cost_estimate=pl.CostEstimate(
            flops=10 * heads * group * group * TILE,
            transcendentals=heads * group * group,
            bytes_accessed=8 * group * cols,
        ),
    )(query, kv, d_mixed, total, rot, *turns, bias)


def swap(value, axis):
    return lax.ppermute(value, axis, SWAP)


def far(value, pair):
    return lax.ppermute(value, pair, [(i, 3 - i) for i in range(4)])


def after(value, *others):
    return lax.optimization_barrier((value,) + others)[0]


def pick(value, at, dim):
    return lax.dynamic_index_in_dim(value, at, dim, keepdims=True)


def both(own, other, axis, dim):
    here = lax.axis_index(axis) == 0
    return jnp.concatenate([jnp.where(here, own, other), jnp.where(here, other, own)], axis=dim)


def heads_grad_kernel(latent_ref, d_ref, out_ref):
    total = contract(latent_ref[...], d_ref[...], 0, 0)
    parts = [total[:, i * TILE : i * TILE + NOPE + ROPE] for i in range(4)]
    out_ref[...] = jnp.concatenate(parts, axis=1).astype(bf16)


def heads_grad(latent, d_heads):
    group, rank = latent.shape
    packs = d_heads.shape[1] // (4 * TILE)
    cols = 4 * (NOPE + ROPE)
    return pl.pallas_call(
        heads_grad_kernel,
        grid=(packs,),
        out_shape=jax.ShapeDtypeStruct((rank, packs * cols), bf16),
        in_specs=[
            pl.BlockSpec((group, rank), lambda i: (0, 0)),
            pl.BlockSpec((group, 4 * TILE), lambda i: (0, i)),
        ],
        out_specs=pl.BlockSpec((rank, cols), lambda i: (0, i)),
        compiler_params=pltpu.CompilerParams(vmem_limit_bytes=32 << 20),
        cost_estimate=pl.CostEstimate(
            flops=2 * group * rank * packs * 4 * TILE,
            transcendentals=0,
            bytes_accessed=2 * (group * packs * 4 * TILE + rank * packs * cols),
        ),
    )(latent, d_heads)


def rows_first(value):
    return with_layout_constraint(value, Layout(major_to_minor=(0, 1)))


def square_scatter(held, first, second, dim):
    here, there = lax.axis_index(first), lax.axis_index(second)

    def part(w, n):
        return pick(pick(held, w, dim), n, dim + 1)

    near = swap(part(here, 1 - there).astype(bf16), second)
    wide = swap(part(1 - here, there).astype(bf16), first)
    corner = far(part(1 - here, 1 - there).astype(bf16), (first, second))
    own = part(here, there).astype(f32)
    return own + near.astype(f32) + wide.astype(f32) + corner.astype(f32)


def place_of(first, second):
    return lax.axis_index(first) * 2 + lax.axis_index(second)


def other_of(axes):
    return {axis: 1 - lax.axis_index(axis) for axis in axes}


def meet(partners):
    barrier = pltpu.get_barrier_semaphore()
    for axes in partners:
        pl.semaphore_signal(
            barrier, inc=1, device_id=other_of(axes), device_id_type=pl.DeviceIdType.MESH
        )
    pl.semaphore_wait(barrier, len(partners))


class Sender:
    def __init__(self, send_sems, recv_sems):
        self.send_sems, self.recv_sems, self.all, self.left = send_sems, recv_sems, [], []

    def start(self, source, target, axes):
        copy = pltpu.make_async_remote_copy(
            src_ref=source,
            dst_ref=target,
            send_sem=self.send_sems.at[len(self.all)],
            recv_sem=self.recv_sems.at[len(self.all)],
            device_id=other_of(axes),
            device_id_type=pl.DeviceIdType.MESH,
        )
        copy.start()
        self.all.append(copy)
        return copy

    def finish(self):
        for copy in self.all:
            if all(copy is not other for other in self.left):
                copy.wait_send()


def first_kernel(
    squares,
    pair,
    spread,
    small_ref,
    gains_ref,
    q_ref,
    kv_ref,
    gate_ref,
    up_ref,
    down_ref,
    small_out,
    gains_out,
    q_out,
    kv_out,
    gate_out,
    others_out,
    staged,
    send_sems,
    recv_sems,
):
    core = lax.axis_index("c")
    places = [place_of(*square) for square in squares]
    me = place_of(*pair)
    sender = Sender(send_sems, recv_sems)
    cols = staged.shape[3]

    small_out[(*places, core)] = small_ref[...]
    gains_out[(*places, core)] = gains_ref[...]
    q_out[tuple(places)] = q_ref[...]
    kv_out[tuple(places)] = kv_ref[...]
    partners = [axes for one, two in squares for axes in ((two,), (one,), (one, two))]
    meet(partners + [pair, ("c",)])

    def blocks(ref, stage, place, tail, lead=()):
        index = lead + (slice(None),) * (stage - len(lead)) + (place,) + tuple(places[stage + 1 :])
        return ref.at[index + tail]

    early = [(small_out, (core,)), (gains_out, (core,))]
    later = [(q_out, ()), (kv_out, ())]

    def send_first(ref, tail):
        mine = blocks(ref, 0, places[0], tail)
        return [sender.start(mine, mine, axes) for axes in partners[:3]]

    def send_square(ref, tail, stage):
        one, two = squares[stage]
        mine = blocks(ref, stage, places[stage], tail)
        return [sender.start(mine, mine, (two,)), sender.start(mine, mine, (one,))]

    def pass_on(ref, tail, stage, copies):
        one, two = squares[stage]
        copies[0].wait_recv()
        half = blocks(ref, stage, places[stage] ^ 1, tail, (slice(0, 2),))
        first = sender.start(half, half, (one,))
        copies[1].wait_recv()
        half = blocks(ref, stage, places[stage] ^ 2, tail, (slice(2, 4),))
        return [first, sender.start(half, half, (two,))]

    def wait(copies):
        for copy in copies:
            copy.wait_recv()

    targets = (gate_out.at[0], others_out.at[0], others_out.at[1])

    def send_columns(away, axes):
        return [
            sender.start(staged.at[which, me ^ away], target.at[me], axes)
            for which, target in enumerate(targets)
        ]

    first = [send_first(*item) for item in early]
    for which, weight_ref in enumerate((gate_ref, up_ref, down_ref)):
        for quarter in range(4):
            staged[which, quarter] = weight_ref[:, quarter * cols : (quarter + 1) * cols]
    columns = [send_columns(1, (pair[1],))]
    for which, target in enumerate(targets):
        target[me] = staged[which, me]
    for copies in first:
        wait(copies)
    sent = [send_square(*item, 1) for item in early]
    first_later = [send_first(*item) for item in later]
    columns.append(send_columns(2, (pair[0],)))
    for stage in range(1, len(squares)):
        if stage > 1:
            sent = [send_square(*item, stage) for item in early]
        passed = [pass_on(*item, stage, copies) for item, copies in zip(early, sent)]
        if stage == 1:
            for copies in first_later:
                wait(copies)
            sent_later = [send_square(*item, 1) for item in later]
            columns.append(send_columns(3, pair))
        for copies in passed:
            wait(copies)
    mine = (slice(None),) * len(squares) + (core,)
    core_sent = [sender.start(ref.at[mine], ref.at[mine], ("c",)) for ref, _ in early]
    for copies in columns:
        copies[0].wait_recv()
    gate_over = [sender.start(gate_out.at[0], gate_out.at[1], (spread[0],))]
    for stage in range(1, len(squares)):
        if stage > 1:
            sent_later = [send_square(*item, stage) for item in later]
        passed = [pass_on(*item, stage, copies) for item, copies in zip(later, sent_later)]
        for copies in passed:
            wait(copies)
    wait(core_sent)
    for copies in columns:
        wait(copies[1:])
    wait(gate_over)
    sender.finish()


def first_gather(squares, pair, spread, small, gains, q_up, kv_up, gate, up, down):
    vmem = pl.BlockSpec(memory_space=pltpu.VMEM)
    rows, cols = gate.shape
    lead = (4,) * len(squares)
    copies = 12 + 16 * (len(squares) - 1) + 2 + 9 + 1
    return pl.pallas_call(
        functools.partial(first_kernel, squares, pair, spread),
        out_shape=(
            jax.ShapeDtypeStruct(lead + (2,) + small.shape, bf16),
            jax.ShapeDtypeStruct(lead + (2,) + gains.shape, bf16),
            jax.ShapeDtypeStruct(lead + q_up.shape, bf16),
            jax.ShapeDtypeStruct(lead + kv_up.shape, bf16),
            jax.ShapeDtypeStruct((2, 4, rows, cols // 4), bf16),
            jax.ShapeDtypeStruct((2, 4, rows, cols // 4), bf16),
        ),
        in_specs=[vmem] * 7,
        out_specs=(vmem,) * 6,
        scratch_shapes=[
            pltpu.VMEM((3, 4, rows, cols // 4), bf16),
            pltpu.SemaphoreType.DMA((copies,)),
            pltpu.SemaphoreType.DMA((copies,)),
        ],
        compiler_params=pltpu.CompilerParams(
            collective_id=0, has_side_effects=True, vmem_limit_bytes=48 << 20
        ),
    )(small, gains, q_up, kv_up, gate, up, down)


def lay_copies(fsdp, pair, spread, pieces, target, sems):
    copies = []
    for number, piece in enumerate(pieces):
        for block in range(4):
            place = 0
            for axis in fsdp:
                if axis == pair[0]:
                    bit = block >> 1
                elif axis == pair[1]:
                    bit = block & 1
                else:
                    bit = lax.axis_index(axis) ^ ((number >> spread.index(axis)) & 1)
                place = place * 2 + bit
            copies.append(pltpu.make_async_copy(piece.at[block], target.at[place], sems.at[len(copies)]))
    for copy in copies:
        copy.start()
    return copies


def lay_kernel(fsdp, pair, spread, *refs):
    count = 2 ** len(spread)
    target, sems = refs[count:]
    for copy in lay_copies(fsdp, pair, spread, refs[:count], target, sems):
        copy.wait()


def lay(pieces, fsdp, pair, spread):
    rows, cols = pieces[0].shape[1:]
    blocks = 4 * len(pieces)
    out = pl.pallas_call(
        functools.partial(lay_kernel, fsdp, pair, spread),
        out_shape=jax.ShapeDtypeStruct((blocks, rows, cols), bf16),
        in_specs=[pl.BlockSpec(memory_space=pltpu.HBM)] * len(pieces),
        out_specs=pl.BlockSpec(memory_space=pltpu.VMEM),
        scratch_shapes=[pltpu.SemaphoreType.DMA((blocks,))],
        compiler_params=pltpu.CompilerParams(vmem_limit_bytes=32 << 20),
        cost_estimate=pl.CostEstimate(
            flops=0, transcendentals=0, bytes_accessed=4 * blocks * rows * cols
        ),
    )(*pieces)
    return out.reshape(blocks * rows, cols)


def tokens_kernel(pair, value_ref, out_ref, send_sems, recv_sems):
    core = lax.axis_index("c")
    me = place_of(*pair)
    one, two = pair
    half = value_ref.shape[0] // 2
    sender = Sender(send_sems, recv_sems)
    out_ref[me, core] = value_ref[...]
    meet([(two,), (one,), ("c",)])

    def send(place, axes, rows=slice(None)):
        mine = out_ref.at[place, core, rows]
        return sender.start(mine, mine, axes)

    near = send(me, (two,))
    wide = send(me, (one,))
    got = [send(me, ("c",))]
    near.wait_recv()
    far = [send(me ^ 1, (one,), slice(0, half))]
    got.append(send(me ^ 1, ("c",)))
    wide.wait_recv()
    far.append(send(me ^ 2, (two,), slice(half, 2 * half)))
    got.append(send(me ^ 2, ("c",)))
    for copy in far:
        copy.wait_recv()
    got.append(send(me ^ 3, ("c",)))
    for copy in got:
        copy.wait_recv()
    sender.finish()


def tokens_of_chips(value, pair):
    rows, cols = value.shape
    vmem = pl.BlockSpec(memory_space=pltpu.VMEM)
    out = pl.pallas_call(
        functools.partial(tokens_kernel, pair),
        out_shape=jax.ShapeDtypeStruct((4, 2, rows, cols), bf16),
        in_specs=[vmem],
        out_specs=vmem,
        scratch_shapes=[pltpu.SemaphoreType.DMA((8,)), pltpu.SemaphoreType.DMA((8,))],
        compiler_params=pltpu.CompilerParams(
            collective_id=1, has_side_effects=True, vmem_limit_bytes=24 << 20
        ),
    )(value)
    return out.reshape(8 * rows, cols)


def merge_kernel(which, parts_ref, out_ref):
    cols = out_ref.shape[1] // 4
    for quarter in range(4):
        out_ref[:, quarter * cols : (quarter + 1) * cols] = parts_ref[0, quarter].astype(f32)


def merge(parts, which):
    rows, cols = parts.shape[2:]
    return pl.pallas_call(
        functools.partial(merge_kernel, which),
        grid=(1,),
        out_shape=jax.ShapeDtypeStruct((rows, 4 * cols), f32),
        in_specs=[pl.BlockSpec((1, 4, rows, cols), lambda i: (which, 0, 0, 0))],
        out_specs=pl.BlockSpec((rows, 4 * cols), lambda i: (0, 0)),
        cost_estimate=pl.CostEstimate(
            flops=0, transcendentals=0, bytes_accessed=24 * rows * cols
        ),
    )(parts)


class Reduction:
    def __init__(self, sender, held, dims, order, buffers, out):
        self.sender, self.held, self.dims, self.order = sender, held, list(dims), list(order)
        self.buffers, self.out = list(buffers), out

    def half(self, at):
        return (slice(None),) * self.dims.index(self.order[0]) + (at,)

    def begin(self):
        axis = self.order[0]
        source = self.held.at[self.half(1 - lax.axis_index(axis))]
        self.copy = self.sender.start(source, self.buffers[0], (axis,))

    def end(self):
        self.copy.wait_recv()
        axis = self.order[0]
        own = self.held[self.half(lax.axis_index(axis))]
        total = own.astype(f32) + self.buffers[0][...].astype(f32)
        self.held = self.buffers.pop(0)
        self.dims.remove(axis)
        self.order.pop(0)
        if self.order:
            self.held[...] = total.astype(bf16)
            self.begin()
        else:
            self.out[...] = total

    def finish(self):
        while self.order:
            self.end()


def halves_of(rows):
    half = rows // 2 // 16 * 16
    return pl.ds(0, half), pl.ds(half, rows - half)


def last_kernel(
    fsdp,
    pair,
    peak_ref,
    small_ref,
    gains_ref,
    q_ref,
    kv_ref,
    out_ref,
    down_ref,
    gate_ref,
    up_ref,
    small_sum,
    gains_sum,
    q_sum,
    kv_sum,
    out_sum,
    ffn_out,
    peak_out,
    *scratch,
):
    scratch = list(scratch)
    stages = len(fsdp)
    sender = Sender(scratch.pop(), scratch.pop())

    def buffers(count):
        taken = scratch[:count]
        del scratch[:count]
        return taken

    down = list(reversed(fsdp))
    turned = [down[1], down[0]] + down[2:]
    with_core = fsdp + ["c"]
    small = Reduction(sender, small_ref, with_core, ["c"] + turned, buffers(stages + 1), small_sum)
    gains = Reduction(sender, gains_ref, with_core, ["c"] + down, buffers(stages + 1), gains_sum)
    q = Reduction(sender, q_ref, fsdp, down, buffers(stages), q_sum)
    kv = Reduction(sender, kv_ref, fsdp, down, buffers(stages), kv_sum)
    outs = []
    for rows in halves_of(out_sum.shape[0]):
        part = out_ref.at[(slice(None),) * stages + (rows,)]
        outs.append(Reduction(sender, part, fsdp, turned, buffers(stages), out_sum.at[rows]))
    over = buffers(1)[0]
    peaks = buffers(stages)
    me = place_of(*pair)
    row = lax.axis_index(fsdp[0])
    meet([(axis,) for axis in with_core] + [pair])

    def send_columns(which, held):
        ffn_out[which, me] = held[me]
        return [
            sender.start(held.at[me ^ away], ffn_out.at[which, me], axes)
            for away, axes in ((1, (pair[1],)), (2, (pair[0],)), (3, pair))
        ]

    peak_out[...] = peak_ref[...]

    def send_peaks(stage):
        return sender.start(peak_out, peaks[stage], (fsdp[stage],))

    def next_peaks(stage, sent):
        sent.wait()
        sender.left.append(sent)
        peak_out[...] = jnp.maximum(peak_out[...], peaks[stage][...])
        return send_peaks(stage + 1) if stage < stages - 1 else None

    for part in (small, gains, q, outs[0], kv):
        part.begin()
    peak_sent = send_peaks(0)
    crossing = sender.start(up_ref.at[1 - row], over, (fsdp[0],))
    outs[1].begin()
    columns = send_columns(0, down_ref)
    small.end()
    gains.end()
    columns += send_columns(1, gate_ref)
    peak_sent = next_peaks(0, peak_sent)
    for part in (q, kv, outs[0]):
        part.end()
    crossing.wait_recv()
    over[...] = (up_ref[row].astype(f32) + over[...].astype(f32)).astype(bf16)
    columns += send_columns(2, over)
    for stage in range(1, stages):
        peak_sent = next_peaks(stage, peak_sent)
        for part in (outs[1], small, gains, q, kv, outs[0]):
            part.end()
    for reduction in (q, kv, outs[0], small, gains, outs[1]):
        reduction.finish()
    for copy in columns:
        copy.wait_recv()
    sender.finish()


def last_scatter(fsdp, pair, peak, small, gains, q, kv, out, down, gate, up):
    vmem = pl.BlockSpec(memory_space=pltpu.VMEM)
    stages = len(fsdp)

    def buffers(array, count, rows=None):
        lead = array.ndim - 2
        block = (rows or array.shape[-2], array.shape[-1])
        return [pltpu.VMEM((2,) * (lead - 1 - i) + block, bf16) for i in range(count)]

    scratch = (
        buffers(small, stages + 1)
        + buffers(gains, stages + 1)
        + buffers(q, stages)
        + buffers(kv, stages)
        + [buf for rows in halves_of(out.shape[-2]) for buf in buffers(out, stages, rows.size)]
        + [pltpu.VMEM(down.shape, bf16)]
        + [pltpu.VMEM(peak.shape, f32)] * stages
    )
    copies = 2 * (stages + 1) + 4 * stages + 1 + 9 + stages
    return pl.pallas_call(
        functools.partial(last_kernel, fsdp, pair),
        out_shape=tuple(jax.ShapeDtypeStruct(x.shape[-2:], f32) for x in (small, gains, q, kv, out))
        + (
            jax.ShapeDtypeStruct((3,) + down.shape, bf16),
            jax.ShapeDtypeStruct(peak.shape, f32),
        ),
        in_specs=[vmem] * 9,
        out_specs=(vmem,) * 7,
        scratch_shapes=scratch
        + [pltpu.SemaphoreType.DMA((copies,)), pltpu.SemaphoreType.DMA((copies,))],
        compiler_params=pltpu.CompilerParams(
            collective_id=2, has_side_effects=True, vmem_limit_bytes=60 << 20
        ),
    )(peak, small, gains, q, kv, out, down, gate, up)


def shards(
    fsdp,
    hidden_in,
    seq_ids,
    block_ids,
    clip_limit,
    cotangent,
    q_down,
    kv_down,
    q_up,
    kv_up,
    out_proj,
    gate_proj,
    up_proj,
    down_proj,
    in_gain,
    q_gain,
    kv_gain,
    post_gain,
):
    tokens_here, width = hidden_in.shape
    seq_row = seq_ids[0]
    block_row = block_ids[0]
    group = seq_row.shape[0]
    heads = q_up.shape[1] // (NOPE + ROPE)
    score_scale = 1.0 / math.sqrt(NOPE + ROPE)
    core = lax.axis_index("c")
    first_row = core * tokens_here
    wide, near = fsdp[1], fsdp[-1]
    pair = (wide, near)
    spread = [axis for axis in fsdp if axis not in pair]
    squares = [(fsdp[i], fsdp[i + 1]) for i in range(0, len(fsdp), 2)]
    at_wide, at_near = lax.axis_index(wide), lax.axis_index(near)
    chips = tuple(fsdp)
    count = 2 ** len(fsdp)

    small_rows = q_down.shape[0]
    q_rank = q_down.shape[1]
    small_cols = q_rank + kv_down.shape[1]

    def row(value):
        return jnp.pad(value, ((0, 0), (0, TILE - value.shape[1])))[:, None, :]

    def rows_of(*values):
        held = jnp.concatenate([row(value) for value in values], axis=1)
        return jnp.pad(held, ((0, 0), (0, 8 - len(values)), (0, 0)))

    small = jnp.concatenate([q_down, kv_down], axis=1)
    gains = rows_of(in_gain[None], post_gain[None], q_gain[None], kv_gain[None])[0]
    q_up_wide = jnp.pad(
        q_up.reshape(-1, heads, NOPE + ROPE), ((0, 0), (0, 0), (0, TILE - NOPE - ROPE))
    ).reshape(-1, heads * TILE)
    small_all, gains_all, q_up_all, kv_up_all, gate_held, others_held = first_gather(
        squares, pair, spread, small, gains, q_up_wide, kv_up, gate_proj, up_proj, down_proj
    )
    down_full = small_all.reshape(-1, small_cols)
    q_up_full = q_up_all.reshape(-1, heads * TILE)
    kv_up_full = kv_up_all.reshape(-1, kv_up.shape[1])
    devices = 2 * count

    def gain(at, size):
        return gains_all.reshape(devices, 8, TILE)[:, at, :size].reshape(-1).astype(f32)

    in_float = gain(0, in_gain.shape[0])
    post_float = gain(1, post_gain.shape[0])
    q_gain_float = gain(2, q_gain.shape[0])
    kv_gain_float = gain(3, kv_gain.shape[0])

    out_full = lax.all_gather(after(out_proj, gains_all), chips, axis=0, tiled=True)
    cot_float = cotangent.astype(f32)

    def over(pieces, axis, *ready):
        return [swap(after(piece, *ready), axis) for piece in pieces]

    def exchange(held, dims, axis):
        at, dim = lax.axis_index(axis), dims.index(axis)
        return swap(pick(held, 1 - at, dim), axis), pick(held, at, dim)

    def sum_of_cores(value):
        held = value.reshape(2, 2, 2, tokens_here, width)
        other = swap(pick(held, 1 - core, 2), "c")
        return (pick(held, core, 2).astype(f32) + other.astype(f32)).astype(bf16)

    def sum_of_chips(held):
        return square_scatter(held, wide, near, 0).reshape(tokens_here, width)

    def core_both(value):
        return both(value, swap(value, "c"), "c", 0)

    def core_sum(value):
        def rows(at):
            return lax.dynamic_slice_in_dim(value, at * tokens_here, tokens_here)

        return rows(core) + swap(rows(1 - core), "c")

    x_float = hidden_in.astype(f32)
    x_normed = rms_scale(x_float, in_float).astype(bf16)
    pre = jnp.dot(x_normed, down_full, preferred_element_type=f32)
    q_pre = pre[:, :q_rank]
    c_lat_pre = pre[:, q_rank : q_rank + KVR]
    c_rot_pre = pre[:, q_rank + KVR :]
    own_cos, own_sin = angles(seq_row, first_row, tokens_here)
    q_latent = rms_scale(q_pre, q_gain_float).astype(bf16)
    kv_latent = rms_scale(c_lat_pre, kv_gain_float).astype(bf16)
    key_rot = rotate(c_rot_pre, own_cos, own_sin).astype(bf16)
    key_rot = jnp.pad(key_rot, ((0, 0), (NOPE, TILE - NOPE - ROPE)))
    latents = core_both(jnp.concatenate([q_latent, kv_latent, key_rot], axis=1))
    q_lat_all = latents[:, :q_rank]
    kv_lat_all = latents[:, q_rank : q_rank + KVR]
    key_rot_all = latents[:, q_rank + KVR :]
    all_cos, all_sin = angles(seq_row, 0, group)
    q_full = jnp.dot(q_lat_all, q_up_full, preferred_element_type=f32)
    kv_full = jnp.dot(kv_lat_all, kv_up_full, preferred_element_type=f32).astype(bf16)
    allowed = (seq_row[None, :] == seq_row[:, None]) & (block_row[:, None] <= block_row[None, :])
    bias = jnp.where(allowed, 0.0, -1e30).astype(f32)
    axes = list(spread)
    gate_pieces = [gate_held[0], gate_held[1]]
    up_pieces = [others_held[0]]
    down_pieces = [others_held[1]]
    up_pieces += over(up_pieces, axes[0])
    for axis in axes[1:]:
        gate_pieces += over(gate_pieces, axis)
    q_full, *early = lax.optimization_barrier((q_full, *gate_pieces, *up_pieces))
    gate_pieces, up_pieces = early[: len(gate_pieces)], early[len(gate_pieces) :]
    attn, queries, log_total, local_peak = attend(
        q_full, kv_full, key_rot_all, tables(all_cos, all_sin), bias, score_scale
    )
    down_pieces += over(down_pieces, axes[0], q_full)
    for axis in axes[1:]:
        up_pieces += over(up_pieces, axis)
    d_ffn = (resid_scale * cot_float).astype(bf16)
    d_ffn_all = lax.all_gather(after(d_ffn, attn), (wide, near, "c"), axis=0, tiled=True)
    branch = core_sum(contract(attn, out_full, 1, 1))
    mid = x_float + resid_scale * branch
    mid_normed = rms_scale(mid, post_float).astype(bf16)
    gate_full = lay([after(piece, attn) for piece in gate_pieces], fsdp, pair, spread)
    mid_all = tokens_of_chips(after(mid_normed, gate_full, *down_pieces), pair)
    for axis in axes[1:]:
        down_pieces += over(down_pieces, axis, mid_all)
    gate = jnp.dot(mid_all, gate_full, preferred_element_type=f32)
    up_full = lay([after(piece, gate) for piece in up_pieces], fsdp, pair, spread)
    up_value = jnp.dot(mid_all, up_full, preferred_element_type=f32)
    down_proj_full = lay([after(piece, up_value) for piece in down_pieces], fsdp, pair, spread)
    sigmoid = jax.nn.sigmoid(gate)
    silu_value = gate * sigmoid
    act = (silu_value * up_value).astype(bf16)

    d_act = jnp.dot(d_ffn_all, down_proj_full, preferred_element_type=f32)
    d_gate = (d_act * up_value * (sigmoid * (1.0 + gate * (1.0 - sigmoid)))).astype(bf16)
    d_up = (d_act * silu_value).astype(bf16)
    dims = list(fsdp)
    first, last = spread[0], spread[-1]
    held_shape = [2] * len(fsdp) + [width // count, -1]

    def added(parts):
        return (parts[0].astype(f32) + parts[1].astype(f32)).astype(bf16)

    def inner(held):
        left = [axis for axis in dims if axis != last]
        for axis in reversed(spread[1:-1]):
            held = added(exchange(held, left, axis))
            left.remove(axis)
        return held

    def begin(grad):
        return exchange(grad.reshape(held_shape), dims, last)

    def cross(held):
        return exchange(held, [first, *pair], first)

    down_grad = rows_first(contract(d_ffn_all, act, 0, 0).astype(bf16))
    down_parts = begin(down_grad)
    d_gate_late, d_up_late, _ = lax.optimization_barrier((d_gate, d_up, down_grad))
    d_mid_part = (
        contract(d_gate_late, gate_full, 1, 1) + contract(d_up_late, up_full, 1, 1)
    ).astype(bf16)
    d_mid_held = sum_of_cores(d_mid_part)
    d_mid_normed = sum_of_chips(d_mid_held)
    mid_late, down_got, down_kept, _ = lax.optimization_barrier(
        (mid_all, *down_parts, d_mid_held)
    )
    gate_grad = rows_first(contract(mid_late, d_gate, 0, 0).astype(bf16))
    gate_parts = begin(gate_grad)
    down_parts = cross(inner(added((down_got, down_kept))))
    up_grad = rows_first(contract(after(mid_late, gate_grad), d_up, 0, 0).astype(bf16))
    up_parts = begin(up_grad)
    ffn_part = contract(after(act, up_grad), down_proj_full, 1, 1).astype(bf16)
    post_pull = jax.vjp(rms_scale, mid, post_float)[1]
    d_mid_norm, post_grad = post_pull(after(d_mid_normed, up_grad, ffn_part))
    ffn = lax.psum_scatter(
        after(ffn_part, d_mid_norm), (wide, near, "c"), scatter_dimension=0, tiled=True
    )
    layer_out = (mid + resid_scale * ffn.astype(f32)).astype(bf16)
    d_mid = cot_float + d_mid_norm
    d_branch = (resid_scale * d_mid).astype(bf16)
    d_branch_all = core_both(d_branch)
    d_attn = jnp.dot(d_branch_all, out_full, preferred_element_type=f32).astype(bf16)
    d_attn_late, gate_got, gate_kept, *down_parts = lax.optimization_barrier(
        (d_attn, *gate_parts, *down_parts)
    )
    gate_parts = cross(inner(added((gate_got, gate_kept))))
    d_q, d_kv, d_rot_part = attend_back(
        queries,
        kv_full,
        d_attn_late,
        log_total,
        key_rot_all,
        tables(all_cos, -all_sin),
        bias,
        score_scale,
    )
    out_grad = rows_first(contract(after(d_branch_all, d_q), attn, 0, 0).astype(bf16))
    q_lat_late, *up_parts = lax.optimization_barrier((q_lat_all, *up_parts))
    q_up_grad = heads_grad(q_lat_late, d_q)
    kv_up_grad = rows_first(contract(kv_lat_all, d_kv, 0, 0).astype(bf16))
    d_q_lat_part = contract(d_q, q_up_full, 1, 1)
    d_kv_lat_part = contract(d_kv, kv_up_full, 1, 1)
    d_latents = core_sum(jnp.concatenate([d_q_lat_part, d_kv_lat_part, d_rot_part], axis=1))
    q_pull = jax.vjp(rms_scale, q_pre, q_gain_float)[1]
    d_q_pre, q_gain_grad = q_pull(d_latents[:, :q_rank])
    kv_pull = jax.vjp(rms_scale, c_lat_pre, kv_gain_float)[1]
    d_c_lat, kv_gain_grad = kv_pull(d_latents[:, q_rank : q_rank + KVR])
    d_key_rot = d_latents[:, q_rank + KVR + NOPE : q_rank + KVR + NOPE + ROPE]
    d_pre = jnp.concatenate(
        [d_q_pre, d_c_lat, rotate(d_key_rot, own_cos, -own_sin)], axis=-1
    ).astype(bf16)
    down_grads = rows_first(contract(x_normed, d_pre, 0, 0).astype(bf16))
    d_x_normed = contract(d_pre, down_full, 1, 1)
    in_pull = jax.vjp(rms_scale, x_float, in_float)[1]
    d_x_norm, in_grad = in_pull(d_x_normed)
    input_grad = d_mid + d_x_norm

    rows_here = width // count
    ffn_held = [
        added(down_parts).reshape(4, rows_here, -1),
        added(gate_parts).reshape(4, rows_here, -1),
        inner(added(up_parts)).reshape(2, 4, rows_here, -1),
    ]
    gain_grads = rows_of(
        *(grad.reshape(devices, -1) for grad in (in_grad, post_grad, q_gain_grad, kv_gain_grad))
    ).astype(bf16)

    def blocks(grad, lead):
        return grad.reshape([2] * lead + [grad.shape[0] // 2**lead, -1])

    small_out, gain_out, q_up_out, kv_up_out, out_out, ffn_cols, peak_all = last_scatter(
        fsdp,
        pair,
        local_peak,
        blocks(down_grads, len(fsdp) + 1),
        gain_grads.reshape([2] * (len(fsdp) + 1) + [8, TILE]),
        blocks(q_up_grad, len(fsdp)),
        blocks(kv_up_grad, len(fsdp)),
        blocks(out_grad, len(fsdp)),
        *ffn_held,
    )
    down_out, gate_out, up_out = (merge(ffn_cols, which) for which in range(3))
    peaks = peak_all[0, :heads]
    limit = clip_limit[0]
    factors = limit / jnp.maximum(peaks, limit)
    root = jnp.sqrt(factors)
    q_cols = jnp.concatenate(
        [
            jnp.broadcast_to(root[:, None], (heads, NOPE)),
            jnp.broadcast_to(factors[:, None], (heads, ROPE)),
        ],
        axis=1,
    ).reshape(heads * (NOPE + ROPE))
    kv_cols = jnp.concatenate(
        [jnp.broadcast_to(root[:, None], (heads, NOPE)), jnp.ones((heads, VD), f32)], axis=1
    ).reshape(heads * (NOPE + VD))
    q_clipped = (q_up.astype(f32) * q_cols[None, :]).astype(bf16)
    kv_clipped = (kv_up.astype(f32) * kv_cols[None, :]).astype(bf16)
    return (
        layer_out,
        input_grad,
        small_out[:, :q_rank],
        small_out[:, q_rank:],
        q_up_out,
        kv_up_out,
        out_out,
        gate_out,
        up_out,
        down_out,
        gain_out[0, : in_gain.shape[0]],
        gain_out[2, : q_gain.shape[0]],
        gain_out[3, : kv_gain.shape[0]],
        gain_out[1, : post_gain.shape[0]],
        q_clipped,
        kv_clipped,
        peaks,
        factors,
    )


def solution(mesh):
    bits = mesh.shape["fsdp"].bit_length() - 1
    fsdp = [f"f{i}" for i in range(bits)]
    fine = Mesh(mesh.devices.reshape((2,) * (bits + 1)), tuple(fsdp) + ("c",))
    split = tuple(fsdp)
    whole = split + ("c",)
    return jax.shard_map(
        functools.partial(shards, fsdp),
        mesh=fine,
        in_specs=(
            P(whole, None),
            P(split, None),
            P(split, None),
            P(),
            P(whole, None),
            P(whole, None),
            P(whole, None),
            P(split, "c"),
            P(split, "c"),
            P(split, "c"),
            P(split, "c"),
            P(split, "c"),
            P(split, "c"),
            P(whole),
            P(whole),
            P(whole),
            P(whole),
        ),
        out_specs=(
            P(whole, None),
            P(whole, None),
            P(whole, None),
            P(whole, None),
            P(split, "c"),
            P(split, "c"),
            P(split, "c"),
            P(split, "c"),
            P(split, "c"),
            P(split, "c"),
            P(whole),
            P(whole),
            P(whole),
            P(whole),
            P(split, "c"),
            P(split, "c"),
            P("c"),
            P("c"),
        ),
        check_vma=False,
    )
```

```python
import functools
import math

import jax
import jax.numpy as jnp
from jax import lax
from jax.experimental import pallas as pl
from jax.experimental.pallas import tpu as pltpu
from jax.experimental.layout import Layout, with_layout_constraint
from jax.sharding import Mesh
from jax.sharding import PartitionSpec as P

NOPE = 64
ROPE = 32
VD = 64
KVR = 256
TILE = 128


eps = 1e-05
resid_scale = 1.4 / math.sqrt(62.0)
rope_base = 10000.0
SWAP = [(0, 1), (1, 0)]
f32 = jnp.float32
bf16 = jnp.bfloat16


def rms_scale(value, gain):
    return value * lax.rsqrt(jnp.mean(value * value, axis=-1, keepdims=True) + eps) * gain


def rotate(value, cosine, sine):
    half = value.shape[-1] // 2
    first = value[..., :half]
    second = value[..., half:]
    return jnp.concatenate(
        [first * cosine - second * sine, second * cosine + first * sine], axis=-1
    )


def angles(seq_row, start, count):
    own_ids = lax.dynamic_slice_in_dim(seq_row, start, count)
    earlier = jnp.sum((seq_row[None, :] < own_ids[:, None]).astype(jnp.int32), axis=1)
    place = (start + jnp.arange(count, dtype=jnp.int32) - earlier).astype(f32)
    freq = jnp.power(rope_base, -jnp.arange(ROPE // 2, dtype=f32) * (2.0 / ROPE))
    turn = place[:, None] * freq[None, :]
    return (jnp.cos(turn), jnp.sin(turn))


def contract(left, right, left_dim, right_dim):
    return lax.dot_general(
        left, right, (((left_dim,), (right_dim,)), ((), ())), preferred_element_type=f32
    )


def turn(value, plain, first, second):
    return (
        value * plain
        + pltpu.roll(value, TILE - ROPE // 2, 1) * first
        + pltpu.roll(value, ROPE // 2, 1) * second
    )


def tables(cosine, sine):
    rows = cosine.shape[0]
    half = ROPE // 2

    def zeros(count):
        return jnp.zeros((rows, count), f32)

    plain = jnp.concatenate([jnp.ones((rows, NOPE), f32), cosine, cosine, zeros(TILE - NOPE - ROPE)], axis=1)
    first = jnp.concatenate([zeros(NOPE), -sine, zeros(TILE - NOPE - half)], axis=1)
    second = jnp.concatenate([zeros(NOPE + half), sine, zeros(TILE - NOPE - ROPE)], axis=1)
    return plain, first, second


def attend_kernel(
    scale,
    q_ref,
    kv_ref,
    rot_ref,
    plain_ref,
    first_ref,
    second_ref,
    bias_ref,
    mixed_ref,
    query_ref,
    total_ref,
    peak_ref,
):
    step = pl.program_id(0)
    lane = lax.broadcasted_iota(jnp.int32, (q_ref.shape[0], TILE), 1)
    spot = lax.broadcasted_iota(jnp.int32, peak_ref.shape, 1)

    @pl.when(step == 0)
    def _():
        peak_ref[...] = jnp.zeros_like(peak_ref)

    outs = []
    for one in range(2):
        cols = slice(one * TILE, (one + 1) * TILE)
        query = turn(q_ref[:, cols], plain_ref[...], first_ref[...], second_ref[...]).astype(bf16)
        query_ref[:, cols] = query
        kv = kv_ref[:, cols]
        keys = jnp.where(lane < NOPE, kv, rot_ref[...])
        masked = contract(keys, query, 1, 1) * scale + bias_ref[...]
        top = jnp.max(masked, axis=0, keepdims=True)
        weights = jnp.exp(masked - top)
        total = jnp.sum(weights, axis=0, keepdims=True)
        chance = (weights * (1.0 / total)).astype(bf16)
        outs.append(contract(chance, kv, 0, 0))
        total_ref[0, one : one + 1, :] = top + jnp.log(total)
        peak_ref[...] = jnp.where(spot == step * 2 + one, jnp.max(top), peak_ref[...])
    mixed_ref[...] = jnp.where(lane < VD, pltpu.roll(outs[0], VD, 1), outs[1]).astype(bf16)


def attend(q, kv, rot, turns, bias, scale):
    group, cols = q.shape
    heads = cols // TILE
    whole = pl.BlockSpec((group, TILE), lambda i: (0, 0))
    two = pl.BlockSpec((group, 2 * TILE), lambda i: (0, i))
    return pl.pallas_call(
        functools.partial(attend_kernel, scale),
        grid=(heads // 2,),
        out_shape=(
            jax.ShapeDtypeStruct((group, heads * VD), bf16),
            jax.ShapeDtypeStruct((group, cols), bf16),
            jax.ShapeDtypeStruct((heads // 2, 2, group), f32),
            jax.ShapeDtypeStruct((8, TILE), f32),
        ),
        in_specs=[two, two, whole, whole, whole, whole, pl.BlockSpec((group, group), lambda i: (0, 0))],
        out_specs=(
            pl.BlockSpec((group, TILE), lambda i: (0, i)),
            two,
            pl.BlockSpec((1, 2, group), lambda i: (i, 0, 0)),
            pl.BlockSpec((8, TILE), lambda i: (0, 0)),
        ),
        compiler_params=pltpu.CompilerParams(
            dimension_semantics=("arbitrary",), vmem_limit_bytes=40 << 20
        ),
        cost_estimate=pl.CostEstimate(flops=1, transcendentals=0, bytes_accessed=1),
    )(q, kv, rot, *turns, bias)


def attend_back_kernel(
    scale,
    query_ref,
    kv_ref,
    d_mixed_ref,
    total_ref,
    rot_ref,
    plain_ref,
    first_ref,
    second_ref,
    bias_ref,
    d_q_ref,
    d_kv_ref,
    d_rot_ref,
):
    step = pl.program_id(0)
    lane = lax.broadcasted_iota(jnp.int32, (query_ref.shape[0], TILE), 1)

    @pl.when(step == 0)
    def _():
        d_rot_ref[...] = jnp.zeros_like(d_rot_ref)

    pair = d_mixed_ref[...].astype(f32)
    for one in range(2):
        cols = slice(one * TILE, (one + 1) * TILE)
        query = query_ref[:, cols]
        kv = kv_ref[:, cols]
        keys = jnp.where(lane < NOPE, kv, rot_ref[...])
        own = pair if one else pltpu.roll(pair, VD, 1)
        d_mixed = jnp.where(lane < VD, 0.0, own).astype(bf16)
        masked = contract(keys, query, 1, 1) * scale + bias_ref[...]
        chance = jnp.exp(masked - total_ref[0, one : one + 1, :])
        d_values = contract(chance.astype(bf16), d_mixed, 1, 0)
        d_chance = contract(kv, d_mixed, 1, 1)
        inner = jnp.sum(chance * d_chance, axis=0, keepdims=True)
        d_raw = (chance * (d_chance - inner) * scale).astype(bf16)
        d_keys = contract(d_raw, query, 1, 0)
        d_query = contract(d_raw, keys, 0, 0)
        d_q_ref[:, cols] = turn(
            d_query, plain_ref[...], first_ref[...], second_ref[...]
        ).astype(bf16)
        d_kv_ref[:, cols] = jnp.where(lane < NOPE, d_keys, d_values).astype(bf16)
        d_rot_ref[...] += d_keys


def attend_back(query, kv, d_mixed, total, rot, turns, bias, scale):
    group, cols = query.shape
    heads = cols // TILE
    whole = pl.BlockSpec((group, TILE), lambda i: (0, 0))
    two = pl.BlockSpec((group, 2 * TILE), lambda i: (0, i))
    return pl.pallas_call(
        functools.partial(attend_back_kernel, scale),
        grid=(heads // 2,),
        out_shape=(
            jax.ShapeDtypeStruct((group, cols), bf16),
            jax.ShapeDtypeStruct((group, cols), bf16),
            jax.ShapeDtypeStruct((group, TILE), f32),
        ),
        in_specs=[
            two,
            two,
            pl.BlockSpec((group, TILE), lambda i: (0, i)),
            pl.BlockSpec((1, 2, group), lambda i: (i, 0, 0)),
            whole,
            whole,
            whole,
            whole,
            pl.BlockSpec((group, group), lambda i: (0, 0)),
        ],
        out_specs=(two, two, whole),
        compiler_params=pltpu.CompilerParams(
            dimension_semantics=("arbitrary",), vmem_limit_bytes=40 << 20
        ),
        cost_estimate=pl.CostEstimate(flops=1, transcendentals=0, bytes_accessed=1),
    )(query, kv, d_mixed, total, rot, *turns, bias)


def swap(value, axis):
    return lax.ppermute(value, axis, SWAP)


def far(value, pair):
    return lax.ppermute(value, pair, [(i, 3 - i) for i in range(4)])


def after(value, *others):
    return lax.optimization_barrier((value,) + others)[0]


def pick(value, at, dim):
    return lax.dynamic_index_in_dim(value, at, dim, keepdims=True)


def both(own, other, axis, dim):
    here = lax.axis_index(axis) == 0
    return jnp.concatenate([jnp.where(here, own, other), jnp.where(here, other, own)], axis=dim)


def heads_grad_kernel(latent_ref, d_ref, out_ref):
    total = contract(latent_ref[...], d_ref[...], 0, 0)
    parts = [total[:, i * TILE : i * TILE + NOPE + ROPE] for i in range(4)]
    out_ref[...] = jnp.concatenate(parts, axis=1).astype(bf16)


def heads_grad(latent, d_heads):
    group, rank = latent.shape
    packs = d_heads.shape[1] // (4 * TILE)
    cols = 4 * (NOPE + ROPE)
    return pl.pallas_call(
        heads_grad_kernel,
        grid=(packs,),
        out_shape=jax.ShapeDtypeStruct((rank, packs * cols), bf16),
        in_specs=[
            pl.BlockSpec((group, rank), lambda i: (0, 0)),
            pl.BlockSpec((group, 4 * TILE), lambda i: (0, i)),
        ],
        out_specs=pl.BlockSpec((rank, cols), lambda i: (0, i)),
        compiler_params=pltpu.CompilerParams(vmem_limit_bytes=32 << 20),
        cost_estimate=pl.CostEstimate(flops=1, transcendentals=0, bytes_accessed=1),
    )(latent, d_heads)


def features_kernel(*refs):
    out_ref = refs[-1]
    total = contract(refs[0][...], refs[1][...], 1, 1)
    for i in range(2, len(refs) - 1, 2):
        total += contract(refs[i][...], refs[i + 1][...], 1, 1)
    out_ref[...] = total.astype(bf16)


def features(*pairs):
    rows, cols = pairs[0][0].shape
    width = pairs[0][1].shape[0]
    tile = min(rows, 512)
    return pl.pallas_call(
        features_kernel,
        grid=(rows // tile,),
        out_shape=jax.ShapeDtypeStruct((rows, width), bf16),
        in_specs=[
            pl.BlockSpec((tile, cols), lambda i: (i, 0)),
            pl.BlockSpec((width, cols), lambda i: (0, 0)),
        ]
        * len(pairs),
        out_specs=pl.BlockSpec((tile, width), lambda i: (i, 0)),
        compiler_params=pltpu.CompilerParams(vmem_limit_bytes=56 << 20),
        cost_estimate=pl.CostEstimate(flops=1, transcendentals=0, bytes_accessed=1),
    )(*(array for pair in pairs for array in pair))


def grad_kernel(axis, left_ref, right_ref, keep_ref, send_ref, total):
    half = total.shape[1]
    value = contract(left_ref[...], right_ref[...], 0, 0).astype(bf16)
    total[0] = value[:half]
    total[1] = value[half:]
    at = lax.axis_index(axis)
    keep_ref[0] = total[at]
    send_ref[0] = total[1 - at]


def grad_halves(left, right, rows, axis):
    tokens, width = left.shape
    cols = right.shape[1]
    tile = 4 * rows
    if tile % TILE:
        held = rows_first(contract(left, right, 0, 0).astype(bf16)).reshape(-1, 2, 2 * rows, cols)
        at = lax.axis_index(axis)
        return tuple(pick(held, i, 1)[:, 0] for i in (at, 1 - at))
    out = jax.ShapeDtypeStruct((width // tile, 2 * rows, cols), bf16)
    return pl.pallas_call(
        functools.partial(grad_kernel, axis),
        grid=(width // tile,),
        out_shape=(out, out),
        in_specs=[
            pl.BlockSpec((tokens, tile), lambda i: (0, i)),
            pl.BlockSpec((tokens, cols), lambda i: (0, 0)),
        ],
        out_specs=(pl.BlockSpec((1, 2 * rows, cols), lambda i: (i, 0, 0)),) * 2,
        scratch_shapes=[pltpu.VMEM((2, 2 * rows, cols), bf16)],
        compiler_params=pltpu.CompilerParams(vmem_limit_bytes=56 << 20),
        cost_estimate=pl.CostEstimate(flops=1, transcendentals=0, bytes_accessed=1),
    )(left, right)


def rows_first(value):
    return with_layout_constraint(value, Layout(major_to_minor=(0, 1)))


def square_scatter(held, first, second, dim):
    here, there = lax.axis_index(first), lax.axis_index(second)

    def part(w, n):
        return pick(pick(held, w, dim), n, dim + 1)

    near = swap(part(here, 1 - there).astype(bf16), second)
    wide = swap(part(1 - here, there).astype(bf16), first)
    corner = far(part(1 - here, 1 - there).astype(bf16), (first, second))
    own = part(here, there).astype(f32)
    return own + near.astype(f32) + wide.astype(f32) + corner.astype(f32)


def place_of(first, second):
    return lax.axis_index(first) * 2 + lax.axis_index(second)


def other_of(axes):
    return {axis: 1 - lax.axis_index(axis) for axis in axes}


def meet(partners):
    barrier = pltpu.get_barrier_semaphore()
    for axes in partners:
        pl.semaphore_signal(
            barrier, inc=1, device_id=other_of(axes), device_id_type=pl.DeviceIdType.MESH
        )
    pl.semaphore_wait(barrier, len(partners))


class Sender:
    def __init__(self, send_sems, recv_sems):
        self.send_sems, self.recv_sems, self.all, self.left = send_sems, recv_sems, [], []

    def start(self, source, target, axes):
        copy = pltpu.make_async_remote_copy(
            src_ref=source,
            dst_ref=target,
            send_sem=self.send_sems.at[len(self.all)],
            recv_sem=self.recv_sems.at[len(self.all)],
            device_id=other_of(axes),
            device_id_type=pl.DeviceIdType.MESH,
        )
        copy.start()
        self.all.append(copy)
        return copy

    def finish(self):
        for copy in self.all:
            if all(copy is not other for other in self.left):
                copy.wait_send()


def first_kernel(
    squares,
    pair,
    spread,
    small_ref,
    gains_ref,
    q_ref,
    kv_ref,
    gate_ref,
    up_ref,
    down_ref,
    small_out,
    gains_out,
    q_out,
    kv_out,
    gate_out,
    gate_over,
    gate_last,
    up_out,
    down_out,
    staged,
    send_sems,
    recv_sems,
):
    core = lax.axis_index("c")
    places = [place_of(*square) for square in squares]
    me = place_of(*pair)
    sender = Sender(send_sems, recv_sems)
    cols = staged.shape[3]

    small_out[(*places, core)] = small_ref[...]
    gains_out[(*places, core)] = gains_ref[...]
    q_out[tuple(places)] = q_ref[...]
    kv_out[tuple(places)] = kv_ref[...]
    partners = [axes for one, two in squares for axes in ((two,), (one,), (one, two))]
    meet(partners + [pair, ("c",)])

    def blocks(ref, stage, place, tail, lead=()):
        index = lead + (slice(None),) * (stage - len(lead)) + (place,) + tuple(places[stage + 1 :])
        return ref.at[index + tail]

    early = [(small_out, (core,)), (gains_out, (core,))]
    later = [(q_out, ()), (kv_out, ())]

    def send_first(ref, tail):
        mine = blocks(ref, 0, places[0], tail)
        return [sender.start(mine, mine, axes) for axes in partners[:3]]

    def send_square(ref, tail, stage):
        one, two = squares[stage]
        mine = blocks(ref, stage, places[stage], tail)
        return [sender.start(mine, mine, (two,)), sender.start(mine, mine, (one,))]

    def pass_on(ref, tail, stage, copies):
        one, two = squares[stage]
        copies[0].wait_recv()
        half = blocks(ref, stage, places[stage] ^ 1, tail, (slice(0, 2),))
        first = sender.start(half, half, (one,))
        copies[1].wait_recv()
        half = blocks(ref, stage, places[stage] ^ 2, tail, (slice(2, 4),))
        return [first, sender.start(half, half, (two,))]

    def wait(copies):
        for copy in copies:
            copy.wait_recv()

    targets = (gate_out, up_out, down_out)

    def send_columns(away, axes):
        return [
            sender.start(staged.at[which, me ^ away], target.at[me], axes)
            for which, target in enumerate(targets)
        ]

    first = [send_first(*item) for item in early]
    for which, weight_ref in enumerate((gate_ref, up_ref, down_ref)):
        for quarter in range(4):
            staged[which, quarter] = weight_ref[:, quarter * cols : (quarter + 1) * cols]
    columns = [send_columns(1, (pair[1],))]
    for which, target in enumerate(targets):
        target[me] = staged[which, me]
    for copies in first:
        wait(copies)
    sent = [send_square(*item, 1) for item in early]
    first_later = [send_first(*item) for item in later]
    columns.append(send_columns(2, (pair[0],)))
    for stage in range(1, len(squares)):
        if stage > 1:
            sent = [send_square(*item, stage) for item in early]
        passed = [pass_on(*item, stage, copies) for item, copies in zip(early, sent)]
        if stage == 1:
            for copies in first_later:
                wait(copies)
            sent_later = [send_square(*item, 1) for item in later]
            columns.append(send_columns(3, pair))
        for copies in passed:
            wait(copies)
    mine = (slice(None),) * len(squares) + (core,)
    core_sent = [sender.start(ref.at[mine], ref.at[mine], ("c",)) for ref, _ in early]
    for copies in columns:
        copies[0].wait_recv()
    over = [
        sender.start(gate_out, gate_over, (spread[0],)),
        sender.start(gate_out, gate_last, (spread[1],)),
    ]
    for stage in range(1, len(squares)):
        if stage > 1:
            sent_later = [send_square(*item, stage) for item in later]
        passed = [pass_on(*item, stage, copies) for item, copies in zip(later, sent_later)]
        for copies in passed:
            wait(copies)
    wait(core_sent)
    for copies in columns:
        wait(copies[1:])
    wait(over)
    sender.finish()


def first_gather(squares, pair, spread, small, gains, q_up, kv_up, gate, up, down):
    vmem = pl.BlockSpec(memory_space=pltpu.VMEM)
    rows, cols = gate.shape
    lead = (4,) * len(squares)
    copies = 12 + 16 * (len(squares) - 1) + 2 + 9 + 2
    return pl.pallas_call(
        functools.partial(first_kernel, squares, pair, spread),
        out_shape=(
            jax.ShapeDtypeStruct(lead + (2,) + small.shape, bf16),
            jax.ShapeDtypeStruct(lead + (2,) + gains.shape, bf16),
            jax.ShapeDtypeStruct(lead + q_up.shape, bf16),
            jax.ShapeDtypeStruct(lead + kv_up.shape, bf16),
        )
        + (jax.ShapeDtypeStruct((4, rows, cols // 4), bf16),) * 5,
        in_specs=[vmem] * 7,
        out_specs=(vmem,) * 9,
        scratch_shapes=[
            pltpu.VMEM((3, 4, rows, cols // 4), bf16),
            pltpu.SemaphoreType.DMA((copies,)),
            pltpu.SemaphoreType.DMA((copies,)),
        ],
        compiler_params=pltpu.CompilerParams(
            collective_id=0, has_side_effects=True, vmem_limit_bytes=48 << 20
        ),
    )(small, gains, q_up, kv_up, gate, up, down)


def lay_copies(fsdp, pair, spread, pieces, target, sems):
    copies = []
    for number, piece in enumerate(pieces):
        for block in range(4):
            place = 0
            for axis in fsdp:
                if axis == pair[0]:
                    bit = block >> 1
                elif axis == pair[1]:
                    bit = block & 1
                else:
                    bit = lax.axis_index(axis) ^ ((number >> spread.index(axis)) & 1)
                place = place * 2 + bit
            copies.append(pltpu.make_async_copy(piece.at[block], target.at[place], sems.at[len(copies)]))
    for copy in copies:
        copy.start()
    return copies


def lay_kernel(fsdp, pair, spread, *refs):
    count = 2 ** len(spread)
    target, sems = refs[count:]
    for copy in lay_copies(fsdp, pair, spread, refs[:count], target, sems):
        copy.wait()


def lay(pieces, fsdp, pair, spread):
    rows, cols = pieces[0].shape[1:]
    blocks = 4 * len(pieces)
    out = pl.pallas_call(
        functools.partial(lay_kernel, fsdp, pair, spread),
        out_shape=jax.ShapeDtypeStruct((blocks, rows, cols), bf16),
        in_specs=[pl.BlockSpec(memory_space=pltpu.HBM)] * len(pieces),
        out_specs=pl.BlockSpec(memory_space=pltpu.VMEM),
        scratch_shapes=[pltpu.SemaphoreType.DMA((blocks,))],
        compiler_params=pltpu.CompilerParams(vmem_limit_bytes=32 << 20),
        cost_estimate=pl.CostEstimate(
            flops=0, transcendentals=0, bytes_accessed=4 * blocks * rows * cols
        ),
    )(*pieces)
    return out.reshape(blocks * rows, cols)


def tokens_kernel(pair, value_ref, out_ref, send_sems, recv_sems):
    core = lax.axis_index("c")
    me = place_of(*pair)
    one, two = pair
    half = value_ref.shape[0] // 2
    sender = Sender(send_sems, recv_sems)
    out_ref[me, core] = value_ref[...]
    meet([(two,), (one,), ("c",)])

    def send(place, axes, rows=slice(None)):
        mine = out_ref.at[place, core, rows]
        return sender.start(mine, mine, axes)

    near = send(me, (two,))
    wide = send(me, (one,))
    got = [send(me, ("c",))]
    near.wait_recv()
    far = [send(me ^ 1, (one,), slice(0, half))]
    got.append(send(me ^ 1, ("c",)))
    wide.wait_recv()
    far.append(send(me ^ 2, (two,), slice(half, 2 * half)))
    got.append(send(me ^ 2, ("c",)))
    for copy in far:
        copy.wait_recv()
    got.append(send(me ^ 3, ("c",)))
    for copy in got:
        copy.wait_recv()
    sender.finish()


def tokens_of_chips(value, pair, number):
    rows, cols = value.shape
    vmem = pl.BlockSpec(memory_space=pltpu.VMEM)
    out = pl.pallas_call(
        functools.partial(tokens_kernel, pair),
        out_shape=jax.ShapeDtypeStruct((4, 2, rows, cols), bf16),
        in_specs=[vmem],
        out_specs=vmem,
        scratch_shapes=[pltpu.SemaphoreType.DMA((8,)), pltpu.SemaphoreType.DMA((8,))],
        compiler_params=pltpu.CompilerParams(
            collective_id=number, has_side_effects=True, vmem_limit_bytes=24 << 20
        ),
        cost_estimate=pl.CostEstimate(flops=1, transcendentals=0, bytes_accessed=1),
    )(value)
    return out.reshape(8 * rows, cols)


def merge_kernel(which, parts_ref, out_ref):
    cols = out_ref.shape[1] // 4
    for quarter in range(4):
        out_ref[:, quarter * cols : (quarter + 1) * cols] = parts_ref[0, quarter].astype(f32)


def merge(parts, which):
    rows, cols = parts.shape[2:]
    return pl.pallas_call(
        functools.partial(merge_kernel, which),
        grid=(1,),
        out_shape=jax.ShapeDtypeStruct((rows, 4 * cols), f32),
        in_specs=[pl.BlockSpec((1, 4, rows, cols), lambda i: (which, 0, 0, 0))],
        out_specs=pl.BlockSpec((rows, 4 * cols), lambda i: (0, 0)),
        cost_estimate=pl.CostEstimate(
            flops=0, transcendentals=0, bytes_accessed=24 * rows * cols
        ),
    )(parts)


class Reduction:
    def __init__(self, sender, held, dims, order, buffers, out):
        self.sender, self.held, self.dims, self.order = sender, held, list(dims), list(order)
        self.buffers, self.out = list(buffers), out

    def half(self, at):
        return (slice(None),) * self.dims.index(self.order[0]) + (at,)

    def begin(self):
        axis = self.order[0]
        source = self.held.at[self.half(1 - lax.axis_index(axis))]
        self.copy = self.sender.start(source, self.buffers[0], (axis,))

    def end(self):
        self.copy.wait_recv()
        axis = self.order[0]
        own = self.held[self.half(lax.axis_index(axis))]
        total = own.astype(f32) + self.buffers[0][...].astype(f32)
        self.held = self.buffers.pop(0)
        self.dims.remove(axis)
        self.order.pop(0)
        if self.order:
            self.held[...] = total.astype(bf16)
            self.begin()
        else:
            self.out[...] = total

    def finish(self):
        while self.order:
            self.end()


def halves_of(rows):
    half = rows // 2 // 16 * 16
    return pl.ds(0, half), pl.ds(half, rows - half)


def last_kernel(
    fsdp,
    pair,
    peak_ref,
    small_ref,
    gains_ref,
    q_ref,
    kv_ref,
    out_ref,
    down_ref,
    gate_ref,
    up_ref,
    small_sum,
    gains_sum,
    q_sum,
    kv_sum,
    out_sum,
    ffn_out,
    peak_out,
    *scratch,
):
    scratch = list(scratch)
    stages = len(fsdp)
    sender = Sender(scratch.pop(), scratch.pop())

    def buffers(count):
        taken = scratch[:count]
        del scratch[:count]
        return taken

    down = list(reversed(fsdp))
    turned = [down[1], down[0]] + down[2:]
    with_core = fsdp + ["c"]
    small = Reduction(sender, small_ref, with_core, ["c"] + turned, buffers(stages + 1), small_sum)
    gains = Reduction(sender, gains_ref, with_core, ["c"] + down, buffers(stages + 1), gains_sum)
    q = Reduction(sender, q_ref, fsdp, down, buffers(stages), q_sum)
    kv = Reduction(sender, kv_ref, fsdp, turned, buffers(stages), kv_sum)
    upward = [down[-2]] + turned[:-2] + [down[-1]]
    outs = []
    for rows, order in zip(halves_of(out_sum.shape[0]), (turned, upward)):
        part = out_ref.at[(slice(None),) * stages + (rows,)]
        outs.append(Reduction(sender, part, fsdp, order, buffers(stages), out_sum.at[rows]))
    over = buffers(1)[0]
    peaks = buffers(stages)
    me = place_of(*pair)
    row = lax.axis_index(fsdp[0])
    meet([(axis,) for axis in with_core] + [pair])

    def send_columns(which, held):
        ffn_out[which, me] = held[me]
        return [
            sender.start(held.at[me ^ away], ffn_out.at[which, me], axes)
            for away, axes in ((1, (pair[1],)), (2, (pair[0],)), (3, pair))
        ]

    peak_out[...] = peak_ref[...]

    def send_peaks(stage):
        return sender.start(peak_out, peaks[stage], (fsdp[stage],))

    def next_peaks(stage, sent):
        sent.wait()
        sender.left.append(sent)
        peak_out[...] = jnp.maximum(peak_out[...], peaks[stage][...])
        return send_peaks(stage + 1) if stage < stages - 1 else None

    for part in (small, gains, q, outs[0], kv):
        part.begin()
    peak_sent = send_peaks(0)
    crossing = sender.start(up_ref.at[1 - row], over, (fsdp[0],))
    outs[1].begin()
    columns = send_columns(0, down_ref)
    small.end()
    gains.end()
    columns += send_columns(1, gate_ref)
    peak_sent = next_peaks(0, peak_sent)
    for part in (q, kv, outs[0]):
        part.end()
    crossing.wait_recv()
    over[...] = (up_ref[row].astype(f32) + over[...].astype(f32)).astype(bf16)
    columns += send_columns(2, over)
    for stage in range(1, stages):
        peak_sent = next_peaks(stage, peak_sent)
        for part in (outs[1], small, gains, q, kv, outs[0]):
            part.end()
    for reduction in (q, kv, outs[0], small, gains, outs[1]):
        reduction.finish()
    for copy in columns:
        copy.wait_recv()
    sender.finish()


def last_scatter(fsdp, pair, peak, small, gains, q, kv, out, down, gate, up):
    vmem = pl.BlockSpec(memory_space=pltpu.VMEM)
    stages = len(fsdp)

    def buffers(array, count, rows=None):
        lead = array.ndim - 2
        block = (rows or array.shape[-2], array.shape[-1])
        return [pltpu.VMEM((2,) * (lead - 1 - i) + block, bf16) for i in range(count)]

    scratch = (
        buffers(small, stages + 1)
        + buffers(gains, stages + 1)
        + buffers(q, stages)
        + buffers(kv, stages)
        + [buf for rows in halves_of(out.shape[-2]) for buf in buffers(out, stages, rows.size)]
        + [pltpu.VMEM(down.shape, bf16)]
        + [pltpu.VMEM(peak.shape, f32)] * stages
    )
    copies = 2 * (stages + 1) + 4 * stages + 1 + 9 + stages
    return pl.pallas_call(
        functools.partial(last_kernel, fsdp, pair),
        out_shape=tuple(jax.ShapeDtypeStruct(x.shape[-2:], f32) for x in (small, gains, q, kv, out))
        + (
            jax.ShapeDtypeStruct((3,) + down.shape, bf16),
            jax.ShapeDtypeStruct(peak.shape, f32),
        ),
        in_specs=[vmem] * 9,
        out_specs=(vmem,) * 7,
        scratch_shapes=scratch
        + [pltpu.SemaphoreType.DMA((copies,)), pltpu.SemaphoreType.DMA((copies,))],
        compiler_params=pltpu.CompilerParams(
            collective_id=2, has_side_effects=True, vmem_limit_bytes=60 << 20
        ),
    )(peak, small, gains, q, kv, out, down, gate, up)


def shards(
    fsdp,
    hidden_in,
    seq_ids,
    block_ids,
    clip_limit,
    cotangent,
    q_down,
    kv_down,
    q_up,
    kv_up,
    out_proj,
    gate_proj,
    up_proj,
    down_proj,
    in_gain,
    q_gain,
    kv_gain,
    post_gain,
):
    tokens_here, width = hidden_in.shape
    seq_row = seq_ids[0]
    block_row = block_ids[0]
    group = seq_row.shape[0]
    heads = q_up.shape[1] // (NOPE + ROPE)
    score_scale = 1.0 / math.sqrt(NOPE + ROPE)
    core = lax.axis_index("c")
    first_row = core * tokens_here
    wide, near = fsdp[1], fsdp[-1]
    pair = (wide, near)
    spread = [axis for axis in fsdp if axis not in pair]
    squares = [(fsdp[i], fsdp[i + 1]) for i in range(0, len(fsdp), 2)]
    at_wide, at_near = lax.axis_index(wide), lax.axis_index(near)
    chips = tuple(fsdp)
    count = 2 ** len(fsdp)

    small_rows = q_down.shape[0]
    q_rank = q_down.shape[1]
    small_cols = q_rank + kv_down.shape[1]

    def row(value):
        return jnp.pad(value, ((0, 0), (0, TILE - value.shape[1])))[:, None, :]

    def rows_of(*values):
        held = jnp.concatenate([row(value) for value in values], axis=1)
        return jnp.pad(held, ((0, 0), (0, 8 - len(values)), (0, 0)))

    small = jnp.concatenate([q_down, kv_down], axis=1)
    gains = rows_of(in_gain[None], post_gain[None], q_gain[None], kv_gain[None])[0]
    q_up_wide = jnp.pad(
        q_up.reshape(-1, heads, NOPE + ROPE), ((0, 0), (0, 0), (0, TILE - NOPE - ROPE))
    ).reshape(-1, heads * TILE)
    small_all, gains_all, q_up_all, kv_up_all, *pieces = first_gather(
        squares, pair, spread, small, gains, q_up_wide, kv_up, gate_proj, up_proj, down_proj
    )
    down_full = small_all.reshape(-1, small_cols)
    q_up_full = q_up_all.reshape(-1, heads * TILE)
    kv_up_full = kv_up_all.reshape(-1, kv_up.shape[1])
    devices = 2 * count

    def gain(at, size):
        return gains_all.reshape(devices, 8, TILE)[:, at, :size].reshape(-1).astype(f32)

    in_float = gain(0, in_gain.shape[0])
    post_float = gain(1, post_gain.shape[0])
    q_gain_float = gain(2, q_gain.shape[0])
    kv_gain_float = gain(3, kv_gain.shape[0])

    out_full = lax.all_gather(after(out_proj, gains_all), chips, axis=0, tiled=True)
    cot_float = cotangent.astype(f32)

    def over(pieces, axis, *ready):
        return [swap(after(piece, *ready), axis) for piece in pieces]

    def exchange(held, dims, axis):
        at, dim = lax.axis_index(axis), dims.index(axis)
        return swap(pick(held, 1 - at, dim), axis), pick(held, at, dim)

    def sum_of_cores(value):
        held = value.reshape(2, 2, 2, tokens_here, width)
        other = swap(pick(held, 1 - core, 2), "c")
        return (pick(held, core, 2).astype(f32) + other.astype(f32)).astype(bf16)

    def sum_of_chips(held):
        return square_scatter(held, wide, near, 0).reshape(tokens_here, width)

    def core_both(value):
        return both(value, swap(value, "c"), "c", 0)

    def core_sum(value):
        def rows(at):
            return lax.dynamic_slice_in_dim(value, at * tokens_here, tokens_here)

        return rows(core) + swap(rows(1 - core), "c")

    x_float = hidden_in.astype(f32)
    x_normed = rms_scale(x_float, in_float).astype(bf16)
    pre = jnp.dot(x_normed, down_full, preferred_element_type=f32)
    q_pre = pre[:, :q_rank]
    c_lat_pre = pre[:, q_rank : q_rank + KVR]
    c_rot_pre = pre[:, q_rank + KVR :]
    own_cos, own_sin = angles(seq_row, first_row, tokens_here)
    q_latent = rms_scale(q_pre, q_gain_float).astype(bf16)
    kv_latent = rms_scale(c_lat_pre, kv_gain_float).astype(bf16)
    key_rot = rotate(c_rot_pre, own_cos, own_sin).astype(bf16)
    key_rot = jnp.pad(key_rot, ((0, 0), (NOPE, TILE - NOPE - ROPE)))
    latents = core_both(jnp.concatenate([q_latent, kv_latent, key_rot], axis=1))
    q_lat_all = latents[:, :q_rank]
    kv_lat_all = latents[:, q_rank : q_rank + KVR]
    key_rot_all = latents[:, q_rank + KVR :]
    all_cos, all_sin = angles(seq_row, 0, group)
    q_full = jnp.dot(q_lat_all, q_up_full, preferred_element_type=f32)
    kv_full = jnp.dot(kv_lat_all, kv_up_full, preferred_element_type=f32).astype(bf16)
    allowed = (seq_row[None, :] == seq_row[:, None]) & (block_row[:, None] <= block_row[None, :])
    bias = jnp.where(allowed, 0.0, -1e30).astype(f32)
    axes = list(spread)
    gate_held, gate_over, gate_last, up_held, down_held = pieces
    gate_pieces = [gate_held, gate_over, gate_last, swap(gate_over, axes[1])]
    for axis in axes[2:]:
        gate_pieces += over(gate_pieces, axis)
    other_pieces = []
    for piece in (up_held, down_held):
        other_pieces += [swap(piece, axes[0]), swap(piece, axes[1])]
    attn, queries, log_total, local_peak = attend(
        q_full, kv_full, key_rot_all, tables(all_cos, all_sin), bias, score_scale
    )
    attn, *early = lax.optimization_barrier((attn, *other_pieces, *gate_pieces))
    other_pieces, gate_pieces = early[:4], early[4:]
    d_ffn = (resid_scale * cot_float).astype(bf16)
    d_ffn_all = lax.all_gather(after(d_ffn, attn), (wide, near, "c"), axis=0, tiled=True)
    branch = core_sum(contract(attn, out_full, 1, 1))
    mid = x_float + resid_scale * branch
    mid_normed = rms_scale(mid, post_float).astype(bf16)
    gate_full = lay(gate_pieces, fsdp, pair, spread)
    mid_all = tokens_of_chips(after(mid_normed, gate_full), pair, 1)
    up_pieces = [up_held, *other_pieces[:2], swap(after(other_pieces[0], attn), axes[1])]
    down_pieces = [down_held, *other_pieces[2:], swap(after(other_pieces[2], attn), axes[1])]
    for axis in axes[2:]:
        up_pieces += over(up_pieces, axis)
        down_pieces += over(down_pieces, axis)
    mid_all, *late = lax.optimization_barrier((mid_all, *up_pieces, *down_pieces))
    up_pieces, down_pieces = late[: len(up_pieces)], late[len(up_pieces) :]
    up_full = lay(up_pieces, fsdp, pair, spread)
    gate = jnp.dot(mid_all, gate_full, preferred_element_type=f32)
    up_value = jnp.dot(mid_all, up_full, preferred_element_type=f32)
    down_proj_full = lay(down_pieces, fsdp, pair, spread)
    sigmoid = jax.nn.sigmoid(gate)
    silu_value = gate * sigmoid
    act = (silu_value * up_value).astype(bf16)

    d_act = jnp.dot(d_ffn_all, down_proj_full, preferred_element_type=f32)
    d_gate = (d_act * up_value * (sigmoid * (1.0 + gate * (1.0 - sigmoid)))).astype(bf16)
    d_up = (d_act * silu_value).astype(bf16)
    dims = list(fsdp)
    first, last = spread[0], spread[-1]

    def added(parts):
        return (parts[0].astype(f32) + parts[1].astype(f32)).astype(bf16)

    def inner(held):
        left = [axis for axis in dims if axis != last]
        for axis in reversed(spread[1:-1]):
            held = added(exchange(held, left, axis))
            left.remove(axis)
        return held

    def begin(left, right, *ready):
        keep, send = grad_halves(left, right, width // count, last)
        shape = [2] * (len(fsdp) - 1) + [width // count, -1]
        return swap(after(send, *ready), last).reshape(shape), keep.reshape(shape), keep

    def cross(held):
        return exchange(held, [first, *pair], first)

    *down_parts, down_grad = begin(d_ffn_all, act)
    d_gate_late, _ = lax.optimization_barrier((d_gate, down_grad))
    gate_keep, gate_send = grad_halves(mid_all, d_gate_late, width // count, last)
    d_up_late, d_gate_late, _ = lax.optimization_barrier((d_up, d_gate, gate_keep))
    d_mid_part = features((d_gate_late, gate_full), (d_up_late, up_full))
    d_mid_part, *down_parts = lax.optimization_barrier((d_mid_part, *down_parts))
    d_mid_held = sum_of_cores(d_mid_part)
    d_mid_normed = sum_of_chips(d_mid_held)
    mid_late, gate_send, _ = lax.optimization_barrier((mid_all, gate_send, d_mid_held))
    shape = [2] * (len(fsdp) - 1) + [width // count, -1]
    gate_parts = (swap(gate_send, last).reshape(shape), gate_keep.reshape(shape))
    down_parts = cross(inner(added(down_parts)))
    *up_parts, up_grad = begin(mid_late, d_up, gate_parts[0])
    ffn_part = features((after(act, up_grad), down_proj_full))
    post_pull = jax.vjp(rms_scale, mid, post_float)[1]
    d_mid_normed, *early = lax.optimization_barrier(
        (d_mid_normed, *down_parts, *gate_parts, ffn_part)
    )
    down_parts, gate_parts, ffn_part = early[:2], early[2:4], early[4]
    d_mid_norm, post_grad = post_pull(d_mid_normed)
    ffn = lax.psum_scatter(
        after(ffn_part, d_mid_norm), (wide, near, "c"), scatter_dimension=0, tiled=True
    )
    layer_out = (mid + resid_scale * ffn.astype(f32)).astype(bf16)
    d_mid = cot_float + d_mid_norm
    d_branch = (resid_scale * d_mid).astype(bf16)
    d_branch_all = core_both(d_branch)
    d_attn = jnp.dot(d_branch_all, out_full, preferred_element_type=f32).astype(bf16)
    gate_parts = cross(inner(added(gate_parts)))
    d_q, d_kv, d_rot_part = attend_back(
        queries,
        kv_full,
        d_attn,
        log_total,
        key_rot_all,
        tables(all_cos, -all_sin),
        bias,
        score_scale,
    )
    q_up_grad = heads_grad(q_lat_all, d_q)
    d_q, d_kv, q_up_grad, *early = lax.optimization_barrier(
        (d_q, d_kv, q_up_grad, *gate_parts, *up_parts)
    )
    gate_parts, up_parts = early[:2], early[2:]
    out_grad = rows_first(contract(after(d_branch_all, d_q), attn, 0, 0).astype(bf16))
    kv_up_grad = rows_first(contract(kv_lat_all, d_kv, 0, 0).astype(bf16))
    d_q_lat_part = contract(d_q, q_up_full, 1, 1)
    d_kv_lat_part = contract(d_kv, kv_up_full, 1, 1)
    d_latents = core_sum(jnp.concatenate([d_q_lat_part, d_kv_lat_part, d_rot_part], axis=1))
    q_pull = jax.vjp(rms_scale, q_pre, q_gain_float)[1]
    d_q_pre, q_gain_grad = q_pull(d_latents[:, :q_rank])
    kv_pull = jax.vjp(rms_scale, c_lat_pre, kv_gain_float)[1]
    d_c_lat, kv_gain_grad = kv_pull(d_latents[:, q_rank : q_rank + KVR])
    d_key_rot = d_latents[:, q_rank + KVR + NOPE : q_rank + KVR + NOPE + ROPE]
    d_pre = jnp.concatenate(
        [d_q_pre, d_c_lat, rotate(d_key_rot, own_cos, -own_sin)], axis=-1
    ).astype(bf16)
    down_grads = rows_first(contract(x_normed, d_pre, 0, 0).astype(bf16))
    d_x_normed = contract(d_pre, down_full, 1, 1)
    in_pull = jax.vjp(rms_scale, x_float, in_float)[1]
    d_x_norm, in_grad = in_pull(d_x_normed)
    input_grad = d_mid + d_x_norm

    rows_here = width // count
    ffn_held = [
        added(down_parts).reshape(4, rows_here, -1),
        added(gate_parts).reshape(4, rows_here, -1),
        inner(added(up_parts)).reshape(2, 4, rows_here, -1),
    ]
    gain_grads = rows_of(
        *(grad.reshape(devices, -1) for grad in (in_grad, post_grad, q_gain_grad, kv_gain_grad))
    ).astype(bf16)

    def blocks(grad, lead):
        return grad.reshape([2] * lead + [grad.shape[0] // 2**lead, -1])

    small_out, gain_out, q_up_out, kv_up_out, out_out, ffn_cols, peak_all = last_scatter(
        fsdp,
        pair,
        local_peak,
        blocks(down_grads, len(fsdp) + 1),
        gain_grads.reshape([2] * (len(fsdp) + 1) + [8, TILE]),
        blocks(q_up_grad, len(fsdp)),
        blocks(kv_up_grad, len(fsdp)),
        blocks(out_grad, len(fsdp)),
        *ffn_held,
    )
    down_out, gate_out, up_out = (merge(ffn_cols, which) for which in range(3))
    peaks = peak_all[0, :heads]
    limit = clip_limit[0]
    factors = limit / jnp.maximum(peaks, limit)
    root = jnp.sqrt(factors)
    q_cols = jnp.concatenate(
        [
            jnp.broadcast_to(root[:, None], (heads, NOPE)),
            jnp.broadcast_to(factors[:, None], (heads, ROPE)),
        ],
        axis=1,
    ).reshape(heads * (NOPE + ROPE))
    kv_cols = jnp.concatenate(
        [jnp.broadcast_to(root[:, None], (heads, NOPE)), jnp.ones((heads, VD), f32)], axis=1
    ).reshape(heads * (NOPE + VD))
    q_clipped = (q_up.astype(f32) * q_cols[None, :]).astype(bf16)
    kv_clipped = (kv_up.astype(f32) * kv_cols[None, :]).astype(bf16)
    return (
        layer_out,
        input_grad,
        small_out[:, :q_rank],
        small_out[:, q_rank:],
        q_up_out,
        kv_up_out,
        out_out,
        gate_out,
        up_out,
        down_out,
        gain_out[0, : in_gain.shape[0]],
        gain_out[2, : q_gain.shape[0]],
        gain_out[3, : kv_gain.shape[0]],
        gain_out[1, : post_gain.shape[0]],
        q_clipped,
        kv_clipped,
        peaks,
        factors,
    )


def solution(mesh):
    bits = mesh.shape["fsdp"].bit_length() - 1
    fsdp = [f"f{i}" for i in range(bits)]
    fine = Mesh(mesh.devices.reshape((2,) * (bits + 1)), tuple(fsdp) + ("c",))
    split = tuple(fsdp)
    whole = split + ("c",)
    return jax.shard_map(
        functools.partial(shards, fsdp),
        mesh=fine,
        in_specs=(
            P(whole, None),
            P(split, None),
            P(split, None),
            P(),
            P(whole, None),
            P(whole, None),
            P(whole, None),
            P(split, "c"),
            P(split, "c"),
            P(split, "c"),
            P(split, "c"),
            P(split, "c"),
            P(split, "c"),
            P(whole),
            P(whole),
            P(whole),
            P(whole),
        ),
        out_specs=(
            P(whole, None),
            P(whole, None),
            P(whole, None),
            P(whole, None),
            P(split, "c"),
            P(split, "c"),
            P(split, "c"),
            P(split, "c"),
            P(split, "c"),
            P(split, "c"),
            P(whole),
            P(whole),
            P(whole),
            P(whole),
            P(split, "c"),
            P(split, "c"),
            P("c"),
            P("c"),
        ),
        check_vma=False,
    )
```

```python
import functools
import math

import jax
import jax.numpy as jnp
from jax import lax
from jax.experimental import pallas as pl
from jax.experimental.pallas import tpu as pltpu
from jax.experimental.layout import Layout, with_layout_constraint
from jax.sharding import Mesh
from jax.sharding import PartitionSpec as P

NOPE = 64
ROPE = 32
VD = 64
KVR = 256
TILE = 128


eps = 1e-05
resid_scale = 1.4 / math.sqrt(62.0)
rope_base = 10000.0
SWAP = [(0, 1), (1, 0)]
f32 = jnp.float32
bf16 = jnp.bfloat16


def rms_scale(value, gain):
    return value * lax.rsqrt(jnp.mean(value * value, axis=-1, keepdims=True) + eps) * gain


def rotate(value, cosine, sine):
    half = value.shape[-1] // 2
    first = value[..., :half]
    second = value[..., half:]
    return jnp.concatenate(
        [first * cosine - second * sine, second * cosine + first * sine], axis=-1
    )


def angles(seq_row, start, count):
    own_ids = lax.dynamic_slice_in_dim(seq_row, start, count)
    earlier = jnp.sum((seq_row[None, :] < own_ids[:, None]).astype(jnp.int32), axis=1)
    place = (start + jnp.arange(count, dtype=jnp.int32) - earlier).astype(f32)
    freq = jnp.power(rope_base, -jnp.arange(ROPE // 2, dtype=f32) * (2.0 / ROPE))
    turn = place[:, None] * freq[None, :]
    return (jnp.cos(turn), jnp.sin(turn))


def contract(left, right, left_dim, right_dim):
    return lax.dot_general(
        left, right, (((left_dim,), (right_dim,)), ((), ())), preferred_element_type=f32
    )


def turn(value, plain, first, second):
    return (
        value * plain
        + pltpu.roll(value, TILE - ROPE // 2, 1) * first
        + pltpu.roll(value, ROPE // 2, 1) * second
    )


def tables(cosine, sine):
    rows = cosine.shape[0]
    half = ROPE // 2

    def zeros(count):
        return jnp.zeros((rows, count), f32)

    plain = jnp.concatenate([jnp.ones((rows, NOPE), f32), cosine, cosine, zeros(TILE - NOPE - ROPE)], axis=1)
    first = jnp.concatenate([zeros(NOPE), -sine, zeros(TILE - NOPE - half)], axis=1)
    second = jnp.concatenate([zeros(NOPE + half), sine, zeros(TILE - NOPE - ROPE)], axis=1)
    return plain, first, second


def attend_kernel(
    scale,
    q_ref,
    kv_ref,
    rot_ref,
    plain_ref,
    first_ref,
    second_ref,
    bias_ref,
    mixed_ref,
    query_ref,
    total_ref,
    peak_ref,
):
    step = pl.program_id(0)
    lane = lax.broadcasted_iota(jnp.int32, (q_ref.shape[0], TILE), 1)
    spot = lax.broadcasted_iota(jnp.int32, peak_ref.shape, 1)

    @pl.when(step == 0)
    def _():
        peak_ref[...] = jnp.zeros_like(peak_ref)

    outs = []
    for one in range(2):
        cols = slice(one * TILE, (one + 1) * TILE)
        query = turn(q_ref[:, cols], plain_ref[...], first_ref[...], second_ref[...]).astype(bf16)
        query_ref[:, cols] = query
        kv = kv_ref[:, cols]
        keys = jnp.where(lane < NOPE, kv, rot_ref[...])
        masked = contract(keys, query, 1, 1) * scale + bias_ref[...]
        top = jnp.max(masked, axis=0, keepdims=True)
        weights = jnp.exp(masked - top)
        total = jnp.sum(weights, axis=0, keepdims=True)
        chance = (weights * (1.0 / total)).astype(bf16)
        outs.append(contract(chance, kv, 0, 0))
        total_ref[0, one : one + 1, :] = top + jnp.log(total)
        peak_ref[...] = jnp.where(spot == step * 2 + one, jnp.max(top), peak_ref[...])
    mixed_ref[...] = jnp.where(lane < VD, pltpu.roll(outs[0], VD, 1), outs[1]).astype(bf16)


def attend(q, kv, rot, turns, bias, scale):
    group, cols = q.shape
    heads = cols // TILE
    whole = pl.BlockSpec((group, TILE), lambda i: (0, 0))
    two = pl.BlockSpec((group, 2 * TILE), lambda i: (0, i))
    return pl.pallas_call(
        functools.partial(attend_kernel, scale),
        grid=(heads // 2,),
        out_shape=(
            jax.ShapeDtypeStruct((group, heads * VD), bf16),
            jax.ShapeDtypeStruct((group, cols), bf16),
            jax.ShapeDtypeStruct((heads // 2, 2, group), f32),
            jax.ShapeDtypeStruct((8, TILE), f32),
        ),
        in_specs=[two, two, whole, whole, whole, whole, pl.BlockSpec((group, group), lambda i: (0, 0))],
        out_specs=(
            pl.BlockSpec((group, TILE), lambda i: (0, i)),
            two,
            pl.BlockSpec((1, 2, group), lambda i: (i, 0, 0)),
            pl.BlockSpec((8, TILE), lambda i: (0, 0)),
        ),
        compiler_params=pltpu.CompilerParams(
            dimension_semantics=("arbitrary",), vmem_limit_bytes=40 << 20
        ),
        cost_estimate=pl.CostEstimate(flops=1, transcendentals=0, bytes_accessed=1),
    )(q, kv, rot, *turns, bias)


def attend_back_kernel(
    scale,
    query_ref,
    kv_ref,
    d_mixed_ref,
    total_ref,
    rot_ref,
    plain_ref,
    first_ref,
    second_ref,
    bias_ref,
    d_q_ref,
    d_kv_ref,
    d_rot_ref,
):
    step = pl.program_id(0)
    lane = lax.broadcasted_iota(jnp.int32, (query_ref.shape[0], TILE), 1)

    @pl.when(step == 0)
    def _():
        d_rot_ref[...] = jnp.zeros_like(d_rot_ref)

    pair = d_mixed_ref[...].astype(f32)
    for one in range(2):
        cols = slice(one * TILE, (one + 1) * TILE)
        query = query_ref[:, cols]
        kv = kv_ref[:, cols]
        keys = jnp.where(lane < NOPE, kv, rot_ref[...])
        own = pair if one else pltpu.roll(pair, VD, 1)
        d_mixed = jnp.where(lane < VD, 0.0, own).astype(bf16)
        masked = contract(keys, query, 1, 1) * scale + bias_ref[...]
        chance = jnp.exp(masked - total_ref[0, one : one + 1, :])
        d_values = contract(chance.astype(bf16), d_mixed, 1, 0)
        d_chance = contract(kv, d_mixed, 1, 1)
        inner = jnp.sum(chance * d_chance, axis=0, keepdims=True)
        d_raw = (chance * (d_chance - inner) * scale).astype(bf16)
        d_keys = contract(d_raw, query, 1, 0)
        d_query = contract(d_raw, keys, 0, 0)
        d_q_ref[:, cols] = turn(
            d_query, plain_ref[...], first_ref[...], second_ref[...]
        ).astype(bf16)
        d_kv_ref[:, cols] = jnp.where(lane < NOPE, d_keys, d_values).astype(bf16)
        d_rot_ref[...] += d_keys


def attend_back(query, kv, d_mixed, total, rot, turns, bias, scale):
    group, cols = query.shape
    heads = cols // TILE
    whole = pl.BlockSpec((group, TILE), lambda i: (0, 0))
    two = pl.BlockSpec((group, 2 * TILE), lambda i: (0, i))
    return pl.pallas_call(
        functools.partial(attend_back_kernel, scale),
        grid=(heads // 2,),
        out_shape=(
            jax.ShapeDtypeStruct((group, cols), bf16),
            jax.ShapeDtypeStruct((group, cols), bf16),
            jax.ShapeDtypeStruct((group, TILE), f32),
        ),
        in_specs=[
            two,
            two,
            pl.BlockSpec((group, TILE), lambda i: (0, i)),
            pl.BlockSpec((1, 2, group), lambda i: (i, 0, 0)),
            whole,
            whole,
            whole,
            whole,
            pl.BlockSpec((group, group), lambda i: (0, 0)),
        ],
        out_specs=(two, two, whole),
        compiler_params=pltpu.CompilerParams(
            dimension_semantics=("arbitrary",), vmem_limit_bytes=40 << 20
        ),
        cost_estimate=pl.CostEstimate(flops=1, transcendentals=0, bytes_accessed=1),
    )(query, kv, d_mixed, total, rot, *turns, bias)


def swap(value, axis):
    return lax.ppermute(value, axis, SWAP)


def far(value, pair):
    return lax.ppermute(value, pair, [(i, 3 - i) for i in range(4)])


def after(value, *others):
    return lax.optimization_barrier((value,) + others)[0]


def pick(value, at, dim):
    return lax.dynamic_index_in_dim(value, at, dim, keepdims=True)


def both(own, other, axis, dim):
    here = lax.axis_index(axis) == 0
    return jnp.concatenate([jnp.where(here, own, other), jnp.where(here, other, own)], axis=dim)


def heads_grad_kernel(latent_ref, d_ref, out_ref):
    total = contract(latent_ref[...], d_ref[...], 0, 0)
    parts = [total[:, i * TILE : i * TILE + NOPE + ROPE] for i in range(4)]
    out_ref[...] = jnp.concatenate(parts, axis=1).astype(bf16)


def heads_grad(latent, d_heads):
    group, rank = latent.shape
    packs = d_heads.shape[1] // (4 * TILE)
    cols = 4 * (NOPE + ROPE)
    return pl.pallas_call(
        heads_grad_kernel,
        grid=(packs,),
        out_shape=jax.ShapeDtypeStruct((rank, packs * cols), bf16),
        in_specs=[
            pl.BlockSpec((group, rank), lambda i: (0, 0)),
            pl.BlockSpec((group, 4 * TILE), lambda i: (0, i)),
        ],
        out_specs=pl.BlockSpec((rank, cols), lambda i: (0, i)),
        compiler_params=pltpu.CompilerParams(vmem_limit_bytes=32 << 20),
        cost_estimate=pl.CostEstimate(flops=1, transcendentals=0, bytes_accessed=1),
    )(latent, d_heads)


def features_kernel(*refs):
    out_ref = refs[-1]
    total = contract(refs[0][...], refs[1][...], 1, 1)
    for i in range(2, len(refs) - 1, 2):
        total += contract(refs[i][...], refs[i + 1][...], 1, 1)
    out_ref[...] = total.astype(bf16)


def features(*pairs):
    rows, cols = pairs[0][0].shape
    width = pairs[0][1].shape[0]
    tile = min(rows, 512)
    return pl.pallas_call(
        features_kernel,
        grid=(rows // tile,),
        out_shape=jax.ShapeDtypeStruct((rows, width), bf16),
        in_specs=[
            pl.BlockSpec((tile, cols), lambda i: (i, 0)),
            pl.BlockSpec((width, cols), lambda i: (0, 0)),
        ]
        * len(pairs),
        out_specs=pl.BlockSpec((tile, width), lambda i: (i, 0)),
        compiler_params=pltpu.CompilerParams(vmem_limit_bytes=56 << 20),
        cost_estimate=pl.CostEstimate(flops=1, transcendentals=0, bytes_accessed=1),
    )(*(array for pair in pairs for array in pair))


def core_features_kernel(*refs):
    *operands, out_ref, total, sent, got, send_sems, recv_sems = refs
    step = pl.program_id(0)
    core = lax.axis_index("c")
    half = total.shape[1]

    @pl.when(step == 0)
    def _():
        meet([("c",)])

    def copy(at):
        return pltpu.make_async_remote_copy(
            src_ref=sent.at[at],
            dst_ref=got.at[at],
            send_sem=send_sems.at[at],
            recv_sem=recv_sems.at[at],
            device_id=other_of(("c",)),
            device_id_type=pl.DeviceIdType.MESH,
        )

    value = contract(operands[0][...], operands[1][...], 1, 1)
    for i in range(2, len(operands), 2):
        value += contract(operands[i][...], operands[i + 1][...], 1, 1)
    total[0] = value[:half].astype(bf16)
    total[1] = value[half:].astype(bf16)
    sent[step] = total[1 - core]
    copy(step).start()
    out_ref[step] = total[core]

    @pl.when(step == pl.num_programs(0) - 1)
    def _():
        for at in range(out_ref.shape[0]):
            copy(at).wait()
            out_ref[at] = (out_ref[at].astype(f32) + got[at].astype(f32)).astype(bf16)


def core_features(rows, number, *pairs):
    cols = pairs[0][0].shape[1]
    width = pairs[0][1].shape[0]
    block = (4, rows, width)
    return pl.pallas_call(
        core_features_kernel,
        grid=(4,),
        out_shape=jax.ShapeDtypeStruct(block, bf16),
        in_specs=[
            pl.BlockSpec((2 * rows, cols), lambda i: (i, 0)),
            pl.BlockSpec((width, cols), lambda i: (0, 0), pipeline_mode=pl.Buffered(1)),
        ]
        * len(pairs),
        out_specs=pl.BlockSpec(block, lambda i: (0, 0, 0)),
        scratch_shapes=[
            pltpu.VMEM((2, rows, width), bf16),
            pltpu.VMEM(block, bf16),
            pltpu.VMEM(block, bf16),
            pltpu.SemaphoreType.DMA((4,)),
            pltpu.SemaphoreType.DMA((4,)),
        ],
        compiler_params=pltpu.CompilerParams(
            dimension_semantics=("arbitrary",),
            collective_id=number,
            has_side_effects=True,
            vmem_limit_bytes=58 << 20,
        ),
        cost_estimate=pl.CostEstimate(flops=1, transcendentals=0, bytes_accessed=1),
    )(*(array for pair in pairs for array in pair))


def grad_kernel(axis, left_ref, right_ref, keep_ref, send_ref, total):
    half = total.shape[1]
    value = contract(left_ref[...], right_ref[...], 0, 0).astype(bf16)
    total[0] = value[:half]
    total[1] = value[half:]
    at = lax.axis_index(axis)
    keep_ref[0] = total[at]
    send_ref[0] = total[1 - at]


def grad_halves(left, right, rows, axis):
    tokens, width = left.shape
    cols = right.shape[1]
    tile = 4 * rows
    if tile % TILE:
        held = rows_first(contract(left, right, 0, 0).astype(bf16)).reshape(-1, 2, 2 * rows, cols)
        at = lax.axis_index(axis)
        return tuple(pick(held, i, 1)[:, 0] for i in (at, 1 - at))
    out = jax.ShapeDtypeStruct((width // tile, 2 * rows, cols), bf16)
    return pl.pallas_call(
        functools.partial(grad_kernel, axis),
        grid=(width // tile,),
        out_shape=(out, out),
        in_specs=[
            pl.BlockSpec((tokens, tile), lambda i: (0, i)),
            pl.BlockSpec((tokens, cols), lambda i: (0, 0)),
        ],
        out_specs=(pl.BlockSpec((1, 2 * rows, cols), lambda i: (i, 0, 0)),) * 2,
        scratch_shapes=[pltpu.VMEM((2, 2 * rows, cols), bf16)],
        compiler_params=pltpu.CompilerParams(vmem_limit_bytes=56 << 20),
        cost_estimate=pl.CostEstimate(flops=1, transcendentals=0, bytes_accessed=1),
    )(left, right)


def rows_first(value):
    return with_layout_constraint(value, Layout(major_to_minor=(0, 1)))


def square_scatter(held, first, second, dim):
    here, there = lax.axis_index(first), lax.axis_index(second)

    def part(w, n):
        return pick(pick(held, w, dim), n, dim + 1)

    near = swap(part(here, 1 - there).astype(bf16), second)
    wide = swap(part(1 - here, there).astype(bf16), first)
    corner = far(part(1 - here, 1 - there).astype(bf16), (first, second))
    own = part(here, there).astype(f32)
    return own + near.astype(f32) + wide.astype(f32) + corner.astype(f32)


def place_of(first, second):
    return lax.axis_index(first) * 2 + lax.axis_index(second)


def other_of(axes):
    return {axis: 1 - lax.axis_index(axis) for axis in axes}


def meet(partners):
    barrier = pltpu.get_barrier_semaphore()
    for axes in partners:
        pl.semaphore_signal(
            barrier, inc=1, device_id=other_of(axes), device_id_type=pl.DeviceIdType.MESH
        )
    pl.semaphore_wait(barrier, len(partners))


class Sender:
    def __init__(self, send_sems, recv_sems):
        self.send_sems, self.recv_sems, self.all, self.left = send_sems, recv_sems, [], []

    def start(self, source, target, axes):
        copy = pltpu.make_async_remote_copy(
            src_ref=source,
            dst_ref=target,
            send_sem=self.send_sems.at[len(self.all)],
            recv_sem=self.recv_sems.at[len(self.all)],
            device_id=other_of(axes),
            device_id_type=pl.DeviceIdType.MESH,
        )
        copy.start()
        self.all.append(copy)
        return copy

    def finish(self):
        for copy in self.all:
            if all(copy is not other for other in self.left):
                copy.wait_send()


def first_kernel(
    squares,
    pair,
    spread,
    small_ref,
    gains_ref,
    q_ref,
    kv_ref,
    gate_ref,
    up_ref,
    down_ref,
    small_out,
    gains_out,
    q_out,
    kv_out,
    gate_out,
    gate_over,
    gate_last,
    up_out,
    down_out,
    staged,
    send_sems,
    recv_sems,
):
    core = lax.axis_index("c")
    places = [place_of(*square) for square in squares]
    me = place_of(*pair)
    sender = Sender(send_sems, recv_sems)
    cols = staged.shape[3]

    small_out[(*places, core)] = small_ref[...]
    gains_out[(*places, core)] = gains_ref[...]
    q_out[tuple(places)] = q_ref[...]
    kv_out[tuple(places)] = kv_ref[...]
    partners = [axes for one, two in squares for axes in ((two,), (one,), (one, two))]
    meet(partners + [pair, ("c",)])

    def blocks(ref, stage, place, tail, lead=()):
        index = lead + (slice(None),) * (stage - len(lead)) + (place,) + tuple(places[stage + 1 :])
        return ref.at[index + tail]

    early = [(small_out, (core,)), (gains_out, (core,))]
    later = [(q_out, ()), (kv_out, ())]

    def send_first(ref, tail):
        mine = blocks(ref, 0, places[0], tail)
        return [sender.start(mine, mine, axes) for axes in partners[:3]]

    def send_square(ref, tail, stage):
        one, two = squares[stage]
        mine = blocks(ref, stage, places[stage], tail)
        return [sender.start(mine, mine, (two,)), sender.start(mine, mine, (one,))]

    def pass_on(ref, tail, stage, copies):
        one, two = squares[stage]
        copies[0].wait_recv()
        half = blocks(ref, stage, places[stage] ^ 1, tail, (slice(0, 2),))
        first = sender.start(half, half, (one,))
        copies[1].wait_recv()
        half = blocks(ref, stage, places[stage] ^ 2, tail, (slice(2, 4),))
        return [first, sender.start(half, half, (two,))]

    def wait(copies):
        for copy in copies:
            copy.wait_recv()

    targets = (gate_out, up_out, down_out)

    def send_columns(away, axes):
        return [
            sender.start(staged.at[which, me ^ away], target.at[me], axes)
            for which, target in enumerate(targets)
        ]

    first = [send_first(*item) for item in early]
    for which, weight_ref in enumerate((gate_ref, up_ref, down_ref)):
        for quarter in range(4):
            staged[which, quarter] = weight_ref[:, quarter * cols : (quarter + 1) * cols]
    columns = [send_columns(1, (pair[1],))]
    for which, target in enumerate(targets):
        target[me] = staged[which, me]
    for copies in first:
        wait(copies)
    sent = [send_square(*item, 1) for item in early]
    first_later = [send_first(*item) for item in later]
    columns.append(send_columns(2, (pair[0],)))
    for stage in range(1, len(squares)):
        if stage > 1:
            sent = [send_square(*item, stage) for item in early]
        passed = [pass_on(*item, stage, copies) for item, copies in zip(early, sent)]
        if stage == 1:
            for copies in first_later:
                wait(copies)
            sent_later = [send_square(*item, 1) for item in later]
            columns.append(send_columns(3, pair))
        for copies in passed:
            wait(copies)
    mine = (slice(None),) * len(squares) + (core,)
    core_sent = [sender.start(ref.at[mine], ref.at[mine], ("c",)) for ref, _ in early]
    for copies in columns:
        copies[0].wait_recv()
    over = [
        sender.start(gate_out, gate_over, (spread[0],)),
        sender.start(gate_out, gate_last, (spread[1],)),
    ]
    for stage in range(1, len(squares)):
        if stage > 1:
            sent_later = [send_square(*item, stage) for item in later]
        passed = [pass_on(*item, stage, copies) for item, copies in zip(later, sent_later)]
        for copies in passed:
            wait(copies)
    wait(core_sent)
    for copies in columns:
        wait(copies[1:])
    wait(over)
    sender.finish()


def first_gather(squares, pair, spread, small, gains, q_up, kv_up, gate, up, down):
    vmem = pl.BlockSpec(memory_space=pltpu.VMEM)
    rows, cols = gate.shape
    lead = (4,) * len(squares)
    copies = 12 + 16 * (len(squares) - 1) + 2 + 9 + 2
    return pl.pallas_call(
        functools.partial(first_kernel, squares, pair, spread),
        out_shape=(
            jax.ShapeDtypeStruct(lead + (2,) + small.shape, bf16),
            jax.ShapeDtypeStruct(lead + (2,) + gains.shape, bf16),
            jax.ShapeDtypeStruct(lead + q_up.shape, bf16),
            jax.ShapeDtypeStruct(lead + kv_up.shape, bf16),
        )
        + (jax.ShapeDtypeStruct((4, rows, cols // 4), bf16),) * 5,
        in_specs=[vmem] * 7,
        out_specs=(vmem,) * 9,
        scratch_shapes=[
            pltpu.VMEM((3, 4, rows, cols // 4), bf16),
            pltpu.SemaphoreType.DMA((copies,)),
            pltpu.SemaphoreType.DMA((copies,)),
        ],
        compiler_params=pltpu.CompilerParams(
            collective_id=0, has_side_effects=True, vmem_limit_bytes=48 << 20
        ),
    )(small, gains, q_up, kv_up, gate, up, down)


def second_kernel(
    squares,
    pair,
    over,
    rows_ref,
    value_ref,
    piece_ref,
    rows_out,
    tokens_out,
    piece_out,
    send_sems,
    recv_sems,
):
    core = lax.axis_index("c")
    places = [place_of(*square) for square in squares]
    me = place_of(*pair)
    one, two = pair
    half = value_ref.shape[0] // 2
    sender = Sender(send_sems, recv_sems)
    rows_out[tuple(places)] = rows_ref[...]
    tokens_out[me, core] = value_ref[...]
    partners = [axes for one_, two_ in squares for axes in ((two_,), (one_,), (one_, two_))]
    meet(partners + [("c",)])

    def blocks(stage, place, lead=()):
        index = lead + (slice(None),) * (stage - len(lead)) + (place,) + tuple(places[stage + 1 :])
        return rows_out.at[index]

    def send_rows(place, axes, rows=slice(None)):
        mine = tokens_out.at[place, core, rows]
        return sender.start(mine, mine, axes)

    mine = blocks(0, places[0])
    first = [sender.start(mine, mine, axes) for axes in partners[:3]]
    near = send_rows(me, (two,))
    wide = send_rows(me, (one,))
    got = [send_rows(me, ("c",))]
    for copy in first:
        copy.wait_recv()
    crossing = sender.start(piece_ref, piece_out, (over,))
    for stage in range(1, len(squares)):
        up, across = squares[stage]
        mine = blocks(stage, places[stage])
        beside = sender.start(mine, mine, (across,))
        above = sender.start(mine, mine, (up,))
        if stage == 1:
            near.wait_recv()
            corner = [send_rows(me ^ 1, (one,), slice(0, half))]
            got.append(send_rows(me ^ 1, ("c",)))
            wide.wait_recv()
            corner.append(send_rows(me ^ 2, (two,), slice(half, 2 * half)))
            got.append(send_rows(me ^ 2, ("c",)))
        beside.wait_recv()
        part = blocks(stage, places[stage] ^ 1, (slice(0, 2),))
        passed = [sender.start(part, part, (up,))]
        above.wait_recv()
        part = blocks(stage, places[stage] ^ 2, (slice(2, 4),))
        passed.append(sender.start(part, part, (across,)))
        if stage == 1:
            for copy in corner:
                copy.wait_recv()
            got.append(send_rows(me ^ 3, ("c",)))
        for copy in passed:
            copy.wait_recv()
    for copy in got:
        copy.wait_recv()
    crossing.wait_recv()
    sender.finish()


def second_gather(squares, pair, over, rows, value, piece):
    vmem = pl.BlockSpec(memory_space=pltpu.VMEM)
    copies = 3 + 4 * (len(squares) - 1) + 9
    gathered, tokens, crossed = pl.pallas_call(
        functools.partial(second_kernel, squares, pair, over),
        out_shape=(
            jax.ShapeDtypeStruct((4,) * len(squares) + rows.shape, bf16),
            jax.ShapeDtypeStruct((4, 2) + value.shape, bf16),
            jax.ShapeDtypeStruct(piece.shape, bf16),
        ),
        in_specs=[vmem] * 3,
        out_specs=(vmem,) * 3,
        scratch_shapes=[pltpu.SemaphoreType.DMA((copies,)), pltpu.SemaphoreType.DMA((copies,))],
        compiler_params=pltpu.CompilerParams(
            collective_id=4, has_side_effects=True, vmem_limit_bytes=40 << 20
        ),
        cost_estimate=pl.CostEstimate(flops=1, transcendentals=0, bytes_accessed=1),
    )(rows, value, piece)
    return gathered.reshape(-1, rows.shape[1]), tokens.reshape(-1, value.shape[1]), crossed


def lay_copies(fsdp, pair, spread, pieces, target, sems):
    copies = []
    for number, piece in enumerate(pieces):
        for block in range(4):
            place = 0
            for axis in fsdp:
                if axis == pair[0]:
                    bit = block >> 1
                elif axis == pair[1]:
                    bit = block & 1
                else:
                    bit = lax.axis_index(axis) ^ ((number >> spread.index(axis)) & 1)
                place = place * 2 + bit
            copies.append(pltpu.make_async_copy(piece.at[block], target.at[place], sems.at[len(copies)]))
    for copy in copies:
        copy.start()
    return copies


def lay_kernel(fsdp, pair, spread, *refs):
    count = 2 ** len(spread)
    target, sems = refs[count:]
    for copy in lay_copies(fsdp, pair, spread, refs[:count], target, sems):
        copy.wait()


def lay(pieces, fsdp, pair, spread):
    rows, cols = pieces[0].shape[1:]
    blocks = 4 * len(pieces)
    out = pl.pallas_call(
        functools.partial(lay_kernel, fsdp, pair, spread),
        out_shape=jax.ShapeDtypeStruct((blocks, rows, cols), bf16),
        in_specs=[pl.BlockSpec(memory_space=pltpu.HBM)] * len(pieces),
        out_specs=pl.BlockSpec(memory_space=pltpu.VMEM),
        scratch_shapes=[pltpu.SemaphoreType.DMA((blocks,))],
        compiler_params=pltpu.CompilerParams(vmem_limit_bytes=32 << 20),
        cost_estimate=pl.CostEstimate(
            flops=0, transcendentals=0, bytes_accessed=4 * blocks * rows * cols
        ),
    )(*pieces)
    return out.reshape(blocks * rows, cols)


def tokens_kernel(pair, value_ref, out_ref, send_sems, recv_sems):
    core = lax.axis_index("c")
    me = place_of(*pair)
    one, two = pair
    half = value_ref.shape[0] // 2
    sender = Sender(send_sems, recv_sems)
    out_ref[me, core] = value_ref[...]
    meet([(two,), (one,), ("c",)])

    def send(place, axes, rows=slice(None)):
        mine = out_ref.at[place, core, rows]
        return sender.start(mine, mine, axes)

    near = send(me, (two,))
    wide = send(me, (one,))
    got = [send(me, ("c",))]
    near.wait_recv()
    far = [send(me ^ 1, (one,), slice(0, half))]
    got.append(send(me ^ 1, ("c",)))
    wide.wait_recv()
    far.append(send(me ^ 2, (two,), slice(half, 2 * half)))
    got.append(send(me ^ 2, ("c",)))
    for copy in far:
        copy.wait_recv()
    got.append(send(me ^ 3, ("c",)))
    for copy in got:
        copy.wait_recv()
    sender.finish()


def tokens_of_chips(value, pair, number):
    rows, cols = value.shape
    vmem = pl.BlockSpec(memory_space=pltpu.VMEM)
    out = pl.pallas_call(
        functools.partial(tokens_kernel, pair),
        out_shape=jax.ShapeDtypeStruct((4, 2, rows, cols), bf16),
        in_specs=[vmem],
        out_specs=vmem,
        scratch_shapes=[pltpu.SemaphoreType.DMA((8,)), pltpu.SemaphoreType.DMA((8,))],
        compiler_params=pltpu.CompilerParams(
            collective_id=number, has_side_effects=True, vmem_limit_bytes=24 << 20
        ),
        cost_estimate=pl.CostEstimate(flops=1, transcendentals=0, bytes_accessed=1),
    )(value)
    return out.reshape(8 * rows, cols)


def merge_kernel(which, parts_ref, out_ref):
    cols = out_ref.shape[1] // 4
    for quarter in range(4):
        out_ref[:, quarter * cols : (quarter + 1) * cols] = parts_ref[0, quarter].astype(f32)


def merge(parts, which):
    rows, cols = parts.shape[2:]
    return pl.pallas_call(
        functools.partial(merge_kernel, which),
        grid=(1,),
        out_shape=jax.ShapeDtypeStruct((rows, 4 * cols), f32),
        in_specs=[pl.BlockSpec((1, 4, rows, cols), lambda i: (which, 0, 0, 0))],
        out_specs=pl.BlockSpec((rows, 4 * cols), lambda i: (0, 0)),
        cost_estimate=pl.CostEstimate(
            flops=0, transcendentals=0, bytes_accessed=24 * rows * cols
        ),
    )(parts)


class Reduction:
    def __init__(self, sender, held, dims, order, buffers, out):
        self.sender, self.held, self.dims, self.order = sender, held, list(dims), list(order)
        self.buffers, self.out = list(buffers), out

    def half(self, at):
        return (slice(None),) * self.dims.index(self.order[0]) + (at,)

    def begin(self):
        axis = self.order[0]
        source = self.held.at[self.half(1 - lax.axis_index(axis))]
        self.copy = self.sender.start(source, self.buffers[0], (axis,))

    def end(self):
        self.copy.wait_recv()
        axis = self.order[0]
        own = self.held[self.half(lax.axis_index(axis))]
        total = own.astype(f32) + self.buffers[0][...].astype(f32)
        self.held = self.buffers.pop(0)
        self.dims.remove(axis)
        self.order.pop(0)
        if self.order:
            self.held[...] = total.astype(bf16)
            self.begin()
        else:
            self.out[...] = total

    def finish(self):
        while self.order:
            self.end()


def halves_of(rows):
    half = rows // 2 // 16 * 16
    return pl.ds(0, half), pl.ds(half, rows - half)


def last_kernel(
    fsdp,
    pair,
    peak_ref,
    small_ref,
    gains_ref,
    q_ref,
    kv_ref,
    out_ref,
    down_ref,
    gate_ref,
    up_ref,
    small_sum,
    gains_sum,
    q_sum,
    kv_sum,
    out_sum,
    ffn_out,
    peak_out,
    *scratch,
):
    scratch = list(scratch)
    stages = len(fsdp)
    sender = Sender(scratch.pop(), scratch.pop())

    def buffers(count):
        taken = scratch[:count]
        del scratch[:count]
        return taken

    down = list(reversed(fsdp))
    turned = [down[1], down[0]] + down[2:]
    with_core = fsdp + ["c"]
    small = Reduction(sender, small_ref, with_core, ["c"] + turned, buffers(stages + 1), small_sum)
    gains = Reduction(sender, gains_ref, with_core, ["c"] + down, buffers(stages + 1), gains_sum)
    q = Reduction(sender, q_ref, fsdp, down, buffers(stages), q_sum)
    kv = Reduction(sender, kv_ref, fsdp, turned, buffers(stages), kv_sum)
    upward = [down[-2]] + turned[:-2] + [down[-1]]
    outs = []
    for rows, order in zip(halves_of(out_sum.shape[0]), (turned, upward)):
        part = out_ref.at[(slice(None),) * stages + (rows,)]
        outs.append(Reduction(sender, part, fsdp, order, buffers(stages), out_sum.at[rows]))
    over = buffers(1)[0]
    peaks = buffers(stages)
    me = place_of(*pair)
    row = lax.axis_index(fsdp[0])
    meet([(axis,) for axis in with_core] + [pair])

    def send_columns(which, held):
        ffn_out[which, me] = held[me]
        return [
            sender.start(held.at[me ^ away], ffn_out.at[which, me], axes)
            for away, axes in ((1, (pair[1],)), (2, (pair[0],)), (3, pair))
        ]

    peak_out[...] = peak_ref[...]

    def send_peaks(stage):
        return sender.start(peak_out, peaks[stage], (fsdp[stage],))

    def next_peaks(stage, sent):
        sent.wait()
        sender.left.append(sent)
        peak_out[...] = jnp.maximum(peak_out[...], peaks[stage][...])
        return send_peaks(stage + 1) if stage < stages - 1 else None

    for part in (small, gains, q, outs[0], kv):
        part.begin()
    peak_sent = send_peaks(0)
    crossing = sender.start(up_ref.at[1 - row], over, (fsdp[0],))
    outs[1].begin()
    columns = send_columns(0, down_ref)
    small.end()
    gains.end()
    columns += send_columns(1, gate_ref)
    peak_sent = next_peaks(0, peak_sent)
    for part in (q, kv, outs[0]):
        part.end()
    crossing.wait_recv()
    over[...] = (up_ref[row].astype(f32) + over[...].astype(f32)).astype(bf16)
    columns += send_columns(2, over)
    for stage in range(1, stages):
        peak_sent = next_peaks(stage, peak_sent)
        for part in (outs[1], small, gains, q, kv, outs[0]):
            part.end()
    for reduction in (q, kv, outs[0], small, gains, outs[1]):
        reduction.finish()
    for copy in columns:
        copy.wait_recv()
    sender.finish()


def last_scatter(fsdp, pair, peak, small, gains, q, kv, out, down, gate, up):
    vmem = pl.BlockSpec(memory_space=pltpu.VMEM)
    stages = len(fsdp)

    def buffers(array, count, rows=None):
        lead = array.ndim - 2
        block = (rows or array.shape[-2], array.shape[-1])
        return [pltpu.VMEM((2,) * (lead - 1 - i) + block, bf16) for i in range(count)]

    scratch = (
        buffers(small, stages + 1)
        + buffers(gains, stages + 1)
        + buffers(q, stages)
        + buffers(kv, stages)
        + [buf for rows in halves_of(out.shape[-2]) for buf in buffers(out, stages, rows.size)]
        + [pltpu.VMEM(down.shape, bf16)]
        + [pltpu.VMEM(peak.shape, f32)] * stages
    )
    copies = 2 * (stages + 1) + 4 * stages + 1 + 9 + stages
    return pl.pallas_call(
        functools.partial(last_kernel, fsdp, pair),
        out_shape=tuple(jax.ShapeDtypeStruct(x.shape[-2:], f32) for x in (small, gains, q, kv, out))
        + (
            jax.ShapeDtypeStruct((3,) + down.shape, bf16),
            jax.ShapeDtypeStruct(peak.shape, f32),
        ),
        in_specs=[vmem] * 9,
        out_specs=(vmem,) * 7,
        scratch_shapes=scratch
        + [pltpu.SemaphoreType.DMA((copies,)), pltpu.SemaphoreType.DMA((copies,))],
        compiler_params=pltpu.CompilerParams(
            collective_id=2, has_side_effects=True, vmem_limit_bytes=60 << 20
        ),
    )(peak, small, gains, q, kv, out, down, gate, up)


def shards(
    fsdp,
    hidden_in,
    seq_ids,
    block_ids,
    clip_limit,
    cotangent,
    q_down,
    kv_down,
    q_up,
    kv_up,
    out_proj,
    gate_proj,
    up_proj,
    down_proj,
    in_gain,
    q_gain,
    kv_gain,
    post_gain,
):
    tokens_here, width = hidden_in.shape
    seq_row = seq_ids[0]
    block_row = block_ids[0]
    group = seq_row.shape[0]
    heads = q_up.shape[1] // (NOPE + ROPE)
    score_scale = 1.0 / math.sqrt(NOPE + ROPE)
    core = lax.axis_index("c")
    first_row = core * tokens_here
    wide, near = fsdp[1], fsdp[-1]
    pair = (wide, near)
    spread = [axis for axis in fsdp if axis not in pair]
    squares = [(fsdp[i], fsdp[i + 1]) for i in range(0, len(fsdp), 2)]
    at_wide, at_near = lax.axis_index(wide), lax.axis_index(near)
    chips = tuple(fsdp)
    count = 2 ** len(fsdp)

    small_rows = q_down.shape[0]
    q_rank = q_down.shape[1]
    small_cols = q_rank + kv_down.shape[1]

    def row(value):
        return jnp.pad(value, ((0, 0), (0, TILE - value.shape[1])))[:, None, :]

    def rows_of(*values):
        held = jnp.concatenate([row(value) for value in values], axis=1)
        return jnp.pad(held, ((0, 0), (0, 8 - len(values)), (0, 0)))

    small = jnp.concatenate([q_down, kv_down], axis=1)
    gains = rows_of(in_gain[None], post_gain[None], q_gain[None], kv_gain[None])[0]
    q_up_wide = jnp.pad(
        q_up.reshape(-1, heads, NOPE + ROPE), ((0, 0), (0, 0), (0, TILE - NOPE - ROPE))
    ).reshape(-1, heads * TILE)
    small_all, gains_all, q_up_all, kv_up_all, *pieces = first_gather(
        squares, pair, spread, small, gains, q_up_wide, kv_up, gate_proj, up_proj, down_proj
    )
    down_full = small_all.reshape(-1, small_cols)
    q_up_full = q_up_all.reshape(-1, heads * TILE)
    kv_up_full = kv_up_all.reshape(-1, kv_up.shape[1])
    devices = 2 * count

    def gain(at, size):
        return gains_all.reshape(devices, 8, TILE)[:, at, :size].reshape(-1).astype(f32)

    in_float = gain(0, in_gain.shape[0])
    post_float = gain(1, post_gain.shape[0])
    q_gain_float = gain(2, q_gain.shape[0])
    kv_gain_float = gain(3, kv_gain.shape[0])

    cot_float = cotangent.astype(f32)

    def over(pieces, axis, *ready):
        return [swap(after(piece, *ready), axis) for piece in pieces]

    def exchange(held, dims, axis):
        at, dim = lax.axis_index(axis), dims.index(axis)
        return swap(pick(held, 1 - at, dim), axis), pick(held, at, dim)

    def sum_of_chips(held):
        held = held.reshape(2, 2, tokens_here, width)
        return square_scatter(held, wide, near, 0).reshape(tokens_here, width)

    def core_both(value):
        return both(value, swap(value, "c"), "c", 0)

    def core_sum(value):
        def rows(at):
            return lax.dynamic_slice_in_dim(value, at * tokens_here, tokens_here)

        return rows(core) + swap(rows(1 - core), "c")

    x_float = hidden_in.astype(f32)
    x_normed = rms_scale(x_float, in_float).astype(bf16)
    pre = jnp.dot(x_normed, down_full, preferred_element_type=f32)
    q_pre = pre[:, :q_rank]
    c_lat_pre = pre[:, q_rank : q_rank + KVR]
    c_rot_pre = pre[:, q_rank + KVR :]
    own_cos, own_sin = angles(seq_row, first_row, tokens_here)
    q_latent = rms_scale(q_pre, q_gain_float).astype(bf16)
    kv_latent = rms_scale(c_lat_pre, kv_gain_float).astype(bf16)
    key_rot = rotate(c_rot_pre, own_cos, own_sin).astype(bf16)
    key_rot = jnp.pad(key_rot, ((0, 0), (NOPE, TILE - NOPE - ROPE)))
    latents = core_both(jnp.concatenate([q_latent, kv_latent, key_rot], axis=1))
    q_lat_all = latents[:, :q_rank]
    kv_lat_all = latents[:, q_rank : q_rank + KVR]
    key_rot_all = latents[:, q_rank + KVR :]
    all_cos, all_sin = angles(seq_row, 0, group)
    q_full = jnp.dot(q_lat_all, q_up_full, preferred_element_type=f32)
    kv_full = jnp.dot(kv_lat_all, kv_up_full, preferred_element_type=f32).astype(bf16)
    allowed = (seq_row[None, :] == seq_row[:, None]) & (block_row[:, None] <= block_row[None, :])
    bias = jnp.where(allowed, 0.0, -1e30).astype(f32)
    axes = list(spread)
    gate_held, gate_over, gate_last, up_held, down_held = pieces
    gate_pieces = [gate_held, gate_over, gate_last, swap(gate_over, axes[1])]
    for axis in axes[2:]:
        gate_pieces += over(gate_pieces, axis)
    up_pieces = [swap(up_held, axes[0]), swap(up_held, axes[1])]
    attn, queries, log_total, local_peak = attend(
        q_full, kv_full, key_rot_all, tables(all_cos, all_sin), bias, score_scale
    )
    d_ffn = (resid_scale * cot_float).astype(bf16)
    out_full, d_ffn_all, down_over = second_gather(
        squares, pair, axes[0], after(out_proj, attn), d_ffn, down_held
    )
    attn, out_full, down_over, *early = lax.optimization_barrier(
        (attn, out_full, down_over, *up_pieces, *gate_pieces)
    )
    up_pieces, gate_pieces = early[:2], early[2:]
    branch = core_sum(contract(attn, out_full, 1, 1))
    mid = x_float + resid_scale * branch
    mid_normed = rms_scale(mid, post_float).astype(bf16)
    gate_full = lay(gate_pieces, fsdp, pair, spread)
    mid_all = tokens_of_chips(after(mid_normed, gate_full), pair, 1)
    up_pieces = [up_held, *up_pieces, swap(after(up_pieces[0], attn), axes[1])]
    down_last = swap(after(down_held, attn), axes[1])
    mid_all, down_last, *up_pieces = lax.optimization_barrier((mid_all, down_last, *up_pieces))
    down_pieces = [down_held, down_over, down_last, swap(after(down_over, mid_all), axes[1])]
    for axis in axes[2:]:
        up_pieces += over(up_pieces, axis)
        down_pieces += over(down_pieces, axis)
    up_full = lay(up_pieces, fsdp, pair, spread)
    gate = jnp.dot(mid_all, gate_full, preferred_element_type=f32)
    up_value = jnp.dot(mid_all, up_full, preferred_element_type=f32)
    down_proj_full = lay(down_pieces, fsdp, pair, spread)
    sigmoid = jax.nn.sigmoid(gate)
    silu_value = gate * sigmoid
    act = (silu_value * up_value).astype(bf16)

    d_act = jnp.dot(d_ffn_all, down_proj_full, preferred_element_type=f32)
    d_gate = (d_act * up_value * (sigmoid * (1.0 + gate * (1.0 - sigmoid)))).astype(bf16)
    d_up = (d_act * silu_value).astype(bf16)
    dims = list(fsdp)
    first, last = spread[0], spread[-1]

    def added(parts):
        return (parts[0].astype(f32) + parts[1].astype(f32)).astype(bf16)

    def inner(held):
        left = [axis for axis in dims if axis != last]
        for axis in reversed(spread[1:-1]):
            held = added(exchange(held, left, axis))
            left.remove(axis)
        return held

    def begin(left, right, *ready):
        keep, send = grad_halves(left, right, width // count, last)
        shape = [2] * (len(fsdp) - 1) + [width // count, -1]
        return swap(after(send, *ready), last).reshape(shape), keep.reshape(shape), keep

    def cross(held):
        return exchange(held, [first, *pair], first)

    *down_parts, down_grad = begin(d_ffn_all, act)
    d_gate_late, _ = lax.optimization_barrier((d_gate, down_grad))
    gate_keep, gate_send = grad_halves(mid_all, d_gate_late, width // count, last)
    d_up_late, d_gate_late, _ = lax.optimization_barrier((d_up, d_gate, gate_keep))
    d_mid_held = core_features(
        tokens_here, 3, (d_gate_late, gate_full), (d_up_late, up_full)
    )
    d_mid_held, *down_parts = lax.optimization_barrier((d_mid_held, *down_parts))
    d_mid_normed = sum_of_chips(d_mid_held)
    mid_late, gate_send, _ = lax.optimization_barrier((mid_all, gate_send, d_mid_held))
    shape = [2] * (len(fsdp) - 1) + [width // count, -1]
    gate_parts = (swap(gate_send, last).reshape(shape), gate_keep.reshape(shape))
    down_parts = cross(inner(added(down_parts)))
    *up_parts, up_grad = begin(mid_late, d_up, gate_parts[0])
    ffn_part = features((after(act, up_grad), down_proj_full))
    post_pull = jax.vjp(rms_scale, mid, post_float)[1]
    d_mid_normed, *early = lax.optimization_barrier(
        (d_mid_normed, *down_parts, *gate_parts, ffn_part)
    )
    down_parts, gate_parts, ffn_part = early[:2], early[2:4], early[4]
    d_mid_norm, post_grad = post_pull(d_mid_normed)
    ffn = lax.psum_scatter(
        after(ffn_part, d_mid_norm), (wide, near, "c"), scatter_dimension=0, tiled=True
    )
    layer_out = (mid + resid_scale * ffn.astype(f32)).astype(bf16)
    d_mid = cot_float + d_mid_norm
    d_branch = (resid_scale * d_mid).astype(bf16)
    d_branch_all = core_both(d_branch)
    d_attn = jnp.dot(d_branch_all, out_full, preferred_element_type=f32).astype(bf16)
    gate_parts = cross(inner(added(gate_parts)))
    d_q, d_kv, d_rot_part = attend_back(
        queries,
        kv_full,
        d_attn,
        log_total,
        key_rot_all,
        tables(all_cos, -all_sin),
        bias,
        score_scale,
    )
    q_up_grad = heads_grad(q_lat_all, d_q)
    d_q, d_kv, q_up_grad, *early = lax.optimization_barrier(
        (d_q, d_kv, q_up_grad, *gate_parts, *up_parts)
    )
    gate_parts, up_parts = early[:2], early[2:]
    out_grad = rows_first(contract(after(d_branch_all, d_q), attn, 0, 0).astype(bf16))
    kv_up_grad = rows_first(contract(kv_lat_all, d_kv, 0, 0).astype(bf16))
    d_q_lat_part = contract(d_q, q_up_full, 1, 1)
    d_kv_lat_part = contract(d_kv, kv_up_full, 1, 1)
    d_latents = core_sum(jnp.concatenate([d_q_lat_part, d_kv_lat_part, d_rot_part], axis=1))
    q_pull = jax.vjp(rms_scale, q_pre, q_gain_float)[1]
    d_q_pre, q_gain_grad = q_pull(d_latents[:, :q_rank])
    kv_pull = jax.vjp(rms_scale, c_lat_pre, kv_gain_float)[1]
    d_c_lat, kv_gain_grad = kv_pull(d_latents[:, q_rank : q_rank + KVR])
    d_key_rot = d_latents[:, q_rank + KVR + NOPE : q_rank + KVR + NOPE + ROPE]
    d_pre = jnp.concatenate(
        [d_q_pre, d_c_lat, rotate(d_key_rot, own_cos, -own_sin)], axis=-1
    ).astype(bf16)
    down_grads = rows_first(contract(x_normed, d_pre, 0, 0).astype(bf16))
    d_x_normed = contract(d_pre, down_full, 1, 1)
    in_pull = jax.vjp(rms_scale, x_float, in_float)[1]
    d_x_norm, in_grad = in_pull(d_x_normed)
    input_grad = d_mid + d_x_norm

    rows_here = width // count
    ffn_held = [
        added(down_parts).reshape(4, rows_here, -1),
        added(gate_parts).reshape(4, rows_here, -1),
        inner(added(up_parts)).reshape(2, 4, rows_here, -1),
    ]
    gain_grads = rows_of(
        *(grad.reshape(devices, -1) for grad in (in_grad, post_grad, q_gain_grad, kv_gain_grad))
    ).astype(bf16)

    def blocks(grad, lead):
        return grad.reshape([2] * lead + [grad.shape[0] // 2**lead, -1])

    small_out, gain_out, q_up_out, kv_up_out, out_out, ffn_cols, peak_all = last_scatter(
        fsdp,
        pair,
        local_peak,
        blocks(down_grads, len(fsdp) + 1),
        gain_grads.reshape([2] * (len(fsdp) + 1) + [8, TILE]),
        blocks(q_up_grad, len(fsdp)),
        blocks(kv_up_grad, len(fsdp)),
        blocks(out_grad, len(fsdp)),
        *ffn_held,
    )
    down_out, gate_out, up_out = (merge(ffn_cols, which) for which in range(3))
    peaks = peak_all[0, :heads]
    limit = clip_limit[0]
    factors = limit / jnp.maximum(peaks, limit)
    root = jnp.sqrt(factors)
    q_cols = jnp.concatenate(
        [
            jnp.broadcast_to(root[:, None], (heads, NOPE)),
            jnp.broadcast_to(factors[:, None], (heads, ROPE)),
        ],
        axis=1,
    ).reshape(heads * (NOPE + ROPE))
    kv_cols = jnp.concatenate(
        [jnp.broadcast_to(root[:, None], (heads, NOPE)), jnp.ones((heads, VD), f32)], axis=1
    ).reshape(heads * (NOPE + VD))
    q_clipped = (q_up.astype(f32) * q_cols[None, :]).astype(bf16)
    kv_clipped = (kv_up.astype(f32) * kv_cols[None, :]).astype(bf16)
    return (
        layer_out,
        input_grad,
        small_out[:, :q_rank],
        small_out[:, q_rank:],
        q_up_out,
        kv_up_out,
        out_out,
        gate_out,
        up_out,
        down_out,
        gain_out[0, : in_gain.shape[0]],
        gain_out[2, : q_gain.shape[0]],
        gain_out[3, : kv_gain.shape[0]],
        gain_out[1, : post_gain.shape[0]],
        q_clipped,
        kv_clipped,
        peaks,
        factors,
    )


def solution(mesh):
    bits = mesh.shape["fsdp"].bit_length() - 1
    fsdp = [f"f{i}" for i in range(bits)]
    fine = Mesh(mesh.devices.reshape((2,) * (bits + 1)), tuple(fsdp) + ("c",))
    split = tuple(fsdp)
    whole = split + ("c",)
    return jax.shard_map(
        functools.partial(shards, fsdp),
        mesh=fine,
        in_specs=(
            P(whole, None),
            P(split, None),
            P(split, None),
            P(),
            P(whole, None),
            P(whole, None),
            P(whole, None),
            P(split, "c"),
            P(split, "c"),
            P(split, "c"),
            P(split, "c"),
            P(split, "c"),
            P(split, "c"),
            P(whole),
            P(whole),
            P(whole),
            P(whole),
        ),
        out_specs=(
            P(whole, None),
            P(whole, None),
            P(whole, None),
            P(whole, None),
            P(split, "c"),
            P(split, "c"),
            P(split, "c"),
            P(split, "c"),
            P(split, "c"),
            P(split, "c"),
            P(whole),
            P(whole),
            P(whole),
            P(whole),
            P(split, "c"),
            P(split, "c"),
            P("c"),
            P("c"),
        ),
        check_vma=False,
    )
```

```python
import functools
import math

import jax
import jax.numpy as jnp
from jax import lax
from jax.experimental import pallas as pl
from jax.experimental.pallas import tpu as pltpu
from jax.experimental.layout import Layout, with_layout_constraint
from jax.sharding import Mesh
from jax.sharding import PartitionSpec as P

NOPE = 64
ROPE = 32
VD = 64
KVR = 256
TILE = 128


eps = 1e-05
resid_scale = 1.4 / math.sqrt(62.0)
rope_base = 10000.0
SWAP = [(0, 1), (1, 0)]
f32 = jnp.float32
bf16 = jnp.bfloat16


def rms_scale(value, gain):
    return value * lax.rsqrt(jnp.mean(value * value, axis=-1, keepdims=True) + eps) * gain


def rotate(value, cosine, sine):
    half = value.shape[-1] // 2
    first = value[..., :half]
    second = value[..., half:]
    return jnp.concatenate(
        [first * cosine - second * sine, second * cosine + first * sine], axis=-1
    )


def angles(seq_row, start, count):
    own_ids = lax.dynamic_slice_in_dim(seq_row, start, count)
    earlier = jnp.sum((seq_row[None, :] < own_ids[:, None]).astype(jnp.int32), axis=1)
    place = (start + jnp.arange(count, dtype=jnp.int32) - earlier).astype(f32)
    freq = jnp.power(rope_base, -jnp.arange(ROPE // 2, dtype=f32) * (2.0 / ROPE))
    turn = place[:, None] * freq[None, :]
    return (jnp.cos(turn), jnp.sin(turn))


def contract(left, right, left_dim, right_dim):
    return lax.dot_general(
        left, right, (((left_dim,), (right_dim,)), ((), ())), preferred_element_type=f32
    )


def turn(value, plain, first, second):
    return (
        value * plain
        + pltpu.roll(value, TILE - ROPE // 2, 1) * first
        + pltpu.roll(value, ROPE // 2, 1) * second
    )


def tables(cosine, sine):
    rows = cosine.shape[0]
    half = ROPE // 2

    def zeros(count):
        return jnp.zeros((rows, count), f32)

    plain = jnp.concatenate([jnp.ones((rows, NOPE), f32), cosine, cosine, zeros(TILE - NOPE - ROPE)], axis=1)
    first = jnp.concatenate([zeros(NOPE), -sine, zeros(TILE - NOPE - half)], axis=1)
    second = jnp.concatenate([zeros(NOPE + half), sine, zeros(TILE - NOPE - ROPE)], axis=1)
    return plain, first, second


def attend_kernel(
    scale,
    q_ref,
    kv_ref,
    rot_ref,
    plain_ref,
    first_ref,
    second_ref,
    bias_ref,
    mixed_ref,
    query_ref,
    total_ref,
    peak_ref,
):
    step = pl.program_id(0)
    lane = lax.broadcasted_iota(jnp.int32, (q_ref.shape[0], TILE), 1)
    spot = lax.broadcasted_iota(jnp.int32, peak_ref.shape, 1)

    @pl.when(step == 0)
    def _():
        peak_ref[...] = jnp.zeros_like(peak_ref)

    outs = []
    for one in range(2):
        cols = slice(one * TILE, (one + 1) * TILE)
        query = turn(q_ref[:, cols], plain_ref[...], first_ref[...], second_ref[...]).astype(bf16)
        query_ref[:, cols] = query
        kv = kv_ref[:, cols]
        keys = jnp.where(lane < NOPE, kv, rot_ref[...])
        masked = contract(keys, query, 1, 1) * scale + bias_ref[...]
        top = jnp.max(masked, axis=0, keepdims=True)
        weights = jnp.exp(masked - top)
        total = jnp.sum(weights, axis=0, keepdims=True)
        chance = (weights * (1.0 / total)).astype(bf16)
        outs.append(contract(chance, kv, 0, 0))
        total_ref[0, one : one + 1, :] = top + jnp.log(total)
        peak_ref[...] = jnp.where(spot == step * 2 + one, jnp.max(top), peak_ref[...])
    mixed_ref[...] = jnp.where(lane < VD, pltpu.roll(outs[0], VD, 1), outs[1]).astype(bf16)


def attend(q, kv, rot, turns, bias, scale):
    group, cols = q.shape
    heads = cols // TILE
    whole = pl.BlockSpec((group, TILE), lambda i: (0, 0))
    two = pl.BlockSpec((group, 2 * TILE), lambda i: (0, i))
    return pl.pallas_call(
        functools.partial(attend_kernel, scale),
        grid=(heads // 2,),
        out_shape=(
            jax.ShapeDtypeStruct((group, heads * VD), bf16),
            jax.ShapeDtypeStruct((group, cols), bf16),
            jax.ShapeDtypeStruct((heads // 2, 2, group), f32),
            jax.ShapeDtypeStruct((8, TILE), f32),
        ),
        in_specs=[two, two, whole, whole, whole, whole, pl.BlockSpec((group, group), lambda i: (0, 0))],
        out_specs=(
            pl.BlockSpec((group, TILE), lambda i: (0, i)),
            two,
            pl.BlockSpec((1, 2, group), lambda i: (i, 0, 0)),
            pl.BlockSpec((8, TILE), lambda i: (0, 0)),
        ),
        compiler_params=pltpu.CompilerParams(
            dimension_semantics=("arbitrary",), vmem_limit_bytes=40 << 20
        ),
        cost_estimate=pl.CostEstimate(flops=1, transcendentals=0, bytes_accessed=1),
    )(q, kv, rot, *turns, bias)


def attend_back_kernel(
    scale,
    query_ref,
    kv_ref,
    d_mixed_ref,
    total_ref,
    rot_ref,
    plain_ref,
    first_ref,
    second_ref,
    bias_ref,
    d_q_ref,
    d_kv_ref,
    d_rot_ref,
):
    step = pl.program_id(0)
    lane = lax.broadcasted_iota(jnp.int32, (query_ref.shape[0], TILE), 1)

    @pl.when(step == 0)
    def _():
        d_rot_ref[...] = jnp.zeros_like(d_rot_ref)

    pair = d_mixed_ref[...].astype(f32)
    for one in range(2):
        cols = slice(one * TILE, (one + 1) * TILE)
        query = query_ref[:, cols]
        kv = kv_ref[:, cols]
        keys = jnp.where(lane < NOPE, kv, rot_ref[...])
        own = pair if one else pltpu.roll(pair, VD, 1)
        d_mixed = jnp.where(lane < VD, 0.0, own).astype(bf16)
        masked = contract(keys, query, 1, 1) * scale + bias_ref[...]
        chance = jnp.exp(masked - total_ref[0, one : one + 1, :])
        d_values = contract(chance.astype(bf16), d_mixed, 1, 0)
        d_chance = contract(kv, d_mixed, 1, 1)
        inner = jnp.sum(chance * d_chance, axis=0, keepdims=True)
        d_raw = (chance * (d_chance - inner) * scale).astype(bf16)
        d_keys = contract(d_raw, query, 1, 0)
        d_query = contract(d_raw, keys, 0, 0)
        d_q_ref[:, cols] = turn(
            d_query, plain_ref[...], first_ref[...], second_ref[...]
        ).astype(bf16)
        d_kv_ref[:, cols] = jnp.where(lane < NOPE, d_keys, d_values).astype(bf16)
        d_rot_ref[...] += d_keys


def attend_back(query, kv, d_mixed, total, rot, turns, bias, scale):
    group, cols = query.shape
    heads = cols // TILE
    whole = pl.BlockSpec((group, TILE), lambda i: (0, 0))
    two = pl.BlockSpec((group, 2 * TILE), lambda i: (0, i))
    return pl.pallas_call(
        functools.partial(attend_back_kernel, scale),
        grid=(heads // 2,),
        out_shape=(
            jax.ShapeDtypeStruct((group, cols), bf16),
            jax.ShapeDtypeStruct((group, cols), bf16),
            jax.ShapeDtypeStruct((group, TILE), f32),
        ),
        in_specs=[
            two,
            two,
            pl.BlockSpec((group, TILE), lambda i: (0, i)),
            pl.BlockSpec((1, 2, group), lambda i: (i, 0, 0)),
            whole,
            whole,
            whole,
            whole,
            pl.BlockSpec((group, group), lambda i: (0, 0)),
        ],
        out_specs=(two, two, whole),
        compiler_params=pltpu.CompilerParams(
            dimension_semantics=("arbitrary",), vmem_limit_bytes=40 << 20
        ),
        cost_estimate=pl.CostEstimate(flops=1, transcendentals=0, bytes_accessed=1),
    )(query, kv, d_mixed, total, rot, *turns, bias)


def swap(value, axis):
    return lax.ppermute(value, axis, SWAP)


def far(value, pair):
    return lax.ppermute(value, pair, [(i, 3 - i) for i in range(4)])


def after(value, *others):
    return lax.optimization_barrier((value,) + others)[0]


def pick(value, at, dim):
    return lax.dynamic_index_in_dim(value, at, dim, keepdims=True)


def both(own, other, axis, dim):
    here = lax.axis_index(axis) == 0
    return jnp.concatenate([jnp.where(here, own, other), jnp.where(here, other, own)], axis=dim)


def plain_grad_kernel(left_ref, right_ref, out_ref):
    out_ref[...] = contract(left_ref[...], right_ref[...], 0, 0).astype(bf16)


def plain_grad(left, right):
    rows, width = left.shape
    cols = right.shape[1]
    tile = 512
    return pl.pallas_call(
        plain_grad_kernel,
        grid=(width // tile,),
        out_shape=jax.ShapeDtypeStruct((width, cols), bf16),
        in_specs=[
            pl.BlockSpec((rows, tile), lambda i: (0, i)),
            pl.BlockSpec((rows, cols), lambda i: (0, 0)),
        ],
        out_specs=pl.BlockSpec((tile, cols), lambda i: (i, 0)),
        compiler_params=pltpu.CompilerParams(vmem_limit_bytes=32 << 20),
        cost_estimate=pl.CostEstimate(flops=1, transcendentals=0, bytes_accessed=1),
    )(left, right)


def heads_grad_kernel(latent_ref, d_ref, out_ref):
    total = contract(latent_ref[...], d_ref[...], 0, 0)
    parts = [total[:, i * TILE : i * TILE + NOPE + ROPE] for i in range(4)]
    out_ref[...] = jnp.concatenate(parts, axis=1).astype(bf16)


def heads_grad(latent, d_heads):
    group, rank = latent.shape
    packs = d_heads.shape[1] // (4 * TILE)
    cols = 4 * (NOPE + ROPE)
    return pl.pallas_call(
        heads_grad_kernel,
        grid=(packs,),
        out_shape=jax.ShapeDtypeStruct((rank, packs * cols), bf16),
        in_specs=[
            pl.BlockSpec((group, rank), lambda i: (0, 0)),
            pl.BlockSpec((group, 4 * TILE), lambda i: (0, i)),
        ],
        out_specs=pl.BlockSpec((rank, cols), lambda i: (0, i)),
        compiler_params=pltpu.CompilerParams(vmem_limit_bytes=32 << 20),
        cost_estimate=pl.CostEstimate(flops=1, transcendentals=0, bytes_accessed=1),
    )(latent, d_heads)


def features_kernel(*refs):
    out_ref = refs[-1]
    total = contract(refs[0][...], refs[1][...], 1, 1)
    for i in range(2, len(refs) - 1, 2):
        total += contract(refs[i][...], refs[i + 1][...], 1, 1)
    out_ref[...] = total.astype(bf16)


def features(*pairs):
    rows, cols = pairs[0][0].shape
    width = pairs[0][1].shape[0]
    tile = min(rows, 512)
    return pl.pallas_call(
        features_kernel,
        grid=(rows // tile,),
        out_shape=jax.ShapeDtypeStruct((rows, width), bf16),
        in_specs=[
            pl.BlockSpec((tile, cols), lambda i: (i, 0)),
            pl.BlockSpec((width, cols), lambda i: (0, 0)),
        ]
        * len(pairs),
        out_specs=pl.BlockSpec((tile, width), lambda i: (i, 0)),
        compiler_params=pltpu.CompilerParams(vmem_limit_bytes=56 << 20),
        cost_estimate=pl.CostEstimate(flops=1, transcendentals=0, bytes_accessed=1),
    )(*(array for pair in pairs for array in pair))


def core_features_kernel(*refs):
    *operands, out_ref, total, sent, got, send_sems, recv_sems = refs
    step = pl.program_id(0)
    core = lax.axis_index("c")
    half = total.shape[1]

    @pl.when(step == 0)
    def _():
        meet([("c",)])

    def copy(at):
        return pltpu.make_async_remote_copy(
            src_ref=sent.at[at],
            dst_ref=got.at[at],
            send_sem=send_sems.at[at],
            recv_sem=recv_sems.at[at],
            device_id=other_of(("c",)),
            device_id_type=pl.DeviceIdType.MESH,
        )

    value = contract(operands[0][...], operands[1][...], 1, 1)
    for i in range(2, len(operands), 2):
        value += contract(operands[i][...], operands[i + 1][...], 1, 1)
    total[0] = value[:half].astype(bf16)
    total[1] = value[half:].astype(bf16)
    sent[step] = total[1 - core]
    copy(step).start()
    out_ref[step] = total[core]

    @pl.when(step == pl.num_programs(0) - 1)
    def _():
        for at in range(out_ref.shape[0]):
            copy(at).wait()
            out_ref[at] = (out_ref[at].astype(f32) + got[at].astype(f32)).astype(bf16)


def core_features(rows, number, *pairs):
    cols = pairs[0][0].shape[1]
    width = pairs[0][1].shape[0]
    block = (4, rows, width)
    return pl.pallas_call(
        core_features_kernel,
        grid=(4,),
        out_shape=jax.ShapeDtypeStruct(block, bf16),
        in_specs=[
            pl.BlockSpec((2 * rows, cols), lambda i: (i, 0)),
            pl.BlockSpec((width, cols), lambda i: (0, 0), pipeline_mode=pl.Buffered(1)),
        ]
        * len(pairs),
        out_specs=pl.BlockSpec(block, lambda i: (0, 0, 0)),
        scratch_shapes=[
            pltpu.VMEM((2, rows, width), bf16),
            pltpu.VMEM(block, bf16),
            pltpu.VMEM(block, bf16),
            pltpu.SemaphoreType.DMA((4,)),
            pltpu.SemaphoreType.DMA((4,)),
        ],
        compiler_params=pltpu.CompilerParams(
            dimension_semantics=("arbitrary",),
            collective_id=number,
            has_side_effects=True,
            vmem_limit_bytes=58 << 20,
        ),
        cost_estimate=pl.CostEstimate(flops=1, transcendentals=0, bytes_accessed=1),
    )(*(array for pair in pairs for array in pair))


def grad_kernel(axis, left_ref, right_ref, keep_ref, send_ref, total):
    half = total.shape[1]
    value = contract(left_ref[...], right_ref[...], 0, 0).astype(bf16)
    total[0] = value[:half]
    total[1] = value[half:]
    at = lax.axis_index(axis)
    keep_ref[0] = total[at]
    send_ref[0] = total[1 - at]


def grad_halves(left, right, rows, axis):
    tokens, width = left.shape
    cols = right.shape[1]
    tile = 4 * rows
    if tile % TILE:
        held = rows_first(contract(left, right, 0, 0).astype(bf16)).reshape(-1, 2, 2 * rows, cols)
        at = lax.axis_index(axis)
        return tuple(pick(held, i, 1)[:, 0] for i in (at, 1 - at))
    out = jax.ShapeDtypeStruct((width // tile, 2 * rows, cols), bf16)
    return pl.pallas_call(
        functools.partial(grad_kernel, axis),
        grid=(width // tile,),
        out_shape=(out, out),
        in_specs=[
            pl.BlockSpec((tokens, tile), lambda i: (0, i)),
            pl.BlockSpec((tokens, cols), lambda i: (0, 0)),
        ],
        out_specs=(pl.BlockSpec((1, 2 * rows, cols), lambda i: (i, 0, 0)),) * 2,
        scratch_shapes=[pltpu.VMEM((2, 2 * rows, cols), bf16)],
        compiler_params=pltpu.CompilerParams(vmem_limit_bytes=56 << 20),
        cost_estimate=pl.CostEstimate(flops=1, transcendentals=0, bytes_accessed=1),
    )(left, right)


def rows_first(value):
    return with_layout_constraint(value, Layout(major_to_minor=(0, 1)))


def square_scatter(held, first, second, dim):
    here, there = lax.axis_index(first), lax.axis_index(second)

    def part(w, n):
        return pick(pick(held, w, dim), n, dim + 1)

    near = swap(part(here, 1 - there).astype(bf16), second)
    wide = swap(part(1 - here, there).astype(bf16), first)
    corner = far(part(1 - here, 1 - there).astype(bf16), (first, second))
    own = part(here, there).astype(f32)
    return own + near.astype(f32) + wide.astype(f32) + corner.astype(f32)


def place_of(first, second):
    return lax.axis_index(first) * 2 + lax.axis_index(second)


def other_of(axes):
    return {axis: 1 - lax.axis_index(axis) for axis in axes}


def meet(partners):
    barrier = pltpu.get_barrier_semaphore()
    for axes in partners:
        pl.semaphore_signal(
            barrier, inc=1, device_id=other_of(axes), device_id_type=pl.DeviceIdType.MESH
        )
    pl.semaphore_wait(barrier, len(partners))


class Sender:
    def __init__(self, send_sems, recv_sems):
        self.send_sems, self.recv_sems, self.all, self.left = send_sems, recv_sems, [], []

    def start(self, source, target, axes):
        copy = pltpu.make_async_remote_copy(
            src_ref=source,
            dst_ref=target,
            send_sem=self.send_sems.at[len(self.all)],
            recv_sem=self.recv_sems.at[len(self.all)],
            device_id=other_of(axes),
            device_id_type=pl.DeviceIdType.MESH,
        )
        copy.start()
        self.all.append(copy)
        return copy

    def finish(self):
        for copy in self.all:
            if all(copy is not other for other in self.left):
                copy.wait_send()


def first_kernel(
    squares,
    pair,
    spread,
    small_ref,
    gains_ref,
    q_ref,
    kv_ref,
    gate_ref,
    up_ref,
    down_ref,
    small_out,
    gains_out,
    q_out,
    kv_out,
    gate_out,
    gate_over,
    gate_last,
    up_out,
    down_out,
    staged,
    send_sems,
    recv_sems,
):
    core = lax.axis_index("c")
    places = [place_of(*square) for square in squares]
    me = place_of(*pair)
    sender = Sender(send_sems, recv_sems)
    cols = staged.shape[3]

    small_out[(*places, core)] = small_ref[...]
    gains_out[(*places, core)] = gains_ref[...]
    q_out[tuple(places)] = q_ref[...]
    kv_out[tuple(places)] = kv_ref[...]
    partners = [axes for one, two in squares for axes in ((two,), (one,), (one, two))]
    meet(partners + [pair, ("c",)])

    def blocks(ref, stage, place, tail, lead=()):
        index = lead + (slice(None),) * (stage - len(lead)) + (place,) + tuple(places[stage + 1 :])
        return ref.at[index + tail]

    early = [(small_out, (core,)), (gains_out, (core,))]
    later = [(q_out, ()), (kv_out, ())]

    def send_first(ref, tail):
        mine = blocks(ref, 0, places[0], tail)
        return [sender.start(mine, mine, axes) for axes in partners[:3]]

    def send_square(ref, tail, stage):
        one, two = squares[stage]
        mine = blocks(ref, stage, places[stage], tail)
        return [sender.start(mine, mine, (two,)), sender.start(mine, mine, (one,))]

    def pass_on(ref, tail, stage, copies):
        one, two = squares[stage]
        copies[0].wait_recv()
        half = blocks(ref, stage, places[stage] ^ 1, tail, (slice(0, 2),))
        first = sender.start(half, half, (one,))
        copies[1].wait_recv()
        half = blocks(ref, stage, places[stage] ^ 2, tail, (slice(2, 4),))
        return [first, sender.start(half, half, (two,))]

    def wait(copies):
        for copy in copies:
            copy.wait_recv()

    targets = (gate_out, up_out, down_out)

    def send_columns(away, axes):
        return [
            sender.start(staged.at[which, me ^ away], target.at[me], axes)
            for which, target in enumerate(targets)
        ]

    first = [send_first(*item) for item in early]
    for which, weight_ref in enumerate((gate_ref, up_ref, down_ref)):
        for quarter in range(4):
            staged[which, quarter] = weight_ref[:, quarter * cols : (quarter + 1) * cols]
    columns = [send_columns(1, (pair[1],))]
    for which, target in enumerate(targets):
        target[me] = staged[which, me]
    for copies in first:
        wait(copies)
    sent = [send_square(*item, 1) for item in early]
    first_later = [send_first(*item) for item in later]
    columns.append(send_columns(2, (pair[0],)))
    for stage in range(1, len(squares)):
        if stage > 1:
            sent = [send_square(*item, stage) for item in early]
        passed = [pass_on(*item, stage, copies) for item, copies in zip(early, sent)]
        if stage == 1:
            for copies in first_later:
                wait(copies)
            sent_later = [send_square(*item, 1) for item in later]
            columns.append(send_columns(3, pair))
        for copies in passed:
            wait(copies)
    mine = (slice(None),) * len(squares) + (core,)
    core_sent = [sender.start(ref.at[mine], ref.at[mine], ("c",)) for ref, _ in early]
    for copies in columns:
        copies[0].wait_recv()
    over = [
        sender.start(gate_out, gate_over, (spread[0],)),
        sender.start(gate_out, gate_last, (spread[1],)),
    ]
    for stage in range(1, len(squares)):
        if stage > 1:
            sent_later = [send_square(*item, stage) for item in later]
        passed = [pass_on(*item, stage, copies) for item, copies in zip(later, sent_later)]
        for copies in passed:
            wait(copies)
    wait(core_sent)
    for copies in columns:
        wait(copies[1:])
    wait(over)
    sender.finish()


def first_gather(squares, pair, spread, small, gains, q_up, kv_up, gate, up, down):
    vmem = pl.BlockSpec(memory_space=pltpu.VMEM)
    rows, cols = gate.shape
    lead = (4,) * len(squares)
    copies = 12 + 16 * (len(squares) - 1) + 2 + 9 + 2
    return pl.pallas_call(
        functools.partial(first_kernel, squares, pair, spread),
        out_shape=(
            jax.ShapeDtypeStruct(lead + (2,) + small.shape, bf16),
            jax.ShapeDtypeStruct(lead + (2,) + gains.shape, bf16),
            jax.ShapeDtypeStruct(lead + q_up.shape, bf16),
            jax.ShapeDtypeStruct(lead + kv_up.shape, bf16),
        )
        + (jax.ShapeDtypeStruct((4, rows, cols // 4), bf16),) * 5,
        in_specs=[vmem] * 7,
        out_specs=(vmem,) * 9,
        scratch_shapes=[
            pltpu.VMEM((3, 4, rows, cols // 4), bf16),
            pltpu.SemaphoreType.DMA((copies,)),
            pltpu.SemaphoreType.DMA((copies,)),
        ],
        compiler_params=pltpu.CompilerParams(
            collective_id=0, has_side_effects=True, vmem_limit_bytes=48 << 20
        ),
    )(small, gains, q_up, kv_up, gate, up, down)


def second_kernel(
    squares,
    pair,
    over,
    rows_ref,
    value_ref,
    piece_ref,
    rows_out,
    tokens_out,
    piece_out,
    send_sems,
    recv_sems,
):
    core = lax.axis_index("c")
    places = [place_of(*square) for square in squares]
    me = place_of(*pair)
    one, two = pair
    half = value_ref.shape[0] // 2
    sender = Sender(send_sems, recv_sems)
    rows_out[tuple(places)] = rows_ref[...]
    tokens_out[me, core] = value_ref[...]
    partners = [axes for one_, two_ in squares for axes in ((two_,), (one_,), (one_, two_))]
    meet(partners + [("c",)])

    def blocks(stage, place, lead=()):
        index = lead + (slice(None),) * (stage - len(lead)) + (place,) + tuple(places[stage + 1 :])
        return rows_out.at[index]

    def send_rows(place, axes, rows=slice(None)):
        mine = tokens_out.at[place, core, rows]
        return sender.start(mine, mine, axes)

    mine = blocks(0, places[0])
    first = [sender.start(mine, mine, axes) for axes in partners[:3]]
    near = send_rows(me, (two,))
    wide = send_rows(me, (one,))
    got = [send_rows(me, ("c",))]
    for copy in first:
        copy.wait_recv()
    crossing = sender.start(piece_ref, piece_out, (over,))
    for stage in range(1, len(squares)):
        up, across = squares[stage]
        mine = blocks(stage, places[stage])
        beside = sender.start(mine, mine, (across,))
        above = sender.start(mine, mine, (up,))
        if stage == 1:
            near.wait_recv()
            corner = [send_rows(me ^ 1, (one,), slice(0, half))]
            got.append(send_rows(me ^ 1, ("c",)))
            wide.wait_recv()
            corner.append(send_rows(me ^ 2, (two,), slice(half, 2 * half)))
            got.append(send_rows(me ^ 2, ("c",)))
        beside.wait_recv()
        part = blocks(stage, places[stage] ^ 1, (slice(0, 2),))
        passed = [sender.start(part, part, (up,))]
        above.wait_recv()
        part = blocks(stage, places[stage] ^ 2, (slice(2, 4),))
        passed.append(sender.start(part, part, (across,)))
        if stage == 1:
            for copy in corner:
                copy.wait_recv()
            got.append(send_rows(me ^ 3, ("c",)))
        for copy in passed:
            copy.wait_recv()
    for copy in got:
        copy.wait_recv()
    crossing.wait_recv()
    sender.finish()


def second_gather(squares, pair, over, rows, value, piece):
    vmem = pl.BlockSpec(memory_space=pltpu.VMEM)
    copies = 3 + 4 * (len(squares) - 1) + 9
    gathered, tokens, crossed = pl.pallas_call(
        functools.partial(second_kernel, squares, pair, over),
        out_shape=(
            jax.ShapeDtypeStruct((4,) * len(squares) + rows.shape, bf16),
            jax.ShapeDtypeStruct((4, 2) + value.shape, bf16),
            jax.ShapeDtypeStruct(piece.shape, bf16),
        ),
        in_specs=[vmem] * 3,
        out_specs=(vmem,) * 3,
        scratch_shapes=[pltpu.SemaphoreType.DMA((copies,)), pltpu.SemaphoreType.DMA((copies,))],
        compiler_params=pltpu.CompilerParams(
            collective_id=4, has_side_effects=True, vmem_limit_bytes=40 << 20
        ),
        cost_estimate=pl.CostEstimate(flops=1, transcendentals=0, bytes_accessed=1),
    )(rows, value, piece)
    return gathered.reshape(-1, rows.shape[1]), tokens.reshape(-1, value.shape[1]), crossed


def lay_copies(fsdp, pair, spread, pieces, target, sems):
    copies = []
    for number, piece in enumerate(pieces):
        for block in range(4):
            place = 0
            for axis in fsdp:
                if axis == pair[0]:
                    bit = block >> 1
                elif axis == pair[1]:
                    bit = block & 1
                else:
                    bit = lax.axis_index(axis) ^ ((number >> spread.index(axis)) & 1)
                place = place * 2 + bit
            copies.append(pltpu.make_async_copy(piece.at[block], target.at[place], sems.at[len(copies)]))
    for copy in copies:
        copy.start()
    return copies


def lay_kernel(fsdp, pair, spread, *refs):
    count = 2 ** len(spread)
    target, sems = refs[count:]
    for copy in lay_copies(fsdp, pair, spread, refs[:count], target, sems):
        copy.wait()


def lay(pieces, fsdp, pair, spread):
    rows, cols = pieces[0].shape[1:]
    blocks = 4 * len(pieces)
    out = pl.pallas_call(
        functools.partial(lay_kernel, fsdp, pair, spread),
        out_shape=jax.ShapeDtypeStruct((blocks, rows, cols), bf16),
        in_specs=[pl.BlockSpec(memory_space=pltpu.HBM)] * len(pieces),
        out_specs=pl.BlockSpec(memory_space=pltpu.VMEM),
        scratch_shapes=[pltpu.SemaphoreType.DMA((blocks,))],
        compiler_params=pltpu.CompilerParams(vmem_limit_bytes=32 << 20),
        cost_estimate=pl.CostEstimate(
            flops=0, transcendentals=0, bytes_accessed=4 * blocks * rows * cols
        ),
    )(*pieces)
    return out.reshape(blocks * rows, cols)


def tokens_kernel(pair, value_ref, out_ref, send_sems, recv_sems):
    core = lax.axis_index("c")
    me = place_of(*pair)
    one, two = pair
    half = value_ref.shape[0] // 2
    sender = Sender(send_sems, recv_sems)
    out_ref[me, core] = value_ref[...]
    meet([(two,), (one,), ("c",)])

    def send(place, axes, rows=slice(None)):
        mine = out_ref.at[place, core, rows]
        return sender.start(mine, mine, axes)

    near = send(me, (two,))
    wide = send(me, (one,))
    got = [send(me, ("c",))]
    near.wait_recv()
    far = [send(me ^ 1, (one,), slice(0, half))]
    got.append(send(me ^ 1, ("c",)))
    wide.wait_recv()
    far.append(send(me ^ 2, (two,), slice(half, 2 * half)))
    got.append(send(me ^ 2, ("c",)))
    for copy in far:
        copy.wait_recv()
    got.append(send(me ^ 3, ("c",)))
    for copy in got:
        copy.wait_recv()
    sender.finish()


def tokens_of_chips(value, pair, number):
    rows, cols = value.shape
    vmem = pl.BlockSpec(memory_space=pltpu.VMEM)
    out = pl.pallas_call(
        functools.partial(tokens_kernel, pair),
        out_shape=jax.ShapeDtypeStruct((4, 2, rows, cols), bf16),
        in_specs=[vmem],
        out_specs=vmem,
        scratch_shapes=[pltpu.SemaphoreType.DMA((8,)), pltpu.SemaphoreType.DMA((8,))],
        compiler_params=pltpu.CompilerParams(
            collective_id=number, has_side_effects=True, vmem_limit_bytes=24 << 20
        ),
        cost_estimate=pl.CostEstimate(flops=1, transcendentals=0, bytes_accessed=1),
    )(value)
    return out.reshape(8 * rows, cols)


def merge_kernel(which, parts_ref, out_ref):
    cols = out_ref.shape[1] // 4
    for quarter in range(4):
        out_ref[:, quarter * cols : (quarter + 1) * cols] = parts_ref[0, quarter].astype(f32)


def merge(parts, which):
    rows, cols = parts.shape[2:]
    return pl.pallas_call(
        functools.partial(merge_kernel, which),
        grid=(1,),
        out_shape=jax.ShapeDtypeStruct((rows, 4 * cols), f32),
        in_specs=[pl.BlockSpec((1, 4, rows, cols), lambda i: (which, 0, 0, 0))],
        out_specs=pl.BlockSpec((rows, 4 * cols), lambda i: (0, 0)),
        cost_estimate=pl.CostEstimate(
            flops=0, transcendentals=0, bytes_accessed=24 * rows * cols
        ),
    )(parts)


class Reduction:
    def __init__(self, sender, held, dims, order, buffers, out):
        self.sender, self.held, self.dims, self.order = sender, held, list(dims), list(order)
        self.buffers, self.out = list(buffers), out

    def half(self, at):
        return (slice(None),) * self.dims.index(self.order[0]) + (at,)

    def begin(self):
        axis = self.order[0]
        source = self.held.at[self.half(1 - lax.axis_index(axis))]
        self.copy = self.sender.start(source, self.buffers[0], (axis,))

    def end(self):
        self.copy.wait_recv()
        axis = self.order[0]
        own = self.held[self.half(lax.axis_index(axis))]
        total = own.astype(f32) + self.buffers[0][...].astype(f32)
        self.held = self.buffers.pop(0)
        self.dims.remove(axis)
        self.order.pop(0)
        if self.order:
            self.held[...] = total.astype(bf16)
            self.begin()
        else:
            self.out[...] = total

    def finish(self):
        while self.order:
            self.end()


def halves_of(rows):
    half = rows // 2 // 16 * 16
    return pl.ds(0, half), pl.ds(half, rows - half)


def last_kernel(
    fsdp,
    pair,
    peak_ref,
    small_ref,
    gains_ref,
    q_ref,
    kv_ref,
    out_ref,
    down_ref,
    gate_ref,
    up_ref,
    small_sum,
    gains_sum,
    q_sum,
    kv_sum,
    out_sum,
    ffn_out,
    peak_out,
    *scratch,
):
    scratch = list(scratch)
    stages = len(fsdp)
    sender = Sender(scratch.pop(), scratch.pop())

    def buffers(count):
        taken = scratch[:count]
        del scratch[:count]
        return taken

    down = list(reversed(fsdp))
    turned = [down[1], down[0]] + down[2:]
    with_core = fsdp + ["c"]
    small = Reduction(sender, small_ref, with_core, ["c"] + turned, buffers(stages + 1), small_sum)
    gains = Reduction(sender, gains_ref, with_core, ["c"] + down, buffers(stages + 1), gains_sum)
    q = Reduction(sender, q_ref, fsdp, down, buffers(stages), q_sum)
    kv = Reduction(sender, kv_ref, fsdp, turned, buffers(stages), kv_sum)
    upward = [down[-2]] + turned[:-2] + [down[-1]]
    outs = []
    for rows, order in zip(halves_of(out_sum.shape[0]), (turned, upward)):
        part = out_ref.at[(slice(None),) * stages + (rows,)]
        outs.append(Reduction(sender, part, fsdp, order, buffers(stages), out_sum.at[rows]))
    over = buffers(2)
    peaks = buffers(stages)
    me = place_of(*pair)
    row = lax.axis_index(fsdp[0])
    meet([(axis,) for axis in with_core] + [pair])

    def send_columns(which, held):
        ffn_out[which, me] = held[me]
        return [
            sender.start(held.at[me ^ away], ffn_out.at[which, me], axes)
            for away, axes in ((1, (pair[1],)), (2, (pair[0],)), (3, pair))
        ]

    peak_out[...] = peak_ref[...]

    def send_peaks(stage):
        return sender.start(peak_out, peaks[stage], (fsdp[stage],))

    def next_peaks(stage, sent):
        sent.wait()
        sender.left.append(sent)
        peak_out[...] = jnp.maximum(peak_out[...], peaks[stage][...])
        return send_peaks(stage + 1) if stage < stages - 1 else None

    for part in (small, gains, q, outs[0], kv):
        part.begin()
    peak_sent = send_peaks(0)
    crossing = sender.start(down_ref.at[1 - row], over[0], (fsdp[0],))
    outs[1].begin()
    columns = send_columns(1, gate_ref)
    small.end()
    gains.end()
    peak_sent = next_peaks(0, peak_sent)
    for part in (q, kv, outs[0]):
        part.end()
    def crossed(which, ref, buffer):
        crossing.wait_recv()
        buffer[...] = (ref[row].astype(f32) + buffer[...].astype(f32)).astype(bf16)
        return send_columns(which, buffer)

    columns += crossed(0, down_ref, over[0])
    crossing = sender.start(up_ref.at[1 - row], over[1], (fsdp[0],))
    for stage in range(1, stages):
        peak_sent = next_peaks(stage, peak_sent)
        for part in (outs[1], small, gains, q, kv, outs[0]):
            part.end()
        if stage == 1:
            columns += crossed(2, up_ref, over[1])
    for reduction in (q, kv, outs[0], small, gains, outs[1]):
        reduction.finish()
    for copy in columns:
        copy.wait_recv()
    sender.finish()


def last_scatter(fsdp, pair, peak, small, gains, q, kv, out, down, gate, up):
    vmem = pl.BlockSpec(memory_space=pltpu.VMEM)
    stages = len(fsdp)

    def buffers(array, count, rows=None):
        lead = array.ndim - 2
        block = (rows or array.shape[-2], array.shape[-1])
        return [pltpu.VMEM((2,) * (lead - 1 - i) + block, bf16) for i in range(count)]

    scratch = (
        buffers(small, stages + 1)
        + buffers(gains, stages + 1)
        + buffers(q, stages)
        + buffers(kv, stages)
        + [buf for rows in halves_of(out.shape[-2]) for buf in buffers(out, stages, rows.size)]
        + [pltpu.VMEM(gate.shape, bf16)] * 2
        + [pltpu.VMEM(peak.shape, f32)] * stages
    )
    copies = 2 * (stages + 1) + 4 * stages + 2 + 9 + stages
    return pl.pallas_call(
        functools.partial(last_kernel, fsdp, pair),
        out_shape=tuple(jax.ShapeDtypeStruct(x.shape[-2:], f32) for x in (small, gains, q, kv, out))
        + (
            jax.ShapeDtypeStruct((3,) + gate.shape, bf16),
            jax.ShapeDtypeStruct(peak.shape, f32),
        ),
        in_specs=[vmem] * 9,
        out_specs=(vmem,) * 7,
        scratch_shapes=scratch
        + [pltpu.SemaphoreType.DMA((copies,)), pltpu.SemaphoreType.DMA((copies,))],
        compiler_params=pltpu.CompilerParams(
            collective_id=2, has_side_effects=True, vmem_limit_bytes=60 << 20
        ),
    )(peak, small, gains, q, kv, out, down, gate, up)


def shards(
    fsdp,
    hidden_in,
    seq_ids,
    block_ids,
    clip_limit,
    cotangent,
    q_down,
    kv_down,
    q_up,
    kv_up,
    out_proj,
    gate_proj,
    up_proj,
    down_proj,
    in_gain,
    q_gain,
    kv_gain,
    post_gain,
):
    tokens_here, width = hidden_in.shape
    seq_row = seq_ids[0]
    block_row = block_ids[0]
    group = seq_row.shape[0]
    heads = q_up.shape[1] // (NOPE + ROPE)
    score_scale = 1.0 / math.sqrt(NOPE + ROPE)
    core = lax.axis_index("c")
    first_row = core * tokens_here
    wide, near = fsdp[1], fsdp[-1]
    pair = (wide, near)
    spread = [axis for axis in fsdp if axis not in pair]
    squares = [(fsdp[i], fsdp[i + 1]) for i in range(0, len(fsdp), 2)]
    at_wide, at_near = lax.axis_index(wide), lax.axis_index(near)
    chips = tuple(fsdp)
    count = 2 ** len(fsdp)

    small_rows = q_down.shape[0]
    q_rank = q_down.shape[1]
    small_cols = q_rank + kv_down.shape[1]

    def row(value):
        return jnp.pad(value, ((0, 0), (0, TILE - value.shape[1])))[:, None, :]

    def rows_of(*values):
        held = jnp.concatenate([row(value) for value in values], axis=1)
        return jnp.pad(held, ((0, 0), (0, 8 - len(values)), (0, 0)))

    small = jnp.concatenate([q_down, kv_down], axis=1)
    gains = rows_of(in_gain[None], post_gain[None], q_gain[None], kv_gain[None])[0]
    q_up_wide = jnp.pad(
        q_up.reshape(-1, heads, NOPE + ROPE), ((0, 0), (0, 0), (0, TILE - NOPE - ROPE))
    ).reshape(-1, heads * TILE)
    small_all, gains_all, q_up_all, kv_up_all, *pieces = first_gather(
        squares, pair, spread, small, gains, q_up_wide, kv_up, gate_proj, up_proj, down_proj
    )
    down_full = small_all.reshape(-1, small_cols)
    q_up_full = q_up_all.reshape(-1, heads * TILE)
    kv_up_full = kv_up_all.reshape(-1, kv_up.shape[1])
    devices = 2 * count

    def gain(at, size):
        return gains_all.reshape(devices, 8, TILE)[:, at, :size].reshape(-1).astype(f32)

    in_float = gain(0, in_gain.shape[0])
    post_float = gain(1, post_gain.shape[0])
    q_gain_float = gain(2, q_gain.shape[0])
    kv_gain_float = gain(3, kv_gain.shape[0])

    cot_float = cotangent.astype(f32)

    def over(pieces, axis, *ready):
        return [swap(after(piece, *ready), axis) for piece in pieces]

    def exchange(held, dims, axis):
        at, dim = lax.axis_index(axis), dims.index(axis)
        return swap(pick(held, 1 - at, dim), axis), pick(held, at, dim)

    def sum_of_chips(held):
        held = held.reshape(2, 2, tokens_here, width)
        return square_scatter(held, wide, near, 0).reshape(tokens_here, width)

    def core_both(value):
        return both(value, swap(value, "c"), "c", 0)

    def core_sum(value):
        def rows(at):
            return lax.dynamic_slice_in_dim(value, at * tokens_here, tokens_here)

        return rows(core) + swap(rows(1 - core), "c")

    x_float = hidden_in.astype(f32)
    x_normed = rms_scale(x_float, in_float).astype(bf16)
    pre = jnp.dot(x_normed, down_full, preferred_element_type=f32)
    q_pre = pre[:, :q_rank]
    c_lat_pre = pre[:, q_rank : q_rank + KVR]
    c_rot_pre = pre[:, q_rank + KVR :]
    own_cos, own_sin = angles(seq_row, first_row, tokens_here)
    q_latent = rms_scale(q_pre, q_gain_float).astype(bf16)
    kv_latent = rms_scale(c_lat_pre, kv_gain_float).astype(bf16)
    key_rot = rotate(c_rot_pre, own_cos, own_sin).astype(bf16)
    key_rot = jnp.pad(key_rot, ((0, 0), (NOPE, TILE - NOPE - ROPE)))
    latents = core_both(jnp.concatenate([q_latent, kv_latent, key_rot], axis=1))
    q_lat_all = latents[:, :q_rank]
    kv_lat_all = latents[:, q_rank : q_rank + KVR]
    key_rot_all = latents[:, q_rank + KVR :]
    all_cos, all_sin = angles(seq_row, 0, group)
    q_full = jnp.dot(q_lat_all, q_up_full, preferred_element_type=f32)
    kv_full = jnp.dot(kv_lat_all, kv_up_full, preferred_element_type=f32).astype(bf16)
    allowed = (seq_row[None, :] == seq_row[:, None]) & (block_row[:, None] <= block_row[None, :])
    bias = jnp.where(allowed, 0.0, -1e30).astype(f32)
    axes = list(spread)
    gate_held, gate_over, gate_last, up_held, down_held = pieces
    gate_pieces = [gate_held, gate_over, gate_last, swap(gate_over, axes[1])]
    for axis in axes[2:]:
        gate_pieces += over(gate_pieces, axis)
    up_pieces = [swap(up_held, axes[0]), swap(up_held, axes[1])]
    attn, queries, log_total, local_peak = attend(
        q_full, kv_full, key_rot_all, tables(all_cos, all_sin), bias, score_scale
    )
    d_ffn = (resid_scale * cot_float).astype(bf16)
    out_full, d_ffn_all, down_over = second_gather(
        squares, pair, axes[0], after(out_proj, attn), d_ffn, down_held
    )
    attn, out_full, down_over, *early = lax.optimization_barrier(
        (attn, out_full, down_over, *up_pieces, *gate_pieces)
    )
    up_pieces, gate_pieces = early[:2], early[2:]
    branch = core_sum(contract(attn, out_full, 1, 1))
    mid = x_float + resid_scale * branch
    mid_normed = rms_scale(mid, post_float).astype(bf16)
    gate_full = lay(gate_pieces, fsdp, pair, spread)
    mid_all = tokens_of_chips(after(mid_normed, gate_full), pair, 1)
    up_pieces = [up_held, *up_pieces, swap(after(up_pieces[0], attn), axes[1])]
    down_last = swap(after(down_held, attn), axes[1])
    mid_all, down_last, *up_pieces = lax.optimization_barrier((mid_all, down_last, *up_pieces))
    down_pieces = [down_held, down_over, down_last, swap(after(down_over, mid_all), axes[1])]
    for axis in axes[2:]:
        up_pieces += over(up_pieces, axis)
        down_pieces += over(down_pieces, axis)
    up_full = lay(up_pieces, fsdp, pair, spread)
    gate = jnp.dot(mid_all, gate_full, preferred_element_type=f32)
    up_value = jnp.dot(mid_all, up_full, preferred_element_type=f32)
    down_proj_full = lay(down_pieces, fsdp, pair, spread)
    sigmoid = jax.nn.sigmoid(gate)
    silu_value = gate * sigmoid
    act = (silu_value * up_value).astype(bf16)

    d_act = jnp.dot(d_ffn_all, down_proj_full, preferred_element_type=f32)
    d_gate = (d_act * up_value * (sigmoid * (1.0 + gate * (1.0 - sigmoid)))).astype(bf16)
    d_up = (d_act * silu_value).astype(bf16)
    dims = list(fsdp)
    first, last = spread[0], spread[-1]

    def added(parts):
        return (parts[0].astype(f32) + parts[1].astype(f32)).astype(bf16)

    def inner(held):
        left = [axis for axis in dims if axis != last]
        for axis in reversed(spread[1:-1]):
            held = added(exchange(held, left, axis))
            left.remove(axis)
        return held

    def begin(left, right, *ready):
        keep, send = grad_halves(left, right, width // count, last)
        shape = [2] * (len(fsdp) - 1) + [width // count, -1]
        return swap(after(send, *ready), last).reshape(shape), keep.reshape(shape), keep

    def cross(held):
        return exchange(held, [first, *pair], first)

    *down_parts, down_grad = begin(d_ffn_all, act)
    d_gate_late, _ = lax.optimization_barrier((d_gate, down_grad))
    gate_keep, gate_send = grad_halves(mid_all, d_gate_late, width // count, last)
    d_up_late, d_gate_late, _ = lax.optimization_barrier((d_up, d_gate, gate_keep))
    d_mid_held = core_features(
        tokens_here, 3, (d_gate_late, gate_full), (d_up_late, up_full)
    )
    d_mid_held, *down_parts = lax.optimization_barrier((d_mid_held, *down_parts))
    d_mid_normed = sum_of_chips(d_mid_held)
    mid_late, gate_send, _ = lax.optimization_barrier((mid_all, gate_send, d_mid_held))
    shape = [2] * (len(fsdp) - 1) + [width // count, -1]
    gate_parts = (swap(gate_send, last).reshape(shape), gate_keep.reshape(shape))
    down_held = inner(added(down_parts))
    *up_parts, up_grad = begin(mid_late, d_up, gate_parts[0])
    ffn_part = features((after(act, up_grad), down_proj_full))
    post_pull = jax.vjp(rms_scale, mid, post_float)[1]
    d_mid_normed, *early = lax.optimization_barrier(
        (d_mid_normed, down_held, *gate_parts, ffn_part)
    )
    down_held, gate_parts, ffn_part = early[0], early[1:3], early[3]
    d_mid_norm, post_grad = post_pull(d_mid_normed)
    ffn = lax.psum_scatter(
        after(ffn_part, d_mid_norm), (wide, near, "c"), scatter_dimension=0, tiled=True
    )
    layer_out = (mid + resid_scale * ffn.astype(f32)).astype(bf16)
    d_mid = cot_float + d_mid_norm
    d_branch = (resid_scale * d_mid).astype(bf16)
    d_branch_all = core_both(d_branch)
    d_attn = jnp.dot(d_branch_all, out_full, preferred_element_type=f32).astype(bf16)
    gate_parts = cross(inner(added(gate_parts)))
    d_q, d_kv, d_rot_part = attend_back(
        queries,
        kv_full,
        d_attn,
        log_total,
        key_rot_all,
        tables(all_cos, -all_sin),
        bias,
        score_scale,
    )
    q_up_grad = heads_grad(q_lat_all, d_q)
    out_grad = plain_grad(after(d_branch_all, q_up_grad), attn)
    d_q_lat_part = contract(d_q, q_up_full, 1, 1)
    d_kv_lat_part = contract(d_kv, kv_up_full, 1, 1)
    d_q_lat_part, d_kv_lat_part, d_kv, out_grad, *early = lax.optimization_barrier(
        (d_q_lat_part, d_kv_lat_part, d_kv, out_grad, *gate_parts, *up_parts)
    )
    gate_parts, up_parts = early[:2], early[2:]
    kv_up_grad = rows_first(contract(kv_lat_all, d_kv, 0, 0).astype(bf16))
    d_latents = core_sum(jnp.concatenate([d_q_lat_part, d_kv_lat_part, d_rot_part], axis=1))
    q_pull = jax.vjp(rms_scale, q_pre, q_gain_float)[1]
    d_q_pre, q_gain_grad = q_pull(d_latents[:, :q_rank])
    kv_pull = jax.vjp(rms_scale, c_lat_pre, kv_gain_float)[1]
    d_c_lat, kv_gain_grad = kv_pull(d_latents[:, q_rank : q_rank + KVR])
    d_key_rot = d_latents[:, q_rank + KVR + NOPE : q_rank + KVR + NOPE + ROPE]
    d_pre = jnp.concatenate(
        [d_q_pre, d_c_lat, rotate(d_key_rot, own_cos, -own_sin)], axis=-1
    ).astype(bf16)
    down_grads = rows_first(contract(x_normed, d_pre, 0, 0).astype(bf16))
    d_x_normed = contract(d_pre, down_full, 1, 1)
    in_pull = jax.vjp(rms_scale, x_float, in_float)[1]
    d_x_norm, in_grad = in_pull(d_x_normed)
    input_grad = d_mid + d_x_norm

    rows_here = width // count
    ffn_held = [
        down_held.reshape(2, 4, rows_here, -1),
        added(gate_parts).reshape(4, rows_here, -1),
        inner(added(up_parts)).reshape(2, 4, rows_here, -1),
    ]
    gain_grads = rows_of(
        *(grad.reshape(devices, -1) for grad in (in_grad, post_grad, q_gain_grad, kv_gain_grad))
    ).astype(bf16)

    def blocks(grad, lead):
        return grad.reshape([2] * lead + [grad.shape[0] // 2**lead, -1])

    small_out, gain_out, q_up_out, kv_up_out, out_out, ffn_cols, peak_all = last_scatter(
        fsdp,
        pair,
        local_peak,
        blocks(down_grads, len(fsdp) + 1),
        gain_grads.reshape([2] * (len(fsdp) + 1) + [8, TILE]),
        blocks(q_up_grad, len(fsdp)),
        blocks(kv_up_grad, len(fsdp)),
        blocks(out_grad, len(fsdp)),
        *ffn_held,
    )
    down_out, gate_out, up_out = (merge(ffn_cols, which) for which in range(3))
    peaks = peak_all[0, :heads]
    limit = clip_limit[0]
    factors = limit / jnp.maximum(peaks, limit)
    root = jnp.sqrt(factors)
    q_cols = jnp.concatenate(
        [
            jnp.broadcast_to(root[:, None], (heads, NOPE)),
            jnp.broadcast_to(factors[:, None], (heads, ROPE)),
        ],
        axis=1,
    ).reshape(heads * (NOPE + ROPE))
    kv_cols = jnp.concatenate(
        [jnp.broadcast_to(root[:, None], (heads, NOPE)), jnp.ones((heads, VD), f32)], axis=1
    ).reshape(heads * (NOPE + VD))
    q_clipped = (q_up.astype(f32) * q_cols[None, :]).astype(bf16)
    kv_clipped = (kv_up.astype(f32) * kv_cols[None, :]).astype(bf16)
    return (
        layer_out,
        input_grad,
        small_out[:, :q_rank],
        small_out[:, q_rank:],
        q_up_out,
        kv_up_out,
        out_out,
        gate_out,
        up_out,
        down_out,
        gain_out[0, : in_gain.shape[0]],
        gain_out[2, : q_gain.shape[0]],
        gain_out[3, : kv_gain.shape[0]],
        gain_out[1, : post_gain.shape[0]],
        q_clipped,
        kv_clipped,
        peaks,
        factors,
    )


def solution(mesh):
    bits = mesh.shape["fsdp"].bit_length() - 1
    fsdp = [f"f{i}" for i in range(bits)]
    fine = Mesh(mesh.devices.reshape((2,) * (bits + 1)), tuple(fsdp) + ("c",))
    split = tuple(fsdp)
    whole = split + ("c",)
    return jax.shard_map(
        functools.partial(shards, fsdp),
        mesh=fine,
        in_specs=(
            P(whole, None),
            P(split, None),
            P(split, None),
            P(),
            P(whole, None),
            P(whole, None),
            P(whole, None),
            P(split, "c"),
            P(split, "c"),
            P(split, "c"),
            P(split, "c"),
            P(split, "c"),
            P(split, "c"),
            P(whole),
            P(whole),
            P(whole),
            P(whole),
        ),
        out_specs=(
            P(whole, None),
            P(whole, None),
            P(whole, None),
            P(whole, None),
            P(split, "c"),
            P(split, "c"),
            P(split, "c"),
            P(split, "c"),
            P(split, "c"),
            P(split, "c"),
            P(whole),
            P(whole),
            P(whole),
            P(whole),
            P(split, "c"),
            P(split, "c"),
            P("c"),
            P("c"),
        ),
        check_vma=False,
    )
```

```python
import functools
import math

import jax
import jax.numpy as jnp
from jax import lax
from jax.experimental import pallas as pl
from jax.experimental.pallas import tpu as pltpu
from jax.experimental.layout import Layout, with_layout_constraint
from jax.sharding import Mesh
from jax.sharding import PartitionSpec as P

NOPE = 64
ROPE = 32
VD = 64
KVR = 256
TILE = 128


eps = 1e-05
resid_scale = 1.4 / math.sqrt(62.0)
rope_base = 10000.0
SWAP = [(0, 1), (1, 0)]
f32 = jnp.float32
bf16 = jnp.bfloat16


def rms_scale(value, gain):
    return value * lax.rsqrt(jnp.mean(value * value, axis=-1, keepdims=True) + eps) * gain


def rotate(value, cosine, sine):
    half = value.shape[-1] // 2
    first = value[..., :half]
    second = value[..., half:]
    return jnp.concatenate(
        [first * cosine - second * sine, second * cosine + first * sine], axis=-1
    )


def angles(seq_row, start, count):
    own_ids = lax.dynamic_slice_in_dim(seq_row, start, count)
    earlier = jnp.sum((seq_row[None, :] < own_ids[:, None]).astype(jnp.int32), axis=1)
    place = (start + jnp.arange(count, dtype=jnp.int32) - earlier).astype(f32)
    freq = jnp.power(rope_base, -jnp.arange(ROPE // 2, dtype=f32) * (2.0 / ROPE))
    turn = place[:, None] * freq[None, :]
    return (jnp.cos(turn), jnp.sin(turn))


def contract(left, right, left_dim, right_dim):
    return lax.dot_general(
        left, right, (((left_dim,), (right_dim,)), ((), ())), preferred_element_type=f32
    )


def turn(value, plain, first, second):
    return (
        value * plain
        + pltpu.roll(value, TILE - ROPE // 2, 1) * first
        + pltpu.roll(value, ROPE // 2, 1) * second
    )


def tables(cosine, sine):
    rows = cosine.shape[0]
    half = ROPE // 2

    def zeros(count):
        return jnp.zeros((rows, count), f32)

    plain = jnp.concatenate([jnp.ones((rows, NOPE), f32), cosine, cosine, zeros(TILE - NOPE - ROPE)], axis=1)
    first = jnp.concatenate([zeros(NOPE), -sine, zeros(TILE - NOPE - half)], axis=1)
    second = jnp.concatenate([zeros(NOPE + half), sine, zeros(TILE - NOPE - ROPE)], axis=1)
    return plain, first, second


def attend_kernel(
    scale,
    q_ref,
    kv_ref,
    rot_ref,
    plain_ref,
    first_ref,
    second_ref,
    bias_ref,
    mixed_ref,
    query_ref,
    total_ref,
    peak_ref,
):
    step = pl.program_id(0)
    lane = lax.broadcasted_iota(jnp.int32, (q_ref.shape[0], TILE), 1)
    spot = lax.broadcasted_iota(jnp.int32, peak_ref.shape, 1)

    @pl.when(step == 0)
    def _():
        peak_ref[...] = jnp.zeros_like(peak_ref)

    outs = []
    for one in range(2):
        cols = slice(one * TILE, (one + 1) * TILE)
        query = turn(q_ref[:, cols], plain_ref[...], first_ref[...], second_ref[...]).astype(bf16)
        query_ref[:, cols] = query
        kv = kv_ref[:, cols]
        keys = jnp.where(lane < NOPE, kv, rot_ref[...])
        masked = contract(keys, query, 1, 1) * scale + bias_ref[...]
        top = jnp.max(masked, axis=0, keepdims=True)
        weights = jnp.exp(masked - top)
        total = jnp.sum(weights, axis=0, keepdims=True)
        chance = (weights * (1.0 / total)).astype(bf16)
        outs.append(contract(chance, kv, 0, 0))
        total_ref[0, one : one + 1, :] = top + jnp.log(total)
        peak_ref[...] = jnp.where(spot == step * 2 + one, jnp.max(top), peak_ref[...])
    mixed_ref[...] = jnp.where(lane < VD, pltpu.roll(outs[0], VD, 1), outs[1]).astype(bf16)


def attend(q, kv, rot, turns, bias, scale):
    group, cols = q.shape
    heads = cols // TILE
    whole = pl.BlockSpec((group, TILE), lambda i: (0, 0))
    two = pl.BlockSpec((group, 2 * TILE), lambda i: (0, i))
    return pl.pallas_call(
        functools.partial(attend_kernel, scale),
        grid=(heads // 2,),
        out_shape=(
            jax.ShapeDtypeStruct((group, heads * VD), bf16),
            jax.ShapeDtypeStruct((group, cols), bf16),
            jax.ShapeDtypeStruct((heads // 2, 2, group), f32),
            jax.ShapeDtypeStruct((8, TILE), f32),
        ),
        in_specs=[two, two, whole, whole, whole, whole, pl.BlockSpec((group, group), lambda i: (0, 0))],
        out_specs=(
            pl.BlockSpec((group, TILE), lambda i: (0, i)),
            two,
            pl.BlockSpec((1, 2, group), lambda i: (i, 0, 0)),
            pl.BlockSpec((8, TILE), lambda i: (0, 0)),
        ),
        compiler_params=pltpu.CompilerParams(
            dimension_semantics=("arbitrary",), vmem_limit_bytes=40 << 20
        ),
        cost_estimate=pl.CostEstimate(flops=1, transcendentals=0, bytes_accessed=1),
    )(q, kv, rot, *turns, bias)


def attend_back_kernel(
    scale,
    query_ref,
    kv_ref,
    d_mixed_ref,
    total_ref,
    rot_ref,
    plain_ref,
    first_ref,
    second_ref,
    bias_ref,
    d_q_ref,
    d_kv_ref,
    d_rot_ref,
):
    step = pl.program_id(0)
    lane = lax.broadcasted_iota(jnp.int32, (query_ref.shape[0], TILE), 1)

    @pl.when(step == 0)
    def _():
        d_rot_ref[...] = jnp.zeros_like(d_rot_ref)

    pair = d_mixed_ref[...].astype(f32)
    for one in range(2):
        cols = slice(one * TILE, (one + 1) * TILE)
        query = query_ref[:, cols]
        kv = kv_ref[:, cols]
        keys = jnp.where(lane < NOPE, kv, rot_ref[...])
        own = pair if one else pltpu.roll(pair, VD, 1)
        d_mixed = jnp.where(lane < VD, 0.0, own).astype(bf16)
        masked = contract(keys, query, 1, 1) * scale + bias_ref[...]
        chance = jnp.exp(masked - total_ref[0, one : one + 1, :])
        d_values = contract(chance.astype(bf16), d_mixed, 1, 0)
        d_chance = contract(kv, d_mixed, 1, 1)
        inner = jnp.sum(chance * d_chance, axis=0, keepdims=True)
        d_raw = (chance * (d_chance - inner) * scale).astype(bf16)
        d_keys = contract(d_raw, query, 1, 0)
        d_query = contract(d_raw, keys, 0, 0)
        d_q_ref[:, cols] = turn(
            d_query, plain_ref[...], first_ref[...], second_ref[...]
        ).astype(bf16)
        d_kv_ref[:, cols] = jnp.where(lane < NOPE, d_keys, d_values).astype(bf16)
        d_rot_ref[...] += d_keys


def attend_back(query, kv, d_mixed, total, rot, turns, bias, scale):
    group, cols = query.shape
    heads = cols // TILE
    whole = pl.BlockSpec((group, TILE), lambda i: (0, 0))
    two = pl.BlockSpec((group, 2 * TILE), lambda i: (0, i))
    return pl.pallas_call(
        functools.partial(attend_back_kernel, scale),
        grid=(heads // 2,),
        out_shape=(
            jax.ShapeDtypeStruct((group, cols), bf16),
            jax.ShapeDtypeStruct((group, cols), bf16),
            jax.ShapeDtypeStruct((group, TILE), f32),
        ),
        in_specs=[
            two,
            two,
            pl.BlockSpec((group, TILE), lambda i: (0, i)),
            pl.BlockSpec((1, 2, group), lambda i: (i, 0, 0)),
            whole,
            whole,
            whole,
            whole,
            pl.BlockSpec((group, group), lambda i: (0, 0)),
        ],
        out_specs=(two, two, whole),
        compiler_params=pltpu.CompilerParams(
            dimension_semantics=("arbitrary",), vmem_limit_bytes=40 << 20
        ),
        cost_estimate=pl.CostEstimate(flops=1, transcendentals=0, bytes_accessed=1),
    )(query, kv, d_mixed, total, rot, *turns, bias)


def swap(value, axis):
    return lax.ppermute(value, axis, SWAP)


def far(value, pair):
    return lax.ppermute(value, pair, [(i, 3 - i) for i in range(4)])


def after(value, *others):
    return lax.optimization_barrier((value,) + others)[0]


def pick(value, at, dim):
    return lax.dynamic_index_in_dim(value, at, dim, keepdims=True)


def both(own, other, axis, dim):
    here = lax.axis_index(axis) == 0
    return jnp.concatenate([jnp.where(here, own, other), jnp.where(here, other, own)], axis=dim)


def plain_grad_kernel(left_ref, right_ref, out_ref):
    out_ref[...] = contract(left_ref[...], right_ref[...], 0, 0).astype(bf16)


def plain_grad(left, right):
    rows, width = left.shape
    cols = right.shape[1]
    tile = 512
    return pl.pallas_call(
        plain_grad_kernel,
        grid=(width // tile,),
        out_shape=jax.ShapeDtypeStruct((width, cols), bf16),
        in_specs=[
            pl.BlockSpec((rows, tile), lambda i: (0, i)),
            pl.BlockSpec((rows, cols), lambda i: (0, 0)),
        ],
        out_specs=pl.BlockSpec((tile, cols), lambda i: (i, 0)),
        compiler_params=pltpu.CompilerParams(vmem_limit_bytes=32 << 20),
        cost_estimate=pl.CostEstimate(flops=1, transcendentals=0, bytes_accessed=1),
    )(left, right)


def heads_grad_kernel(latent_ref, d_ref, out_ref):
    total = contract(latent_ref[...], d_ref[...], 0, 0)
    parts = [total[:, i * TILE : i * TILE + NOPE + ROPE] for i in range(4)]
    out_ref[...] = jnp.concatenate(parts, axis=1).astype(bf16)


def heads_grad(latent, d_heads):
    group, rank = latent.shape
    packs = d_heads.shape[1] // (4 * TILE)
    cols = 4 * (NOPE + ROPE)
    return pl.pallas_call(
        heads_grad_kernel,
        grid=(packs,),
        out_shape=jax.ShapeDtypeStruct((rank, packs * cols), bf16),
        in_specs=[
            pl.BlockSpec((group, rank), lambda i: (0, 0)),
            pl.BlockSpec((group, 4 * TILE), lambda i: (0, i)),
        ],
        out_specs=pl.BlockSpec((rank, cols), lambda i: (0, i)),
        compiler_params=pltpu.CompilerParams(vmem_limit_bytes=32 << 20),
        cost_estimate=pl.CostEstimate(flops=1, transcendentals=0, bytes_accessed=1),
    )(latent, d_heads)


def features_kernel(*refs):
    out_ref = refs[-1]
    total = contract(refs[0][...], refs[1][...], 1, 1)
    for i in range(2, len(refs) - 1, 2):
        total += contract(refs[i][...], refs[i + 1][...], 1, 1)
    out_ref[...] = total.astype(bf16)


def features(*pairs):
    rows, cols = pairs[0][0].shape
    width = pairs[0][1].shape[0]
    tile = min(rows, 512)
    return pl.pallas_call(
        features_kernel,
        grid=(rows // tile,),
        out_shape=jax.ShapeDtypeStruct((rows, width), bf16),
        in_specs=[
            pl.BlockSpec((tile, cols), lambda i: (i, 0)),
            pl.BlockSpec((width, cols), lambda i: (0, 0)),
        ]
        * len(pairs),
        out_specs=pl.BlockSpec((tile, width), lambda i: (i, 0)),
        compiler_params=pltpu.CompilerParams(vmem_limit_bytes=56 << 20),
        cost_estimate=pl.CostEstimate(flops=1, transcendentals=0, bytes_accessed=1),
    )(*(array for pair in pairs for array in pair))


def core_features_kernel(*refs):
    *operands, out_ref, total, sent, got, send_sems, recv_sems = refs
    step = pl.program_id(0)
    core = lax.axis_index("c")
    half = total.shape[1]

    @pl.when(step == 0)
    def _():
        meet([("c",)])

    def copy(at):
        return pltpu.make_async_remote_copy(
            src_ref=sent.at[at],
            dst_ref=got.at[at],
            send_sem=send_sems.at[at],
            recv_sem=recv_sems.at[at],
            device_id=other_of(("c",)),
            device_id_type=pl.DeviceIdType.MESH,
        )

    value = contract(operands[0][...], operands[1][...], 1, 1)
    for i in range(2, len(operands), 2):
        value += contract(operands[i][...], operands[i + 1][...], 1, 1)
    total[0] = value[:half].astype(bf16)
    total[1] = value[half:].astype(bf16)
    sent[step] = total[1 - core]
    copy(step).start()
    out_ref[step] = total[core]

    @pl.when(step == pl.num_programs(0) - 1)
    def _():
        for at in range(out_ref.shape[0]):
            copy(at).wait()
            out_ref[at] = (out_ref[at].astype(f32) + got[at].astype(f32)).astype(bf16)


def core_features(rows, number, *pairs):
    cols = pairs[0][0].shape[1]
    width = pairs[0][1].shape[0]
    block = (4, rows, width)
    return pl.pallas_call(
        core_features_kernel,
        grid=(4,),
        out_shape=jax.ShapeDtypeStruct(block, bf16),
        in_specs=[
            pl.BlockSpec((2 * rows, cols), lambda i: (i, 0)),
            pl.BlockSpec((width, cols), lambda i: (0, 0), pipeline_mode=pl.Buffered(1)),
        ]
        * len(pairs),
        out_specs=pl.BlockSpec(block, lambda i: (0, 0, 0)),
        scratch_shapes=[
            pltpu.VMEM((2, rows, width), bf16),
            pltpu.VMEM(block, bf16),
            pltpu.VMEM(block, bf16),
            pltpu.SemaphoreType.DMA((4,)),
            pltpu.SemaphoreType.DMA((4,)),
        ],
        compiler_params=pltpu.CompilerParams(
            dimension_semantics=("arbitrary",),
            collective_id=number,
            has_side_effects=True,
            vmem_limit_bytes=58 << 20,
        ),
        cost_estimate=pl.CostEstimate(flops=1, transcendentals=0, bytes_accessed=1),
    )(*(array for pair in pairs for array in pair))


def grad_kernel(axis, left_ref, right_ref, keep_ref, send_ref, total):
    half = total.shape[1]
    value = contract(left_ref[...], right_ref[...], 0, 0).astype(bf16)
    total[0] = value[:half]
    total[1] = value[half:]
    at = lax.axis_index(axis)
    keep_ref[0] = total[at]
    send_ref[0] = total[1 - at]


def grad_halves(left, right, rows, axis):
    tokens, width = left.shape
    cols = right.shape[1]
    tile = 4 * rows
    if tile % TILE:
        held = rows_first(contract(left, right, 0, 0).astype(bf16)).reshape(-1, 2, 2 * rows, cols)
        at = lax.axis_index(axis)
        return tuple(pick(held, i, 1)[:, 0] for i in (at, 1 - at))
    out = jax.ShapeDtypeStruct((width // tile, 2 * rows, cols), bf16)
    return pl.pallas_call(
        functools.partial(grad_kernel, axis),
        grid=(width // tile,),
        out_shape=(out, out),
        in_specs=[
            pl.BlockSpec((tokens, tile), lambda i: (0, i)),
            pl.BlockSpec((tokens, cols), lambda i: (0, 0)),
        ],
        out_specs=(pl.BlockSpec((1, 2 * rows, cols), lambda i: (i, 0, 0)),) * 2,
        scratch_shapes=[pltpu.VMEM((2, 2 * rows, cols), bf16)],
        compiler_params=pltpu.CompilerParams(vmem_limit_bytes=56 << 20),
        cost_estimate=pl.CostEstimate(flops=1, transcendentals=0, bytes_accessed=1),
    )(left, right)


def rows_first(value):
    return with_layout_constraint(value, Layout(major_to_minor=(0, 1)))


def square_scatter(held, first, second, dim):
    here, there = lax.axis_index(first), lax.axis_index(second)

    def part(w, n):
        return pick(pick(held, w, dim), n, dim + 1)

    near = swap(part(here, 1 - there).astype(bf16), second)
    wide = swap(part(1 - here, there).astype(bf16), first)
    corner = far(part(1 - here, 1 - there).astype(bf16), (first, second))
    own = part(here, there).astype(f32)
    return own + near.astype(f32) + wide.astype(f32) + corner.astype(f32)


def place_of(first, second):
    return lax.axis_index(first) * 2 + lax.axis_index(second)


def other_of(axes):
    return {axis: 1 - lax.axis_index(axis) for axis in axes}


def meet(partners):
    barrier = pltpu.get_barrier_semaphore()
    for axes in partners:
        pl.semaphore_signal(
            barrier, inc=1, device_id=other_of(axes), device_id_type=pl.DeviceIdType.MESH
        )
    pl.semaphore_wait(barrier, len(partners))


class Sender:
    def __init__(self, send_sems, recv_sems):
        self.send_sems, self.recv_sems, self.all, self.left = send_sems, recv_sems, [], []

    def start(self, source, target, axes):
        copy = pltpu.make_async_remote_copy(
            src_ref=source,
            dst_ref=target,
            send_sem=self.send_sems.at[len(self.all)],
            recv_sem=self.recv_sems.at[len(self.all)],
            device_id=other_of(axes),
            device_id_type=pl.DeviceIdType.MESH,
        )
        copy.start()
        self.all.append(copy)
        return copy

    def finish(self):
        for copy in self.all:
            if all(copy is not other for other in self.left):
                copy.wait_send()


def first_kernel(
    squares,
    pair,
    spread,
    small_ref,
    gains_ref,
    q_ref,
    kv_ref,
    gate_ref,
    up_ref,
    down_ref,
    small_out,
    gains_out,
    q_out,
    kv_out,
    gate_out,
    gate_over,
    gate_last,
    up_out,
    down_out,
    staged,
    send_sems,
    recv_sems,
):
    core = lax.axis_index("c")
    places = [place_of(*square) for square in squares]
    me = place_of(*pair)
    sender = Sender(send_sems, recv_sems)
    cols = staged.shape[3]

    small_out[(*places, core)] = small_ref[...]
    gains_out[(*places, core)] = gains_ref[...]
    q_out[tuple(places)] = q_ref[...]
    kv_out[tuple(places)] = kv_ref[...]
    partners = [axes for one, two in squares for axes in ((two,), (one,), (one, two))]
    meet(partners + [pair, ("c",)])

    def blocks(ref, stage, place, tail, lead=()):
        index = lead + (slice(None),) * (stage - len(lead)) + (place,) + tuple(places[stage + 1 :])
        return ref.at[index + tail]

    early = [(small_out, (core,)), (gains_out, (core,))]
    later = [(q_out, ()), (kv_out, ())]

    def send_first(ref, tail):
        mine = blocks(ref, 0, places[0], tail)
        return [sender.start(mine, mine, axes) for axes in partners[:3]]

    def send_square(ref, tail, stage):
        one, two = squares[stage]
        mine = blocks(ref, stage, places[stage], tail)
        return [sender.start(mine, mine, (two,)), sender.start(mine, mine, (one,))]

    def pass_on(ref, tail, stage, copies):
        one, two = squares[stage]
        copies[0].wait_recv()
        half = blocks(ref, stage, places[stage] ^ 1, tail, (slice(0, 2),))
        first = sender.start(half, half, (one,))
        copies[1].wait_recv()
        half = blocks(ref, stage, places[stage] ^ 2, tail, (slice(2, 4),))
        return [first, sender.start(half, half, (two,))]

    def wait(copies):
        for copy in copies:
            copy.wait_recv()

    targets = (gate_out, up_out, down_out)

    def send_columns(away, axes):
        return [
            sender.start(staged.at[which, me ^ away], target.at[me], axes)
            for which, target in enumerate(targets)
        ]

    first = [send_first(*item) for item in early]
    for which, weight_ref in enumerate((gate_ref, up_ref, down_ref)):
        for quarter in range(4):
            staged[which, quarter] = weight_ref[:, quarter * cols : (quarter + 1) * cols]
    columns = [send_columns(1, (pair[1],))]
    for which, target in enumerate(targets):
        target[me] = staged[which, me]
    for copies in first:
        wait(copies)
    sent = [send_square(*item, 1) for item in early]
    first_later = [send_first(*item) for item in later]
    columns.append(send_columns(2, (pair[0],)))
    for stage in range(1, len(squares)):
        if stage > 1:
            sent = [send_square(*item, stage) for item in early]
        passed = [pass_on(*item, stage, copies) for item, copies in zip(early, sent)]
        if stage == 1:
            for copies in first_later:
                wait(copies)
            sent_later = [send_square(*item, 1) for item in later]
            columns.append(send_columns(3, pair))
        for copies in passed:
            wait(copies)
    mine = (slice(None),) * len(squares) + (core,)
    core_sent = [sender.start(ref.at[mine], ref.at[mine], ("c",)) for ref, _ in early]
    for copies in columns:
        copies[0].wait_recv()
    over = [
        sender.start(gate_out, gate_over, (spread[0],)),
        sender.start(gate_out, gate_last, (spread[1],)),
    ]
    for stage in range(1, len(squares)):
        if stage > 1:
            sent_later = [send_square(*item, stage) for item in later]
        passed = [pass_on(*item, stage, copies) for item, copies in zip(later, sent_later)]
        for copies in passed:
            wait(copies)
    wait(core_sent)
    for copies in columns:
        wait(copies[1:])
    wait(over)
    sender.finish()


def first_gather(squares, pair, spread, small, gains, q_up, kv_up, gate, up, down):
    vmem = pl.BlockSpec(memory_space=pltpu.VMEM)
    rows, cols = gate.shape
    lead = (4,) * len(squares)
    copies = 12 + 16 * (len(squares) - 1) + 2 + 9 + 2
    return pl.pallas_call(
        functools.partial(first_kernel, squares, pair, spread),
        out_shape=(
            jax.ShapeDtypeStruct(lead + (2,) + small.shape, bf16),
            jax.ShapeDtypeStruct(lead + (2,) + gains.shape, bf16),
            jax.ShapeDtypeStruct(lead + q_up.shape, bf16),
            jax.ShapeDtypeStruct(lead + kv_up.shape, bf16),
        )
        + (jax.ShapeDtypeStruct((4, rows, cols // 4), bf16),) * 5,
        in_specs=[vmem] * 7,
        out_specs=(vmem,) * 9,
        scratch_shapes=[
            pltpu.VMEM((3, 4, rows, cols // 4), bf16),
            pltpu.SemaphoreType.DMA((copies,)),
            pltpu.SemaphoreType.DMA((copies,)),
        ],
        compiler_params=pltpu.CompilerParams(
            collective_id=0, has_side_effects=True, vmem_limit_bytes=48 << 20
        ),
    )(small, gains, q_up, kv_up, gate, up, down)


def second_kernel(
    squares,
    pair,
    over,
    rows_ref,
    value_ref,
    piece_ref,
    rows_out,
    tokens_out,
    piece_out,
    send_sems,
    recv_sems,
):
    core = lax.axis_index("c")
    places = [place_of(*square) for square in squares]
    me = place_of(*pair)
    one, two = pair
    half = value_ref.shape[0] // 2
    sender = Sender(send_sems, recv_sems)
    rows_out[tuple(places)] = rows_ref[...]
    tokens_out[me, core] = value_ref[...]
    partners = [axes for one_, two_ in squares for axes in ((two_,), (one_,), (one_, two_))]
    meet(partners + [("c",)])

    def blocks(stage, place, lead=()):
        index = lead + (slice(None),) * (stage - len(lead)) + (place,) + tuple(places[stage + 1 :])
        return rows_out.at[index]

    def send_rows(place, axes, rows=slice(None)):
        mine = tokens_out.at[place, core, rows]
        return sender.start(mine, mine, axes)

    mine = blocks(0, places[0])
    first = [sender.start(mine, mine, axes) for axes in partners[:3]]
    near = send_rows(me, (two,))
    wide = send_rows(me, (one,))
    got = [send_rows(me, ("c",))]
    for copy in first:
        copy.wait_recv()
    crossing = sender.start(piece_ref, piece_out, (over,))
    for stage in range(1, len(squares)):
        up, across = squares[stage]
        mine = blocks(stage, places[stage])
        beside = sender.start(mine, mine, (across,))
        above = sender.start(mine, mine, (up,))
        if stage == 1:
            near.wait_recv()
            corner = [send_rows(me ^ 1, (one,), slice(0, half))]
            got.append(send_rows(me ^ 1, ("c",)))
            wide.wait_recv()
            corner.append(send_rows(me ^ 2, (two,), slice(half, 2 * half)))
            got.append(send_rows(me ^ 2, ("c",)))
        beside.wait_recv()
        part = blocks(stage, places[stage] ^ 1, (slice(0, 2),))
        passed = [sender.start(part, part, (up,))]
        above.wait_recv()
        part = blocks(stage, places[stage] ^ 2, (slice(2, 4),))
        passed.append(sender.start(part, part, (across,)))
        if stage == 1:
            for copy in corner:
                copy.wait_recv()
            got.append(send_rows(me ^ 3, ("c",)))
        for copy in passed:
            copy.wait_recv()
    for copy in got:
        copy.wait_recv()
    crossing.wait_recv()
    sender.finish()


def second_gather(squares, pair, over, rows, value, piece):
    vmem = pl.BlockSpec(memory_space=pltpu.VMEM)
    copies = 3 + 4 * (len(squares) - 1) + 9
    gathered, tokens, crossed = pl.pallas_call(
        functools.partial(second_kernel, squares, pair, over),
        out_shape=(
            jax.ShapeDtypeStruct((4,) * len(squares) + rows.shape, bf16),
            jax.ShapeDtypeStruct((4, 2) + value.shape, bf16),
            jax.ShapeDtypeStruct(piece.shape, bf16),
        ),
        in_specs=[vmem] * 3,
        out_specs=(vmem,) * 3,
        scratch_shapes=[pltpu.SemaphoreType.DMA((copies,)), pltpu.SemaphoreType.DMA((copies,))],
        compiler_params=pltpu.CompilerParams(
            collective_id=4, has_side_effects=True, vmem_limit_bytes=40 << 20
        ),
        cost_estimate=pl.CostEstimate(flops=1, transcendentals=0, bytes_accessed=1),
    )(rows, value, piece)
    return gathered.reshape(-1, rows.shape[1]), tokens.reshape(-1, value.shape[1]), crossed


def lay_copies(fsdp, pair, spread, pieces, target, sems):
    copies = []
    for number, piece in enumerate(pieces):
        for block in range(4):
            place = 0
            for axis in fsdp:
                if axis == pair[0]:
                    bit = block >> 1
                elif axis == pair[1]:
                    bit = block & 1
                else:
                    bit = lax.axis_index(axis) ^ ((number >> spread.index(axis)) & 1)
                place = place * 2 + bit
            copies.append(pltpu.make_async_copy(piece.at[block], target.at[place], sems.at[len(copies)]))
    for copy in copies:
        copy.start()
    return copies


def lay_kernel(fsdp, pair, spread, *refs):
    count = 2 ** len(spread)
    target, sems = refs[count:]
    for copy in lay_copies(fsdp, pair, spread, refs[:count], target, sems):
        copy.wait()


def lay(pieces, fsdp, pair, spread):
    rows, cols = pieces[0].shape[1:]
    blocks = 4 * len(pieces)
    out = pl.pallas_call(
        functools.partial(lay_kernel, fsdp, pair, spread),
        out_shape=jax.ShapeDtypeStruct((blocks, rows, cols), bf16),
        in_specs=[pl.BlockSpec(memory_space=pltpu.HBM)] * len(pieces),
        out_specs=pl.BlockSpec(memory_space=pltpu.VMEM),
        scratch_shapes=[pltpu.SemaphoreType.DMA((blocks,))],
        compiler_params=pltpu.CompilerParams(vmem_limit_bytes=32 << 20),
        cost_estimate=pl.CostEstimate(
            flops=0, transcendentals=0, bytes_accessed=4 * blocks * rows * cols
        ),
    )(*pieces)
    return out.reshape(blocks * rows, cols)


def tokens_kernel(pair, value_ref, out_ref, send_sems, recv_sems):
    core = lax.axis_index("c")
    me = place_of(*pair)
    one, two = pair
    half = value_ref.shape[0] // 2
    sender = Sender(send_sems, recv_sems)
    out_ref[me, core] = value_ref[...]
    meet([(two,), (one,), ("c",)])

    def send(place, axes, rows=slice(None)):
        mine = out_ref.at[place, core, rows]
        return sender.start(mine, mine, axes)

    near = send(me, (two,))
    wide = send(me, (one,))
    got = [send(me, ("c",))]
    near.wait_recv()
    far = [send(me ^ 1, (one,), slice(0, half))]
    got.append(send(me ^ 1, ("c",)))
    wide.wait_recv()
    far.append(send(me ^ 2, (two,), slice(half, 2 * half)))
    got.append(send(me ^ 2, ("c",)))
    for copy in far:
        copy.wait_recv()
    got.append(send(me ^ 3, ("c",)))
    for copy in got:
        copy.wait_recv()
    sender.finish()


def tokens_of_chips(value, pair, number):
    rows, cols = value.shape
    vmem = pl.BlockSpec(memory_space=pltpu.VMEM)
    out = pl.pallas_call(
        functools.partial(tokens_kernel, pair),
        out_shape=jax.ShapeDtypeStruct((4, 2, rows, cols), bf16),
        in_specs=[vmem],
        out_specs=vmem,
        scratch_shapes=[pltpu.SemaphoreType.DMA((8,)), pltpu.SemaphoreType.DMA((8,))],
        compiler_params=pltpu.CompilerParams(
            collective_id=number, has_side_effects=True, vmem_limit_bytes=24 << 20
        ),
        cost_estimate=pl.CostEstimate(flops=1, transcendentals=0, bytes_accessed=1),
    )(value)
    return out.reshape(8 * rows, cols)


def merge_kernel(which, parts_ref, out_ref):
    cols = out_ref.shape[1] // 4
    for quarter in range(4):
        out_ref[:, quarter * cols : (quarter + 1) * cols] = parts_ref[0, quarter].astype(f32)


def merge(parts, which):
    rows, cols = parts.shape[2:]
    return pl.pallas_call(
        functools.partial(merge_kernel, which),
        grid=(1,),
        out_shape=jax.ShapeDtypeStruct((rows, 4 * cols), f32),
        in_specs=[pl.BlockSpec((1, 4, rows, cols), lambda i: (which, 0, 0, 0))],
        out_specs=pl.BlockSpec((rows, 4 * cols), lambda i: (0, 0)),
        cost_estimate=pl.CostEstimate(
            flops=0, transcendentals=0, bytes_accessed=24 * rows * cols
        ),
    )(parts)


class Reduction:
    def __init__(self, sender, held, dims, order, buffers, out):
        self.sender, self.held, self.dims, self.order = sender, held, list(dims), list(order)
        self.buffers, self.out = list(buffers), out

    def half(self, at):
        return (slice(None),) * self.dims.index(self.order[0]) + (at,)

    def begin(self):
        axis = self.order[0]
        source = self.held.at[self.half(1 - lax.axis_index(axis))]
        self.copy = self.sender.start(source, self.buffers[0], (axis,))

    def end(self):
        self.copy.wait_recv()
        axis = self.order[0]
        own = self.held[self.half(lax.axis_index(axis))]
        total = own.astype(f32) + self.buffers[0][...].astype(f32)
        self.held = self.buffers.pop(0)
        self.dims.remove(axis)
        self.order.pop(0)
        if self.order:
            self.held[...] = total.astype(bf16)
            self.begin()
        else:
            self.out[...] = total

    def finish(self):
        while self.order:
            self.end()


def halves_of(rows):
    half = rows // 2 // 16 * 16
    return pl.ds(0, half), pl.ds(half, rows - half)


def last_kernel(
    fsdp,
    pair,
    peak_ref,
    small_ref,
    gains_ref,
    q_ref,
    kv_ref,
    out_ref,
    down_ref,
    gate_ref,
    gate_got,
    up_refs,
    small_sum,
    gains_sum,
    q_sum,
    kv_sum,
    out_sum,
    ffn_out,
    peak_out,
    *scratch,
):
    scratch = list(scratch)
    stages = len(fsdp)
    sender = Sender(scratch.pop(), scratch.pop())

    def buffers(count):
        taken = scratch[:count]
        del scratch[:count]
        return taken

    down = list(reversed(fsdp))
    turned = [down[1], down[0]] + down[2:]
    with_core = fsdp + ["c"]
    small = Reduction(sender, small_ref, with_core, ["c"] + turned, buffers(stages + 1), small_sum)
    gains = Reduction(sender, gains_ref, with_core, ["c"] + down, buffers(stages + 1), gains_sum)
    q = Reduction(sender, q_ref, fsdp, down, buffers(stages), q_sum)
    kv = Reduction(sender, kv_ref, fsdp, turned, buffers(stages), kv_sum)
    upward = [down[-2]] + turned[:-2] + [down[-1]]
    outs = []
    for rows, order in zip(halves_of(out_sum.shape[0]), (turned, upward)):
        part = out_ref.at[(slice(None),) * stages + (rows,)]
        outs.append(Reduction(sender, part, fsdp, order, buffers(stages), out_sum.at[rows]))
    over = buffers(2)
    gate_sum, up_sum = buffers(2)
    peaks = buffers(stages)
    me = place_of(*pair)
    row = lax.axis_index(fsdp[0])
    meet([(axis,) for axis in with_core] + [pair])

    def send_columns(which, held):
        ffn_out[which, me] = held[me]
        return [
            sender.start(held.at[me ^ away], ffn_out.at[which, me], axes)
            for away, axes in ((1, (pair[1],)), (2, (pair[0],)), (3, pair))
        ]

    peak_out[...] = peak_ref[...]

    def send_peaks(stage):
        return sender.start(peak_out, peaks[stage], (fsdp[stage],))

    def next_peaks(stage, sent):
        sent.wait()
        sender.left.append(sent)
        peak_out[...] = jnp.maximum(peak_out[...], peaks[stage][...])
        return send_peaks(stage + 1) if stage < stages - 1 else None

    for part in (small, gains, q, outs[0], kv):
        part.begin()
    peak_sent = send_peaks(0)
    crossing = sender.start(down_ref.at[1 - row], over[0], (fsdp[0],))
    outs[1].begin()
    gate_sum[...] = (gate_ref[...].astype(f32) + gate_got[...].astype(f32)).astype(bf16)
    columns = send_columns(1, gate_sum)
    small.end()
    gains.end()
    up_sum[...] = sum(ref[...].astype(f32) for ref in up_refs).astype(bf16)
    peak_sent = next_peaks(0, peak_sent)
    for part in (q, kv, outs[0]):
        part.end()
    def crossed(which, ref, buffer):
        crossing.wait_recv()
        buffer[...] = (ref[row].astype(f32) + buffer[...].astype(f32)).astype(bf16)
        return send_columns(which, buffer)

    columns += crossed(0, down_ref, over[0])
    crossing = sender.start(up_sum.at[1 - row], over[1], (fsdp[0],))
    for stage in range(1, stages):
        peak_sent = next_peaks(stage, peak_sent)
        for part in (outs[1], small, gains, q, kv, outs[0]):
            part.end()
        if stage == 1:
            columns += crossed(2, up_sum, over[1])
    for reduction in (q, kv, outs[0], small, gains, outs[1]):
        reduction.finish()
    for copy in columns:
        copy.wait_recv()
    sender.finish()


def last_scatter(fsdp, pair, peak, small, gains, q, kv, out, down, gate, up):
    vmem = pl.BlockSpec(memory_space=pltpu.VMEM)
    stages = len(fsdp)

    def buffers(array, count, rows=None):
        lead = array.ndim - 2
        block = (rows or array.shape[-2], array.shape[-1])
        return [pltpu.VMEM((2,) * (lead - 1 - i) + block, bf16) for i in range(count)]

    scratch = (
        buffers(small, stages + 1)
        + buffers(gains, stages + 1)
        + buffers(q, stages)
        + buffers(kv, stages)
        + [buf for rows in halves_of(out.shape[-2]) for buf in buffers(out, stages, rows.size)]
        + [pltpu.VMEM(gate[0].shape, bf16)] * 3
        + [pltpu.VMEM(down.shape, bf16)]
        + [pltpu.VMEM(peak.shape, f32)] * stages
    )
    copies = 2 * (stages + 1) + 4 * stages + 2 + 9 + stages
    return pl.pallas_call(
        lambda *refs: last_kernel(fsdp, pair, *refs[:9], refs[9 : 9 + len(up)], *refs[9 + len(up) :]),
        out_shape=tuple(jax.ShapeDtypeStruct(x.shape[-2:], f32) for x in (small, gains, q, kv, out))
        + (
            jax.ShapeDtypeStruct((3,) + gate[0].shape, bf16),
            jax.ShapeDtypeStruct(peak.shape, f32),
        ),
        in_specs=[vmem] * (9 + len(up)),
        out_specs=(vmem,) * 7,
        scratch_shapes=scratch
        + [pltpu.SemaphoreType.DMA((copies,)), pltpu.SemaphoreType.DMA((copies,))],
        compiler_params=pltpu.CompilerParams(
            collective_id=2, has_side_effects=True, vmem_limit_bytes=60 << 20
        ),
    )(peak, small, gains, q, kv, out, down, *gate, *up)


def shards(
    fsdp,
    hidden_in,
    seq_ids,
    block_ids,
    clip_limit,
    cotangent,
    q_down,
    kv_down,
    q_up,
    kv_up,
    out_proj,
    gate_proj,
    up_proj,
    down_proj,
    in_gain,
    q_gain,
    kv_gain,
    post_gain,
):
    tokens_here, width = hidden_in.shape
    seq_row = seq_ids[0]
    block_row = block_ids[0]
    group = seq_row.shape[0]
    heads = q_up.shape[1] // (NOPE + ROPE)
    score_scale = 1.0 / math.sqrt(NOPE + ROPE)
    core = lax.axis_index("c")
    first_row = core * tokens_here
    wide, near = fsdp[1], fsdp[-1]
    pair = (wide, near)
    spread = [axis for axis in fsdp if axis not in pair]
    squares = [(fsdp[i], fsdp[i + 1]) for i in range(0, len(fsdp), 2)]
    at_wide, at_near = lax.axis_index(wide), lax.axis_index(near)
    chips = tuple(fsdp)
    count = 2 ** len(fsdp)

    small_rows = q_down.shape[0]
    q_rank = q_down.shape[1]
    small_cols = q_rank + kv_down.shape[1]

    def row(value):
        return jnp.pad(value, ((0, 0), (0, TILE - value.shape[1])))[:, None, :]

    def rows_of(*values):
        held = jnp.concatenate([row(value) for value in values], axis=1)
        return jnp.pad(held, ((0, 0), (0, 8 - len(values)), (0, 0)))

    small = jnp.concatenate([q_down, kv_down], axis=1)
    gains = rows_of(in_gain[None], post_gain[None], q_gain[None], kv_gain[None])[0]
    q_up_wide = jnp.pad(
        q_up.reshape(-1, heads, NOPE + ROPE), ((0, 0), (0, 0), (0, TILE - NOPE - ROPE))
    ).reshape(-1, heads * TILE)
    small_all, gains_all, q_up_all, kv_up_all, *pieces = first_gather(
        squares, pair, spread, small, gains, q_up_wide, kv_up, gate_proj, up_proj, down_proj
    )
    down_full = small_all.reshape(-1, small_cols)
    q_up_full = q_up_all.reshape(-1, heads * TILE)
    kv_up_full = kv_up_all.reshape(-1, kv_up.shape[1])
    devices = 2 * count

    def gain(at, size):
        return gains_all.reshape(devices, 8, TILE)[:, at, :size].reshape(-1).astype(f32)

    in_float = gain(0, in_gain.shape[0])
    post_float = gain(1, post_gain.shape[0])
    q_gain_float = gain(2, q_gain.shape[0])
    kv_gain_float = gain(3, kv_gain.shape[0])

    cot_float = cotangent.astype(f32)

    def over(pieces, axis, *ready):
        return [swap(after(piece, *ready), axis) for piece in pieces]

    def exchange(held, dims, axis):
        at, dim = lax.axis_index(axis), dims.index(axis)
        return swap(pick(held, 1 - at, dim), axis), pick(held, at, dim)

    def sum_of_chips(held):
        held = held.reshape(2, 2, tokens_here, width)
        return square_scatter(held, wide, near, 0).reshape(tokens_here, width)

    def core_both(value):
        return both(value, swap(value, "c"), "c", 0)

    def core_sum(value):
        def rows(at):
            return lax.dynamic_slice_in_dim(value, at * tokens_here, tokens_here)

        return rows(core) + swap(rows(1 - core), "c")

    x_float = hidden_in.astype(f32)
    x_normed = rms_scale(x_float, in_float).astype(bf16)
    pre = jnp.dot(x_normed, down_full, preferred_element_type=f32)
    q_pre = pre[:, :q_rank]
    c_lat_pre = pre[:, q_rank : q_rank + KVR]
    c_rot_pre = pre[:, q_rank + KVR :]
    own_cos, own_sin = angles(seq_row, first_row, tokens_here)
    q_latent = rms_scale(q_pre, q_gain_float).astype(bf16)
    kv_latent = rms_scale(c_lat_pre, kv_gain_float).astype(bf16)
    key_rot = rotate(c_rot_pre, own_cos, own_sin).astype(bf16)
    key_rot = jnp.pad(key_rot, ((0, 0), (NOPE, TILE - NOPE - ROPE)))
    latents = core_both(jnp.concatenate([q_latent, kv_latent, key_rot], axis=1))
    q_lat_all = latents[:, :q_rank]
    kv_lat_all = latents[:, q_rank : q_rank + KVR]
    key_rot_all = latents[:, q_rank + KVR :]
    all_cos, all_sin = angles(seq_row, 0, group)
    q_full = jnp.dot(q_lat_all, q_up_full, preferred_element_type=f32)
    kv_full = jnp.dot(kv_lat_all, kv_up_full, preferred_element_type=f32).astype(bf16)
    allowed = (seq_row[None, :] == seq_row[:, None]) & (block_row[:, None] <= block_row[None, :])
    bias = jnp.where(allowed, 0.0, -1e30).astype(f32)
    axes = list(spread)
    gate_held, gate_over, gate_last, up_held, down_held = pieces
    gate_pieces = [gate_held, gate_over, gate_last, swap(gate_over, axes[1])]
    for axis in axes[2:]:
        gate_pieces += over(gate_pieces, axis)
    up_pieces = [swap(up_held, axes[0]), swap(up_held, axes[1])]
    attn, queries, log_total, local_peak = attend(
        q_full, kv_full, key_rot_all, tables(all_cos, all_sin), bias, score_scale
    )
    d_ffn = (resid_scale * cot_float).astype(bf16)
    out_full, d_ffn_all, down_over = second_gather(
        squares, pair, axes[0], after(out_proj, attn), d_ffn, down_held
    )
    attn, out_full, down_over, *early = lax.optimization_barrier(
        (attn, out_full, down_over, *up_pieces, *gate_pieces)
    )
    up_pieces, gate_pieces = early[:2], early[2:]
    branch = core_sum(contract(attn, out_full, 1, 1))
    mid = x_float + resid_scale * branch
    mid_normed = rms_scale(mid, post_float).astype(bf16)
    gate_full = lay(gate_pieces, fsdp, pair, spread)
    mid_all = tokens_of_chips(after(mid_normed, gate_full), pair, 1)
    up_pieces = [up_held, *up_pieces, swap(after(up_pieces[0], attn), axes[1])]
    down_last = swap(after(down_held, attn), axes[1])
    mid_all, down_last, *up_pieces = lax.optimization_barrier((mid_all, down_last, *up_pieces))
    down_pieces = [down_held, down_over, down_last, swap(after(down_over, mid_all), axes[1])]
    for axis in axes[2:]:
        up_pieces += over(up_pieces, axis)
        down_pieces += over(down_pieces, axis)
    up_full = lay(up_pieces, fsdp, pair, spread)
    gate = jnp.dot(mid_all, gate_full, preferred_element_type=f32)
    up_value = jnp.dot(mid_all, up_full, preferred_element_type=f32)
    down_proj_full = lay(down_pieces, fsdp, pair, spread)
    sigmoid = jax.nn.sigmoid(gate)
    silu_value = gate * sigmoid
    act = (silu_value * up_value).astype(bf16)

    d_act = jnp.dot(d_ffn_all, down_proj_full, preferred_element_type=f32)
    d_gate = (d_act * up_value * (sigmoid * (1.0 + gate * (1.0 - sigmoid)))).astype(bf16)
    d_up = (d_act * silu_value).astype(bf16)
    dims = list(fsdp)
    first, last = spread[0], spread[-1]

    def added(parts):
        return (parts[0].astype(f32) + parts[1].astype(f32)).astype(bf16)

    def inner(held):
        left = [axis for axis in dims if axis != last]
        for axis in reversed(spread[1:-1]):
            held = added(exchange(held, left, axis))
            left.remove(axis)
        return held

    def begin(left, right, *ready):
        keep, send = grad_halves(left, right, width // count, last)
        shape = [2] * (len(fsdp) - 1) + [width // count, -1]
        return swap(after(send, *ready), last).reshape(shape), keep.reshape(shape), keep

    def cross(held):
        return exchange(held, [first, *pair], first)

    *down_parts, down_grad = begin(d_ffn_all, act)
    d_gate_late, _ = lax.optimization_barrier((d_gate, down_grad))
    gate_keep, gate_send = grad_halves(mid_all, d_gate_late, width // count, last)
    d_up_late, d_gate_late, _ = lax.optimization_barrier((d_up, d_gate, gate_keep))
    d_mid_held = core_features(
        tokens_here, 3, (d_gate_late, gate_full), (d_up_late, up_full)
    )
    d_mid_held, *down_parts = lax.optimization_barrier((d_mid_held, *down_parts))
    d_mid_normed = sum_of_chips(d_mid_held)
    mid_late, gate_send, _ = lax.optimization_barrier((mid_all, gate_send, d_mid_held))
    shape = [2] * (len(fsdp) - 1) + [width // count, -1]
    gate_parts = (swap(gate_send, last).reshape(shape), gate_keep.reshape(shape))
    down_held = inner(added(down_parts))
    *up_parts, up_grad = begin(mid_late, d_up, gate_parts[0])
    ffn_part = features((after(act, up_grad), down_proj_full))
    post_pull = jax.vjp(rms_scale, mid, post_float)[1]
    d_mid_normed, *early = lax.optimization_barrier(
        (d_mid_normed, down_held, *gate_parts, ffn_part)
    )
    down_held, gate_parts, ffn_part = early[0], early[1:3], early[3]
    d_mid_norm, post_grad = post_pull(d_mid_normed)
    ffn = lax.psum_scatter(
        after(ffn_part, d_mid_norm), (wide, near, "c"), scatter_dimension=0, tiled=True
    )
    layer_out = (mid + resid_scale * ffn.astype(f32)).astype(bf16)
    d_mid = cot_float + d_mid_norm
    d_branch = (resid_scale * d_mid).astype(bf16)
    d_branch_all = core_both(d_branch)
    d_attn = jnp.dot(d_branch_all, out_full, preferred_element_type=f32).astype(bf16)
    gate_parts = cross(inner(added(gate_parts)))
    d_q, d_kv, d_rot_part = attend_back(
        queries,
        kv_full,
        d_attn,
        log_total,
        key_rot_all,
        tables(all_cos, -all_sin),
        bias,
        score_scale,
    )
    q_up_grad = heads_grad(q_lat_all, d_q)
    out_grad = plain_grad(after(d_branch_all, q_up_grad), attn)
    d_q_lat_part = contract(d_q, q_up_full, 1, 1)
    d_kv_lat_part = contract(d_kv, kv_up_full, 1, 1)
    d_q_lat_part, d_kv_lat_part, d_kv, out_grad, *early = lax.optimization_barrier(
        (d_q_lat_part, d_kv_lat_part, d_kv, out_grad, *gate_parts, *up_parts)
    )
    gate_parts, up_parts = early[:2], early[2:]
    kv_up_grad = rows_first(contract(kv_lat_all, d_kv, 0, 0).astype(bf16))
    d_latents = core_sum(jnp.concatenate([d_q_lat_part, d_kv_lat_part, d_rot_part], axis=1))
    q_pull = jax.vjp(rms_scale, q_pre, q_gain_float)[1]
    d_q_pre, q_gain_grad = q_pull(d_latents[:, :q_rank])
    kv_pull = jax.vjp(rms_scale, c_lat_pre, kv_gain_float)[1]
    d_c_lat, kv_gain_grad = kv_pull(d_latents[:, q_rank : q_rank + KVR])
    d_key_rot = d_latents[:, q_rank + KVR + NOPE : q_rank + KVR + NOPE + ROPE]
    d_pre = jnp.concatenate(
        [d_q_pre, d_c_lat, rotate(d_key_rot, own_cos, -own_sin)], axis=-1
    ).astype(bf16)
    down_grads = rows_first(contract(x_normed, d_pre, 0, 0).astype(bf16))
    d_x_normed = contract(d_pre, down_full, 1, 1)
    in_pull = jax.vjp(rms_scale, x_float, in_float)[1]
    d_x_norm, in_grad = in_pull(d_x_normed)
    input_grad = d_mid + d_x_norm

    rows_here = width // count
    block = (4, rows_here, gate_parts[0].shape[-1])
    if len(spread) > 2:
        up_parts = (inner(added(up_parts)),)
    ffn_held = [
        down_held.reshape((2,) + block),
        tuple(part.reshape(block) for part in gate_parts),
        tuple(part.reshape((2,) + block) for part in up_parts),
    ]
    gain_grads = rows_of(
        *(grad.reshape(devices, -1) for grad in (in_grad, post_grad, q_gain_grad, kv_gain_grad))
    ).astype(bf16)

    def blocks(grad, lead):
        return grad.reshape([2] * lead + [grad.shape[0] // 2**lead, -1])

    small_out, gain_out, q_up_out, kv_up_out, out_out, ffn_cols, peak_all = last_scatter(
        fsdp,
        pair,
        local_peak,
        blocks(down_grads, len(fsdp) + 1),
        gain_grads.reshape([2] * (len(fsdp) + 1) + [8, TILE]),
        blocks(q_up_grad, len(fsdp)),
        blocks(kv_up_grad, len(fsdp)),
        blocks(out_grad, len(fsdp)),
        *ffn_held,
    )
    down_out, gate_out, up_out = (merge(ffn_cols, which) for which in range(3))
    peaks = peak_all[0, :heads]
    limit = clip_limit[0]
    factors = limit / jnp.maximum(peaks, limit)
    root = jnp.sqrt(factors)
    q_cols = jnp.concatenate(
        [
            jnp.broadcast_to(root[:, None], (heads, NOPE)),
            jnp.broadcast_to(factors[:, None], (heads, ROPE)),
        ],
        axis=1,
    ).reshape(heads * (NOPE + ROPE))
    kv_cols = jnp.concatenate(
        [jnp.broadcast_to(root[:, None], (heads, NOPE)), jnp.ones((heads, VD), f32)], axis=1
    ).reshape(heads * (NOPE + VD))
    q_clipped = (q_up.astype(f32) * q_cols[None, :]).astype(bf16)
    kv_clipped = (kv_up.astype(f32) * kv_cols[None, :]).astype(bf16)
    return (
        layer_out,
        input_grad,
        small_out[:, :q_rank],
        small_out[:, q_rank:],
        q_up_out,
        kv_up_out,
        out_out,
        gate_out,
        up_out,
        down_out,
        gain_out[0, : in_gain.shape[0]],
        gain_out[2, : q_gain.shape[0]],
        gain_out[3, : kv_gain.shape[0]],
        gain_out[1, : post_gain.shape[0]],
        q_clipped,
        kv_clipped,
        peaks,
        factors,
    )


def solution(mesh):
    bits = mesh.shape["fsdp"].bit_length() - 1
    fsdp = [f"f{i}" for i in range(bits)]
    fine = Mesh(mesh.devices.reshape((2,) * (bits + 1)), tuple(fsdp) + ("c",))
    split = tuple(fsdp)
    whole = split + ("c",)
    return jax.shard_map(
        functools.partial(shards, fsdp),
        mesh=fine,
        in_specs=(
            P(whole, None),
            P(split, None),
            P(split, None),
            P(),
            P(whole, None),
            P(whole, None),
            P(whole, None),
            P(split, "c"),
            P(split, "c"),
            P(split, "c"),
            P(split, "c"),
            P(split, "c"),
            P(split, "c"),
            P(whole),
            P(whole),
            P(whole),
            P(whole),
        ),
        out_specs=(
            P(whole, None),
            P(whole, None),
            P(whole, None),
            P(whole, None),
            P(split, "c"),
            P(split, "c"),
            P(split, "c"),
            P(split, "c"),
            P(split, "c"),
            P(split, "c"),
            P(whole),
            P(whole),
            P(whole),
            P(whole),
            P(split, "c"),
            P(split, "c"),
            P("c"),
            P("c"),
        ),
        check_vma=False,
    )
```

```python
import functools
import math

import jax
import jax.numpy as jnp
from jax import lax
from jax.experimental import pallas as pl
from jax.experimental.pallas import tpu as pltpu
from jax.experimental.layout import Layout, with_layout_constraint
from jax.sharding import Mesh
from jax.sharding import PartitionSpec as P

NOPE = 64
ROPE = 32
VD = 64
KVR = 256
TILE = 128


eps = 1e-05
resid_scale = 1.4 / math.sqrt(62.0)
rope_base = 10000.0
SWAP = [(0, 1), (1, 0)]
f32 = jnp.float32
bf16 = jnp.bfloat16


def rms_scale(value, gain):
    return value * lax.rsqrt(jnp.mean(value * value, axis=-1, keepdims=True) + eps) * gain


def rotate(value, cosine, sine):
    half = value.shape[-1] // 2
    first = value[..., :half]
    second = value[..., half:]
    return jnp.concatenate(
        [first * cosine - second * sine, second * cosine + first * sine], axis=-1
    )


def angles(seq_row, start, count):
    own_ids = lax.dynamic_slice_in_dim(seq_row, start, count)
    earlier = jnp.sum((seq_row[None, :] < own_ids[:, None]).astype(jnp.int32), axis=1)
    place = (start + jnp.arange(count, dtype=jnp.int32) - earlier).astype(f32)
    freq = jnp.power(rope_base, -jnp.arange(ROPE // 2, dtype=f32) * (2.0 / ROPE))
    turn = place[:, None] * freq[None, :]
    return (jnp.cos(turn), jnp.sin(turn))


def contract(left, right, left_dim, right_dim):
    return lax.dot_general(
        left, right, (((left_dim,), (right_dim,)), ((), ())), preferred_element_type=f32
    )


def turn(value, plain, first, second):
    return (
        value * plain
        + pltpu.roll(value, TILE - ROPE // 2, 1) * first
        + pltpu.roll(value, ROPE // 2, 1) * second
    )


def tables(cosine, sine):
    rows = cosine.shape[0]
    half = ROPE // 2

    def zeros(count):
        return jnp.zeros((rows, count), f32)

    plain = jnp.concatenate([jnp.ones((rows, NOPE), f32), cosine, cosine, zeros(TILE - NOPE - ROPE)], axis=1)
    first = jnp.concatenate([zeros(NOPE), -sine, zeros(TILE - NOPE - half)], axis=1)
    second = jnp.concatenate([zeros(NOPE + half), sine, zeros(TILE - NOPE - ROPE)], axis=1)
    return plain, first, second


def attend_kernel(
    scale,
    q_ref,
    kv_ref,
    rot_ref,
    plain_ref,
    first_ref,
    second_ref,
    bias_ref,
    mixed_ref,
    query_ref,
    total_ref,
    peak_ref,
):
    step = pl.program_id(0)
    lane = lax.broadcasted_iota(jnp.int32, (q_ref.shape[0], TILE), 1)
    spot = lax.broadcasted_iota(jnp.int32, peak_ref.shape, 1)

    @pl.when(step == 0)
    def _():
        peak_ref[...] = jnp.zeros_like(peak_ref)

    outs = []
    for one in range(2):
        cols = slice(one * TILE, (one + 1) * TILE)
        query = turn(q_ref[:, cols], plain_ref[...], first_ref[...], second_ref[...]).astype(bf16)
        query_ref[:, cols] = query
        kv = kv_ref[:, cols]
        keys = jnp.where(lane < NOPE, kv, rot_ref[...])
        masked = contract(keys, query, 1, 1) * scale + bias_ref[...]
        top = jnp.max(masked, axis=0, keepdims=True)
        weights = jnp.exp(masked - top)
        total = jnp.sum(weights, axis=0, keepdims=True)
        chance = (weights * (1.0 / total)).astype(bf16)
        outs.append(contract(chance, kv, 0, 0))
        total_ref[0, one : one + 1, :] = top + jnp.log(total)
        peak_ref[...] = jnp.where(spot == step * 2 + one, jnp.max(top), peak_ref[...])
    mixed_ref[...] = jnp.where(lane < VD, pltpu.roll(outs[0], VD, 1), outs[1]).astype(bf16)


def attend(q, kv, rot, turns, bias, scale):
    group, cols = q.shape
    heads = cols // TILE
    whole = pl.BlockSpec((group, TILE), lambda i: (0, 0))
    two = pl.BlockSpec((group, 2 * TILE), lambda i: (0, i))
    return pl.pallas_call(
        functools.partial(attend_kernel, scale),
        grid=(heads // 2,),
        out_shape=(
            jax.ShapeDtypeStruct((group, heads * VD), bf16),
            jax.ShapeDtypeStruct((group, cols), bf16),
            jax.ShapeDtypeStruct((heads // 2, 2, group), f32),
            jax.ShapeDtypeStruct((8, TILE), f32),
        ),
        in_specs=[two, two, whole, whole, whole, whole, pl.BlockSpec((group, group), lambda i: (0, 0))],
        out_specs=(
            pl.BlockSpec((group, TILE), lambda i: (0, i)),
            two,
            pl.BlockSpec((1, 2, group), lambda i: (i, 0, 0)),
            pl.BlockSpec((8, TILE), lambda i: (0, 0)),
        ),
        compiler_params=pltpu.CompilerParams(
            dimension_semantics=("arbitrary",), vmem_limit_bytes=40 << 20
        ),
        cost_estimate=pl.CostEstimate(flops=1, transcendentals=0, bytes_accessed=1),
    )(q, kv, rot, *turns, bias)


def attend_back_kernel(
    scale,
    query_ref,
    kv_ref,
    d_mixed_ref,
    total_ref,
    rot_ref,
    plain_ref,
    first_ref,
    second_ref,
    bias_ref,
    d_q_ref,
    d_kv_ref,
    d_rot_ref,
):
    step = pl.program_id(0)
    lane = lax.broadcasted_iota(jnp.int32, (query_ref.shape[0], TILE), 1)

    @pl.when(step == 0)
    def _():
        d_rot_ref[...] = jnp.zeros_like(d_rot_ref)

    pair = d_mixed_ref[...].astype(f32)
    for one in range(2):
        cols = slice(one * TILE, (one + 1) * TILE)
        query = query_ref[:, cols]
        kv = kv_ref[:, cols]
        keys = jnp.where(lane < NOPE, kv, rot_ref[...])
        own = pair if one else pltpu.roll(pair, VD, 1)
        d_mixed = jnp.where(lane < VD, 0.0, own).astype(bf16)
        masked = contract(keys, query, 1, 1) * scale + bias_ref[...]
        chance = jnp.exp(masked - total_ref[0, one : one + 1, :])
        d_values = contract(chance.astype(bf16), d_mixed, 1, 0)
        d_chance = contract(kv, d_mixed, 1, 1)
        inner = jnp.sum(chance * d_chance, axis=0, keepdims=True)
        d_raw = (chance * (d_chance - inner) * scale).astype(bf16)
        d_keys = contract(d_raw, query, 1, 0)
        d_query = contract(d_raw, keys, 0, 0)
        d_q_ref[:, cols] = turn(
            d_query, plain_ref[...], first_ref[...], second_ref[...]
        ).astype(bf16)
        d_kv_ref[:, cols] = jnp.where(lane < NOPE, d_keys, d_values).astype(bf16)
        d_rot_ref[...] += d_keys


def attend_back(query, kv, d_mixed, total, rot, turns, bias, scale):
    group, cols = query.shape
    heads = cols // TILE
    whole = pl.BlockSpec((group, TILE), lambda i: (0, 0))
    two = pl.BlockSpec((group, 2 * TILE), lambda i: (0, i))
    return pl.pallas_call(
        functools.partial(attend_back_kernel, scale),
        grid=(heads // 2,),
        out_shape=(
            jax.ShapeDtypeStruct((group, cols), bf16),
            jax.ShapeDtypeStruct((group, cols), bf16),
            jax.ShapeDtypeStruct((group, TILE), f32),
        ),
        in_specs=[
            two,
            two,
            pl.BlockSpec((group, TILE), lambda i: (0, i)),
            pl.BlockSpec((1, 2, group), lambda i: (i, 0, 0)),
            whole,
            whole,
            whole,
            whole,
            pl.BlockSpec((group, group), lambda i: (0, 0)),
        ],
        out_specs=(two, two, whole),
        compiler_params=pltpu.CompilerParams(
            dimension_semantics=("arbitrary",), vmem_limit_bytes=40 << 20
        ),
        cost_estimate=pl.CostEstimate(flops=1, transcendentals=0, bytes_accessed=1),
    )(query, kv, d_mixed, total, rot, *turns, bias)


def swap(value, axis):
    return lax.ppermute(value, axis, SWAP)


def far(value, pair):
    return lax.ppermute(value, pair, [(i, 3 - i) for i in range(4)])


def after(value, *others):
    return lax.optimization_barrier((value,) + others)[0]


def pick(value, at, dim):
    return lax.dynamic_index_in_dim(value, at, dim, keepdims=True)


def both(own, other, axis, dim):
    here = lax.axis_index(axis) == 0
    return jnp.concatenate([jnp.where(here, own, other), jnp.where(here, other, own)], axis=dim)


def plain_grad_kernel(left_ref, right_ref, out_ref):
    out_ref[...] = contract(left_ref[...], right_ref[...], 0, 0).astype(bf16)


def plain_grad(left, right):
    rows, width = left.shape
    cols = right.shape[1]
    tile = 512
    return pl.pallas_call(
        plain_grad_kernel,
        grid=(width // tile,),
        out_shape=jax.ShapeDtypeStruct((width, cols), bf16),
        in_specs=[
            pl.BlockSpec((rows, tile), lambda i: (0, i)),
            pl.BlockSpec((rows, cols), lambda i: (0, 0)),
        ],
        out_specs=pl.BlockSpec((tile, cols), lambda i: (i, 0)),
        compiler_params=pltpu.CompilerParams(vmem_limit_bytes=32 << 20),
        cost_estimate=pl.CostEstimate(flops=1, transcendentals=0, bytes_accessed=1),
    )(left, right)


def heads_grad_kernel(latent_ref, d_ref, out_ref):
    total = contract(latent_ref[...], d_ref[...], 0, 0)
    parts = [total[:, i * TILE : i * TILE + NOPE + ROPE] for i in range(4)]
    out_ref[...] = jnp.concatenate(parts, axis=1).astype(bf16)


def heads_grad(latent, d_heads):
    group, rank = latent.shape
    packs = d_heads.shape[1] // (4 * TILE)
    cols = 4 * (NOPE + ROPE)
    return pl.pallas_call(
        heads_grad_kernel,
        grid=(packs,),
        out_shape=jax.ShapeDtypeStruct((rank, packs * cols), bf16),
        in_specs=[
            pl.BlockSpec((group, rank), lambda i: (0, 0)),
            pl.BlockSpec((group, 4 * TILE), lambda i: (0, i)),
        ],
        out_specs=pl.BlockSpec((rank, cols), lambda i: (0, i)),
        compiler_params=pltpu.CompilerParams(vmem_limit_bytes=32 << 20),
        cost_estimate=pl.CostEstimate(flops=1, transcendentals=0, bytes_accessed=1),
    )(latent, d_heads)


def features_kernel(*refs):
    out_ref = refs[-1]
    total = contract(refs[0][...], refs[1][...], 1, 1)
    for i in range(2, len(refs) - 1, 2):
        total += contract(refs[i][...], refs[i + 1][...], 1, 1)
    out_ref[...] = total.astype(bf16)


def features(*pairs):
    rows, cols = pairs[0][0].shape
    width = pairs[0][1].shape[0]
    tile = min(rows, 512)
    return pl.pallas_call(
        features_kernel,
        grid=(rows // tile,),
        out_shape=jax.ShapeDtypeStruct((rows, width), bf16),
        in_specs=[
            pl.BlockSpec((tile, cols), lambda i: (i, 0)),
            pl.BlockSpec((width, cols), lambda i: (0, 0)),
        ]
        * len(pairs),
        out_specs=pl.BlockSpec((tile, width), lambda i: (i, 0)),
        compiler_params=pltpu.CompilerParams(vmem_limit_bytes=56 << 20),
        cost_estimate=pl.CostEstimate(flops=1, transcendentals=0, bytes_accessed=1),
    )(*(array for pair in pairs for array in pair))


def core_features_kernel(*refs):
    *operands, out_ref, total, sent, got, send_sems, recv_sems = refs
    step = pl.program_id(0)
    core = lax.axis_index("c")
    half = total.shape[1]

    @pl.when(step == 0)
    def _():
        meet([("c",)])

    def copy(at):
        return pltpu.make_async_remote_copy(
            src_ref=sent.at[at],
            dst_ref=got.at[at],
            send_sem=send_sems.at[at],
            recv_sem=recv_sems.at[at],
            device_id=other_of(("c",)),
            device_id_type=pl.DeviceIdType.MESH,
        )

    value = contract(operands[0][...], operands[1][...], 1, 1)
    for i in range(2, len(operands), 2):
        value += contract(operands[i][...], operands[i + 1][...], 1, 1)
    total[0] = value[:half].astype(bf16)
    total[1] = value[half:].astype(bf16)
    sent[step] = total[1 - core]
    copy(step).start()
    out_ref[step] = total[core]

    @pl.when(step == pl.num_programs(0) - 1)
    def _():
        for at in range(out_ref.shape[0]):
            copy(at).wait()
            out_ref[at] = (out_ref[at].astype(f32) + got[at].astype(f32)).astype(bf16)


def core_features(rows, number, *pairs):
    cols = pairs[0][0].shape[1]
    width = pairs[0][1].shape[0]
    block = (4, rows, width)
    return pl.pallas_call(
        core_features_kernel,
        grid=(4,),
        out_shape=jax.ShapeDtypeStruct(block, bf16),
        in_specs=[
            pl.BlockSpec((2 * rows, cols), lambda i: (i, 0)),
            pl.BlockSpec((width, cols), lambda i: (0, 0), pipeline_mode=pl.Buffered(1)),
        ]
        * len(pairs),
        out_specs=pl.BlockSpec(block, lambda i: (0, 0, 0)),
        scratch_shapes=[
            pltpu.VMEM((2, rows, width), bf16),
            pltpu.VMEM(block, bf16),
            pltpu.VMEM(block, bf16),
            pltpu.SemaphoreType.DMA((4,)),
            pltpu.SemaphoreType.DMA((4,)),
        ],
        compiler_params=pltpu.CompilerParams(
            dimension_semantics=("arbitrary",),
            collective_id=number,
            has_side_effects=True,
            vmem_limit_bytes=58 << 20,
        ),
        cost_estimate=pl.CostEstimate(flops=1, transcendentals=0, bytes_accessed=1),
    )(*(array for pair in pairs for array in pair))


def grad_kernel(axis, left_ref, right_ref, keep_ref, send_ref, total):
    half = total.shape[1]
    value = contract(left_ref[...], right_ref[...], 0, 0).astype(bf16)
    total[0] = value[:half]
    total[1] = value[half:]
    at = lax.axis_index(axis)
    keep_ref[0] = total[at]
    send_ref[0] = total[1 - at]


def grad_halves(left, right, rows, axis):
    tokens, width = left.shape
    cols = right.shape[1]
    tile = 4 * rows
    if tile % TILE:
        held = rows_first(contract(left, right, 0, 0).astype(bf16)).reshape(-1, 2, 2 * rows, cols)
        at = lax.axis_index(axis)
        return tuple(pick(held, i, 1)[:, 0] for i in (at, 1 - at))
    out = jax.ShapeDtypeStruct((width // tile, 2 * rows, cols), bf16)
    return pl.pallas_call(
        functools.partial(grad_kernel, axis),
        grid=(width // tile,),
        out_shape=(out, out),
        in_specs=[
            pl.BlockSpec((tokens, tile), lambda i: (0, i)),
            pl.BlockSpec((tokens, cols), lambda i: (0, 0)),
        ],
        out_specs=(pl.BlockSpec((1, 2 * rows, cols), lambda i: (i, 0, 0)),) * 2,
        scratch_shapes=[pltpu.VMEM((2, 2 * rows, cols), bf16)],
        compiler_params=pltpu.CompilerParams(vmem_limit_bytes=56 << 20),
        cost_estimate=pl.CostEstimate(flops=1, transcendentals=0, bytes_accessed=1),
    )(left, right)


def rows_first(value):
    return with_layout_constraint(value, Layout(major_to_minor=(0, 1)))


def square_scatter(held, first, second, dim):
    here, there = lax.axis_index(first), lax.axis_index(second)

    def part(w, n):
        return pick(pick(held, w, dim), n, dim + 1)

    near = swap(part(here, 1 - there).astype(bf16), second)
    wide = swap(part(1 - here, there).astype(bf16), first)
    corner = far(part(1 - here, 1 - there).astype(bf16), (first, second))
    own = part(here, there).astype(f32)
    return own + near.astype(f32) + wide.astype(f32) + corner.astype(f32)


def place_of(first, second):
    return lax.axis_index(first) * 2 + lax.axis_index(second)


def other_of(axes):
    return {axis: 1 - lax.axis_index(axis) for axis in axes}


def meet(partners):
    barrier = pltpu.get_barrier_semaphore()
    for axes in partners:
        pl.semaphore_signal(
            barrier, inc=1, device_id=other_of(axes), device_id_type=pl.DeviceIdType.MESH
        )
    pl.semaphore_wait(barrier, len(partners))


class Sender:
    def __init__(self, send_sems, recv_sems):
        self.send_sems, self.recv_sems, self.all, self.left = send_sems, recv_sems, [], []

    def start(self, source, target, axes):
        copy = pltpu.make_async_remote_copy(
            src_ref=source,
            dst_ref=target,
            send_sem=self.send_sems.at[len(self.all)],
            recv_sem=self.recv_sems.at[len(self.all)],
            device_id=other_of(axes),
            device_id_type=pl.DeviceIdType.MESH,
        )
        copy.start()
        self.all.append(copy)
        return copy

    def finish(self):
        for copy in self.all:
            if all(copy is not other for other in self.left):
                copy.wait_send()


def first_kernel(
    squares,
    pair,
    spread,
    small_ref,
    gains_ref,
    q_ref,
    kv_ref,
    gate_ref,
    up_ref,
    down_ref,
    small_out,
    gains_out,
    q_out,
    kv_out,
    gate_out,
    gate_over,
    gate_last,
    up_out,
    down_out,
    staged,
    send_sems,
    recv_sems,
):
    core = lax.axis_index("c")
    places = [place_of(*square) for square in squares]
    me = place_of(*pair)
    sender = Sender(send_sems, recv_sems)
    cols = staged.shape[3]

    small_out[(*places, core)] = small_ref[...]
    gains_out[(*places, core)] = gains_ref[...]
    q_out[tuple(places)] = q_ref[...]
    kv_out[tuple(places)] = kv_ref[...]
    partners = [axes for one, two in squares for axes in ((two,), (one,), (one, two))]
    meet(partners + [pair, ("c",)])

    def blocks(ref, stage, place, tail, lead=()):
        index = lead + (slice(None),) * (stage - len(lead)) + (place,) + tuple(places[stage + 1 :])
        return ref.at[index + tail]

    early = [(small_out, (core,)), (gains_out, (core,))]
    later = [(q_out, ()), (kv_out, ())]

    def send_first(ref, tail):
        mine = blocks(ref, 0, places[0], tail)
        return [sender.start(mine, mine, axes) for axes in partners[:3]]

    def send_square(ref, tail, stage):
        one, two = squares[stage]
        mine = blocks(ref, stage, places[stage], tail)
        return [sender.start(mine, mine, (two,)), sender.start(mine, mine, (one,))]

    def pass_on(ref, tail, stage, copies):
        one, two = squares[stage]
        copies[0].wait_recv()
        half = blocks(ref, stage, places[stage] ^ 1, tail, (slice(0, 2),))
        first = sender.start(half, half, (one,))
        copies[1].wait_recv()
        half = blocks(ref, stage, places[stage] ^ 2, tail, (slice(2, 4),))
        return [first, sender.start(half, half, (two,))]

    def wait(copies):
        for copy in copies:
            copy.wait_recv()

    targets = (gate_out, up_out, down_out)

    def send_columns(away, axes):
        return [
            sender.start(staged.at[which, me ^ away], target.at[me], axes)
            for which, target in enumerate(targets)
        ]

    first = [send_first(*item) for item in early]
    for which, weight_ref in enumerate((gate_ref, up_ref, down_ref)):
        for quarter in range(4):
            staged[which, quarter] = weight_ref[:, quarter * cols : (quarter + 1) * cols]
    columns = [send_columns(1, (pair[1],))]
    for which, target in enumerate(targets):
        target[me] = staged[which, me]
    for copies in first:
        wait(copies)
    sent = [send_square(*item, 1) for item in early]
    first_later = [send_first(*item) for item in later]
    columns.append(send_columns(2, (pair[0],)))
    for stage in range(1, len(squares)):
        if stage > 1:
            sent = [send_square(*item, stage) for item in early]
        passed = [pass_on(*item, stage, copies) for item, copies in zip(early, sent)]
        if stage == 1:
            for copies in first_later:
                wait(copies)
            sent_later = [send_square(*item, 1) for item in later]
            columns.append(send_columns(3, pair))
        for copies in passed:
            wait(copies)
    mine = (slice(None),) * len(squares) + (core,)
    core_sent = [sender.start(ref.at[mine], ref.at[mine], ("c",)) for ref, _ in early]
    for copies in columns:
        copies[0].wait_recv()
    over = [
        sender.start(gate_out, gate_over, (spread[0],)),
        sender.start(gate_out, gate_last, (spread[1],)),
    ]
    for stage in range(1, len(squares)):
        if stage > 1:
            sent_later = [send_square(*item, stage) for item in later]
        passed = [pass_on(*item, stage, copies) for item, copies in zip(later, sent_later)]
        for copies in passed:
            wait(copies)
    wait(core_sent)
    for copies in columns:
        wait(copies[1:])
    wait(over)
    sender.finish()


def first_gather(squares, pair, spread, small, gains, q_up, kv_up, gate, up, down):
    vmem = pl.BlockSpec(memory_space=pltpu.VMEM)
    rows, cols = gate.shape
    lead = (4,) * len(squares)
    copies = 12 + 16 * (len(squares) - 1) + 2 + 9 + 2
    return pl.pallas_call(
        functools.partial(first_kernel, squares, pair, spread),
        out_shape=(
            jax.ShapeDtypeStruct(lead + (2,) + small.shape, bf16),
            jax.ShapeDtypeStruct(lead + (2,) + gains.shape, bf16),
            jax.ShapeDtypeStruct(lead + q_up.shape, bf16),
            jax.ShapeDtypeStruct(lead + kv_up.shape, bf16),
        )
        + (jax.ShapeDtypeStruct((4, rows, cols // 4), bf16),) * 5,
        in_specs=[vmem] * 7,
        out_specs=(vmem,) * 9,
        scratch_shapes=[
            pltpu.VMEM((3, 4, rows, cols // 4), bf16),
            pltpu.SemaphoreType.DMA((copies,)),
            pltpu.SemaphoreType.DMA((copies,)),
        ],
        compiler_params=pltpu.CompilerParams(
            collective_id=0, has_side_effects=True, vmem_limit_bytes=48 << 20
        ),
    )(small, gains, q_up, kv_up, gate, up, down)


def second_kernel(
    squares,
    pair,
    over,
    rows_ref,
    value_ref,
    piece_ref,
    rows_out,
    tokens_out,
    piece_out,
    send_sems,
    recv_sems,
):
    core = lax.axis_index("c")
    places = [place_of(*square) for square in squares]
    me = place_of(*pair)
    one, two = pair
    half = value_ref.shape[0] // 2
    sender = Sender(send_sems, recv_sems)
    rows_out[tuple(places)] = rows_ref[...]
    tokens_out[me, core] = value_ref[...]
    partners = [axes for one_, two_ in squares for axes in ((two_,), (one_,), (one_, two_))]
    meet(partners + [("c",)])

    def blocks(stage, place, lead=()):
        index = lead + (slice(None),) * (stage - len(lead)) + (place,) + tuple(places[stage + 1 :])
        return rows_out.at[index]

    def send_rows(place, axes, rows=slice(None)):
        mine = tokens_out.at[place, core, rows]
        return sender.start(mine, mine, axes)

    mine = blocks(0, places[0])
    first = [sender.start(mine, mine, axes) for axes in partners[:3]]
    near = send_rows(me, (two,))
    wide = send_rows(me, (one,))
    got = [send_rows(me, ("c",))]
    for copy in first:
        copy.wait_recv()
    crossing = sender.start(piece_ref, piece_out, (over,))
    for stage in range(1, len(squares)):
        up, across = squares[stage]
        mine = blocks(stage, places[stage])
        beside = sender.start(mine, mine, (across,))
        above = sender.start(mine, mine, (up,))
        if stage == 1:
            near.wait_recv()
            corner = [send_rows(me ^ 1, (one,), slice(0, half))]
            got.append(send_rows(me ^ 1, ("c",)))
            wide.wait_recv()
            corner.append(send_rows(me ^ 2, (two,), slice(half, 2 * half)))
            got.append(send_rows(me ^ 2, ("c",)))
        beside.wait_recv()
        part = blocks(stage, places[stage] ^ 1, (slice(0, 2),))
        passed = [sender.start(part, part, (up,))]
        above.wait_recv()
        part = blocks(stage, places[stage] ^ 2, (slice(2, 4),))
        passed.append(sender.start(part, part, (across,)))
        if stage == 1:
            for copy in corner:
                copy.wait_recv()
            got.append(send_rows(me ^ 3, ("c",)))
        for copy in passed:
            copy.wait_recv()
    for copy in got:
        copy.wait_recv()
    crossing.wait_recv()
    sender.finish()


def second_gather(squares, pair, over, rows, value, piece):
    vmem = pl.BlockSpec(memory_space=pltpu.VMEM)
    copies = 3 + 4 * (len(squares) - 1) + 9
    gathered, tokens, crossed = pl.pallas_call(
        functools.partial(second_kernel, squares, pair, over),
        out_shape=(
            jax.ShapeDtypeStruct((4,) * len(squares) + rows.shape, bf16),
            jax.ShapeDtypeStruct((4, 2) + value.shape, bf16),
            jax.ShapeDtypeStruct(piece.shape, bf16),
        ),
        in_specs=[vmem] * 3,
        out_specs=(vmem,) * 3,
        scratch_shapes=[pltpu.SemaphoreType.DMA((copies,)), pltpu.SemaphoreType.DMA((copies,))],
        compiler_params=pltpu.CompilerParams(
            collective_id=4, has_side_effects=True, vmem_limit_bytes=40 << 20
        ),
        cost_estimate=pl.CostEstimate(flops=1, transcendentals=0, bytes_accessed=1),
    )(rows, value, piece)
    return gathered.reshape(-1, rows.shape[1]), tokens.reshape(-1, value.shape[1]), crossed


def lay_copies(fsdp, pair, spread, pieces, target, sems):
    copies = []
    for number, piece in enumerate(pieces):
        for block in range(4):
            place = 0
            for axis in fsdp:
                if axis == pair[0]:
                    bit = block >> 1
                elif axis == pair[1]:
                    bit = block & 1
                else:
                    bit = lax.axis_index(axis) ^ ((number >> spread.index(axis)) & 1)
                place = place * 2 + bit
            copies.append(pltpu.make_async_copy(piece.at[block], target.at[place], sems.at[len(copies)]))
    for copy in copies:
        copy.start()
    return copies


def lay_kernel(fsdp, pair, spread, *refs):
    count = 2 ** len(spread)
    target, sems = refs[count:]
    for copy in lay_copies(fsdp, pair, spread, refs[:count], target, sems):
        copy.wait()


def lay(pieces, fsdp, pair, spread):
    rows, cols = pieces[0].shape[1:]
    blocks = 4 * len(pieces)
    out = pl.pallas_call(
        functools.partial(lay_kernel, fsdp, pair, spread),
        out_shape=jax.ShapeDtypeStruct((blocks, rows, cols), bf16),
        in_specs=[pl.BlockSpec(memory_space=pltpu.HBM)] * len(pieces),
        out_specs=pl.BlockSpec(memory_space=pltpu.VMEM),
        scratch_shapes=[pltpu.SemaphoreType.DMA((blocks,))],
        compiler_params=pltpu.CompilerParams(vmem_limit_bytes=32 << 20),
        cost_estimate=pl.CostEstimate(
            flops=0, transcendentals=0, bytes_accessed=4 * blocks * rows * cols
        ),
    )(*pieces)
    return out.reshape(blocks * rows, cols)


def tokens_kernel(pair, value_ref, out_ref, send_sems, recv_sems):
    core = lax.axis_index("c")
    me = place_of(*pair)
    one, two = pair
    half = value_ref.shape[0] // 2
    sender = Sender(send_sems, recv_sems)
    out_ref[me, core] = value_ref[...]
    meet([(two,), (one,), ("c",)])

    def send(place, axes, rows=slice(None)):
        mine = out_ref.at[place, core, rows]
        return sender.start(mine, mine, axes)

    near = send(me, (two,))
    wide = send(me, (one,))
    got = [send(me, ("c",))]
    near.wait_recv()
    far = [send(me ^ 1, (one,), slice(0, half))]
    got.append(send(me ^ 1, ("c",)))
    wide.wait_recv()
    far.append(send(me ^ 2, (two,), slice(half, 2 * half)))
    got.append(send(me ^ 2, ("c",)))
    for copy in far:
        copy.wait_recv()
    got.append(send(me ^ 3, ("c",)))
    for copy in got:
        copy.wait_recv()
    sender.finish()


def tokens_of_chips(value, pair, number):
    rows, cols = value.shape
    vmem = pl.BlockSpec(memory_space=pltpu.VMEM)
    out = pl.pallas_call(
        functools.partial(tokens_kernel, pair),
        out_shape=jax.ShapeDtypeStruct((4, 2, rows, cols), bf16),
        in_specs=[vmem],
        out_specs=vmem,
        scratch_shapes=[pltpu.SemaphoreType.DMA((8,)), pltpu.SemaphoreType.DMA((8,))],
        compiler_params=pltpu.CompilerParams(
            collective_id=number, has_side_effects=True, vmem_limit_bytes=24 << 20
        ),
        cost_estimate=pl.CostEstimate(flops=1, transcendentals=0, bytes_accessed=1),
    )(value)
    return out.reshape(8 * rows, cols)


def merge_kernel(which, parts_ref, out_ref):
    cols = out_ref.shape[1] // 4
    for quarter in range(4):
        out_ref[:, quarter * cols : (quarter + 1) * cols] = parts_ref[0, quarter].astype(f32)


def merge(parts, which):
    rows, cols = parts.shape[2:]
    return pl.pallas_call(
        functools.partial(merge_kernel, which),
        grid=(1,),
        out_shape=jax.ShapeDtypeStruct((rows, 4 * cols), f32),
        in_specs=[pl.BlockSpec((1, 4, rows, cols), lambda i: (which, 0, 0, 0))],
        out_specs=pl.BlockSpec((rows, 4 * cols), lambda i: (0, 0)),
        cost_estimate=pl.CostEstimate(
            flops=0, transcendentals=0, bytes_accessed=24 * rows * cols
        ),
    )(parts)


class Reduction:
    def __init__(self, sender, held, dims, order, buffers, out):
        self.sender, self.held, self.dims, self.order = sender, held, list(dims), list(order)
        self.buffers, self.out = list(buffers), out

    def half(self, at):
        return (slice(None),) * self.dims.index(self.order[0]) + (at,)

    def begin(self):
        axis = self.order[0]
        source = self.held.at[self.half(1 - lax.axis_index(axis))]
        self.copy = self.sender.start(source, self.buffers[0], (axis,))

    def end(self):
        self.copy.wait_recv()
        axis = self.order[0]
        own = self.held[self.half(lax.axis_index(axis))]
        total = own.astype(f32) + self.buffers[0][...].astype(f32)
        self.held = self.buffers.pop(0)
        self.dims.remove(axis)
        self.order.pop(0)
        if self.order:
            self.held[...] = total.astype(bf16)
            self.begin()
        else:
            self.out[...] = total

    def finish(self):
        while self.order:
            self.end()


def halves_of(rows):
    half = rows // 2 // 16 * 16
    return pl.ds(0, half), pl.ds(half, rows - half)


def last_kernel(
    fsdp,
    pair,
    peak_ref,
    small_ref,
    gains_ref,
    q_ref,
    kv_ref,
    out_ref,
    down_ref,
    gate_ref,
    gate_got,
    up_refs,
    small_sum,
    gains_sum,
    q_sum,
    kv_sum,
    out_sum,
    ffn_out,
    peak_out,
    *scratch,
):
    scratch = list(scratch)
    stages = len(fsdp)
    sender = Sender(scratch.pop(), scratch.pop())

    def buffers(count):
        taken = scratch[:count]
        del scratch[:count]
        return taken

    down = list(reversed(fsdp))
    turned = [down[1], down[0]] + down[2:]
    with_core = fsdp + ["c"]
    small = Reduction(sender, small_ref, with_core, ["c"] + turned, buffers(stages + 1), small_sum)
    gains = Reduction(sender, gains_ref, with_core, ["c"] + down, buffers(stages + 1), gains_sum)
    q = Reduction(sender, q_ref, fsdp, down, buffers(stages), q_sum)
    kv = Reduction(sender, kv_ref, fsdp, turned, buffers(stages), kv_sum)
    upward = [down[-2]] + turned[:-2] + [down[-1]]
    outs = []
    for rows, order in zip(halves_of(out_sum.shape[0]), (turned, upward)):
        part = out_ref.at[(slice(None),) * stages + (rows,)]
        outs.append(Reduction(sender, part, fsdp, order, buffers(stages), out_sum.at[rows]))
    over = buffers(2)
    gate_sum, up_sum = buffers(2)
    peaks = buffers(stages)
    me = place_of(*pair)
    row = lax.axis_index(fsdp[0])
    meet([(axis,) for axis in with_core] + [pair])

    def send_columns(which, held):
        ffn_out[which, me] = held[me]
        return [
            sender.start(held.at[me ^ away], ffn_out.at[which, me], axes)
            for away, axes in ((1, (pair[1],)), (2, (pair[0],)), (3, pair))
        ]

    peak_out[...] = peak_ref[...]

    def send_peaks(stage):
        return sender.start(peak_out, peaks[stage], (fsdp[stage],))

    def next_peaks(stage, sent):
        sent.wait()
        sender.left.append(sent)
        peak_out[...] = jnp.maximum(peak_out[...], peaks[stage][...])
        return send_peaks(stage + 1) if stage < stages - 1 else None

    for part in (small, gains, q, outs[0], kv):
        part.begin()
    peak_sent = send_peaks(0)
    crossing = sender.start(down_ref.at[1 - row], over[0], (fsdp[0],))
    outs[1].begin()
    gate_sum[...] = (gate_ref[...].astype(f32) + gate_got[...].astype(f32)).astype(bf16)
    columns = send_columns(1, gate_sum)
    small.end()
    gains.end()
    up_sum[...] = sum(ref[...].astype(f32) for ref in up_refs).astype(bf16)
    peak_sent = next_peaks(0, peak_sent)
    for part in (q, kv, outs[0]):
        part.end()
    def crossed(which, ref, buffer):
        crossing.wait_recv()
        buffer[...] = (ref[row].astype(f32) + buffer[...].astype(f32)).astype(bf16)
        return send_columns(which, buffer)

    columns += crossed(0, down_ref, over[0])
    crossing = sender.start(up_sum.at[1 - row], over[1], (fsdp[0],))
    for stage in range(1, stages):
        peak_sent = next_peaks(stage, peak_sent)
        for part in (outs[1], small, gains, q, kv, outs[0]):
            part.end()
        if stage == 1:
            columns += crossed(2, up_sum, over[1])
    for reduction in (q, kv, outs[0], small, gains, outs[1]):
        reduction.finish()
    for copy in columns:
        copy.wait_recv()
    sender.finish()


def last_scatter(fsdp, pair, peak, small, gains, q, kv, out, down, gate, up):
    vmem = pl.BlockSpec(memory_space=pltpu.VMEM)
    stages = len(fsdp)

    def buffers(array, count, rows=None):
        lead = array.ndim - 2
        block = (rows or array.shape[-2], array.shape[-1])
        return [pltpu.VMEM((2,) * (lead - 1 - i) + block, bf16) for i in range(count)]

    scratch = (
        buffers(small, stages + 1)
        + buffers(gains, stages + 1)
        + buffers(q, stages)
        + buffers(kv, stages)
        + [buf for rows in halves_of(out.shape[-2]) for buf in buffers(out, stages, rows.size)]
        + [pltpu.VMEM(gate[0].shape, bf16)] * 3
        + [pltpu.VMEM(down.shape, bf16)]
        + [pltpu.VMEM(peak.shape, f32)] * stages
    )
    copies = 2 * (stages + 1) + 4 * stages + 2 + 9 + stages
    return pl.pallas_call(
        lambda *refs: last_kernel(fsdp, pair, *refs[:9], refs[9 : 9 + len(up)], *refs[9 + len(up) :]),
        out_shape=tuple(jax.ShapeDtypeStruct(x.shape[-2:], f32) for x in (small, gains, q, kv, out))
        + (
            jax.ShapeDtypeStruct((3,) + gate[0].shape, bf16),
            jax.ShapeDtypeStruct(peak.shape, f32),
        ),
        in_specs=[vmem] * (9 + len(up)),
        out_specs=(vmem,) * 7,
        scratch_shapes=scratch
        + [pltpu.SemaphoreType.DMA((copies,)), pltpu.SemaphoreType.DMA((copies,))],
        compiler_params=pltpu.CompilerParams(
            collective_id=2, has_side_effects=True, vmem_limit_bytes=60 << 20
        ),
    )(peak, small, gains, q, kv, out, down, *gate, *up)


def shards(
    fsdp,
    hidden_in,
    seq_ids,
    block_ids,
    clip_limit,
    cotangent,
    q_down,
    kv_down,
    q_up,
    kv_up,
    out_proj,
    gate_proj,
    up_proj,
    down_proj,
    in_gain,
    q_gain,
    kv_gain,
    post_gain,
):
    tokens_here, width = hidden_in.shape
    seq_row = seq_ids[0]
    block_row = block_ids[0]
    group = seq_row.shape[0]
    heads = q_up.shape[1] // (NOPE + ROPE)
    score_scale = 1.0 / math.sqrt(NOPE + ROPE)
    core = lax.axis_index("c")
    first_row = core * tokens_here
    wide, near = fsdp[1], fsdp[-1]
    pair = (wide, near)
    spread = [axis for axis in fsdp if axis not in pair]
    squares = [(fsdp[i], fsdp[i + 1]) for i in range(0, len(fsdp), 2)]
    at_wide, at_near = lax.axis_index(wide), lax.axis_index(near)
    chips = tuple(fsdp)
    count = 2 ** len(fsdp)

    small_rows = q_down.shape[0]
    q_rank = q_down.shape[1]
    small_cols = q_rank + kv_down.shape[1]

    def row(value):
        return jnp.pad(value, ((0, 0), (0, TILE - value.shape[1])))[:, None, :]

    def rows_of(*values):
        held = jnp.concatenate([row(value) for value in values], axis=1)
        return jnp.pad(held, ((0, 0), (0, 8 - len(values)), (0, 0)))

    small = jnp.concatenate([q_down, kv_down], axis=1)
    gains = rows_of(in_gain[None], post_gain[None], q_gain[None], kv_gain[None])[0]
    q_up_wide = jnp.pad(
        q_up.reshape(-1, heads, NOPE + ROPE), ((0, 0), (0, 0), (0, TILE - NOPE - ROPE))
    ).reshape(-1, heads * TILE)
    small_all, gains_all, q_up_all, kv_up_all, *pieces = first_gather(
        squares, pair, spread, small, gains, q_up_wide, kv_up, gate_proj, up_proj, down_proj
    )
    down_full = small_all.reshape(-1, small_cols)
    q_up_full = q_up_all.reshape(-1, heads * TILE)
    kv_up_full = kv_up_all.reshape(-1, kv_up.shape[1])
    devices = 2 * count

    def gain(at, size):
        return gains_all.reshape(devices, 8, TILE)[:, at, :size].reshape(-1).astype(f32)

    in_float = gain(0, in_gain.shape[0])
    post_float = gain(1, post_gain.shape[0])
    q_gain_float = gain(2, q_gain.shape[0])
    kv_gain_float = gain(3, kv_gain.shape[0])

    cot_float = cotangent.astype(f32)

    def over(pieces, axis, *ready):
        return [swap(after(piece, *ready), axis) for piece in pieces]

    def exchange(held, dims, axis):
        at, dim = lax.axis_index(axis), dims.index(axis)
        return swap(pick(held, 1 - at, dim), axis), pick(held, at, dim)

    def sum_of_chips(held):
        held = held.reshape(2, 2, tokens_here, width)
        return square_scatter(held, wide, near, 0).reshape(tokens_here, width)

    def core_both(value):
        return both(value, swap(value, "c"), "c", 0)

    def core_sum(value):
        def rows(at):
            return lax.dynamic_slice_in_dim(value, at * tokens_here, tokens_here)

        return rows(core) + swap(rows(1 - core), "c")

    x_float = hidden_in.astype(f32)
    x_normed = rms_scale(x_float, in_float).astype(bf16)
    pre = jnp.dot(x_normed, down_full, preferred_element_type=f32)
    q_pre = pre[:, :q_rank]
    c_lat_pre = pre[:, q_rank : q_rank + KVR]
    c_rot_pre = pre[:, q_rank + KVR :]
    own_cos, own_sin = angles(seq_row, first_row, tokens_here)
    q_latent = rms_scale(q_pre, q_gain_float).astype(bf16)
    kv_latent = rms_scale(c_lat_pre, kv_gain_float).astype(bf16)
    key_rot = rotate(c_rot_pre, own_cos, own_sin).astype(bf16)
    key_rot = jnp.pad(key_rot, ((0, 0), (NOPE, TILE - NOPE - ROPE)))
    latents = core_both(jnp.concatenate([q_latent, kv_latent, key_rot], axis=1))
    q_lat_all = latents[:, :q_rank]
    kv_lat_all = latents[:, q_rank : q_rank + KVR]
    key_rot_all = latents[:, q_rank + KVR :]
    all_cos, all_sin = angles(seq_row, 0, group)
    q_full = jnp.dot(q_lat_all, q_up_full, preferred_element_type=f32)
    kv_full = jnp.dot(kv_lat_all, kv_up_full, preferred_element_type=f32).astype(bf16)
    allowed = (seq_row[None, :] == seq_row[:, None]) & (block_row[:, None] <= block_row[None, :])
    bias = jnp.where(allowed, 0.0, -1e30).astype(f32)
    axes = list(spread)
    gate_held, gate_over, gate_last, up_held, down_held = pieces
    gate_pieces = [gate_held, gate_over, gate_last, swap(gate_over, axes[1])]
    for axis in axes[2:]:
        gate_pieces += over(gate_pieces, axis)
    up_pieces = [swap(up_held, axes[0]), swap(up_held, axes[1])]
    attn, queries, log_total, local_peak = attend(
        q_full, kv_full, key_rot_all, tables(all_cos, all_sin), bias, score_scale
    )
    d_ffn = (resid_scale * cot_float).astype(bf16)
    out_full, d_ffn_all, down_over = second_gather(
        squares, pair, axes[0], after(out_proj, attn), d_ffn, down_held
    )
    attn, out_full, down_over, *early = lax.optimization_barrier(
        (attn, out_full, down_over, *up_pieces, *gate_pieces)
    )
    up_pieces, gate_pieces = early[:2], early[2:]
    branch = core_sum(contract(attn, out_full, 1, 1))
    mid = x_float + resid_scale * branch
    mid_normed = rms_scale(mid, post_float).astype(bf16)
    gate_full = lay(gate_pieces, fsdp, pair, spread)
    mid_all = tokens_of_chips(after(mid_normed, gate_full), pair, 1)
    up_pieces = [up_held, *up_pieces, swap(after(up_pieces[0], attn), axes[1])]
    down_last = swap(after(down_held, attn), axes[1])
    mid_all, down_last, *up_pieces = lax.optimization_barrier((mid_all, down_last, *up_pieces))
    down_pieces = [down_held, down_over, down_last, swap(after(down_over, mid_all), axes[1])]
    for axis in axes[2:]:
        up_pieces += over(up_pieces, axis)
        down_pieces += over(down_pieces, axis)
    up_full = lay(up_pieces, fsdp, pair, spread)
    gate = jnp.dot(mid_all, gate_full, preferred_element_type=f32)
    up_value = jnp.dot(mid_all, up_full, preferred_element_type=f32)
    down_proj_full = lay(down_pieces, fsdp, pair, spread)
    sigmoid = jax.nn.sigmoid(gate)
    silu_value = gate * sigmoid
    act = (silu_value * up_value).astype(bf16)

    d_act = jnp.dot(d_ffn_all, down_proj_full, preferred_element_type=f32)
    d_gate = (d_act * up_value * (sigmoid * (1.0 + gate * (1.0 - sigmoid)))).astype(bf16)
    d_up = (d_act * silu_value).astype(bf16)
    dims = list(fsdp)
    first, last = spread[0], spread[-1]

    def added(parts):
        return (parts[0].astype(f32) + parts[1].astype(f32)).astype(bf16)

    def inner(held):
        left = [axis for axis in dims if axis != last]
        for axis in reversed(spread[1:-1]):
            held = added(exchange(held, left, axis))
            left.remove(axis)
        return held

    def begin(left, right, *ready):
        keep, send = grad_halves(left, right, width // count, last)
        shape = [2] * (len(fsdp) - 1) + [width // count, -1]
        return swap(after(send, *ready), last).reshape(shape), keep.reshape(shape), keep

    def cross(held):
        return exchange(held, [first, *pair], first)

    *down_parts, down_grad = begin(d_ffn_all, act)
    d_gate_late, _ = lax.optimization_barrier((d_gate, down_grad))
    gate_keep, gate_send = grad_halves(mid_all, d_gate_late, width // count, last)
    d_up_late, d_gate_late, _ = lax.optimization_barrier((d_up, d_gate, gate_keep))
    d_mid_held = core_features(
        tokens_here, 3, (d_gate_late, gate_full), (d_up_late, up_full)
    )
    d_mid_held, *down_parts = lax.optimization_barrier((d_mid_held, *down_parts))
    d_mid_normed = sum_of_chips(d_mid_held)
    mid_late, gate_send, _ = lax.optimization_barrier((mid_all, gate_send, d_mid_held))
    shape = [2] * (len(fsdp) - 1) + [width // count, -1]
    gate_parts = (swap(gate_send, last).reshape(shape), gate_keep.reshape(shape))
    down_held = inner(added(down_parts))
    *up_parts, up_grad = begin(mid_late, d_up, gate_parts[0])
    ffn_part = features((after(act, up_grad), down_proj_full))
    post_pull = jax.vjp(rms_scale, mid, post_float)[1]
    d_mid_normed, *early = lax.optimization_barrier(
        (d_mid_normed, down_held, *gate_parts, ffn_part)
    )
    down_held, gate_parts, ffn_part = early[0], early[1:3], early[3]
    d_mid_norm, post_grad = post_pull(d_mid_normed)
    ffn = lax.psum_scatter(
        ffn_part, (wide, near, "c"), scatter_dimension=0, tiled=True
    )
    layer_out = (mid + resid_scale * ffn.astype(f32)).astype(bf16)
    d_mid = cot_float + d_mid_norm
    d_branch = (resid_scale * d_mid).astype(bf16)
    d_branch_all = core_both(d_branch)
    d_attn = jnp.dot(d_branch_all, out_full, preferred_element_type=f32).astype(bf16)
    gate_parts = cross(inner(added(gate_parts)))
    d_q, d_kv, d_rot_part = attend_back(
        queries,
        kv_full,
        d_attn,
        log_total,
        key_rot_all,
        tables(all_cos, -all_sin),
        bias,
        score_scale,
    )
    q_up_grad = heads_grad(q_lat_all, d_q)
    out_grad = plain_grad(after(d_branch_all, q_up_grad), attn)
    d_q_lat_part = contract(d_q, q_up_full, 1, 1)
    d_kv_lat_part = contract(d_kv, kv_up_full, 1, 1)
    d_q_lat_part, d_kv_lat_part, d_kv, out_grad, *early = lax.optimization_barrier(
        (d_q_lat_part, d_kv_lat_part, d_kv, out_grad, *gate_parts, *up_parts)
    )
    gate_parts, up_parts = early[:2], early[2:]
    kv_up_grad = rows_first(contract(kv_lat_all, d_kv, 0, 0).astype(bf16))
    d_latents = core_sum(jnp.concatenate([d_q_lat_part, d_kv_lat_part, d_rot_part], axis=1))
    q_pull = jax.vjp(rms_scale, q_pre, q_gain_float)[1]
    d_q_pre, q_gain_grad = q_pull(d_latents[:, :q_rank])
    kv_pull = jax.vjp(rms_scale, c_lat_pre, kv_gain_float)[1]
    d_c_lat, kv_gain_grad = kv_pull(d_latents[:, q_rank : q_rank + KVR])
    d_key_rot = d_latents[:, q_rank + KVR + NOPE : q_rank + KVR + NOPE + ROPE]
    d_pre = jnp.concatenate(
        [d_q_pre, d_c_lat, rotate(d_key_rot, own_cos, -own_sin)], axis=-1
    ).astype(bf16)
    down_grads = rows_first(contract(x_normed, d_pre, 0, 0).astype(bf16))
    d_x_normed = contract(d_pre, down_full, 1, 1)
    in_pull = jax.vjp(rms_scale, x_float, in_float)[1]
    d_x_norm, in_grad = in_pull(d_x_normed)
    input_grad = d_mid + d_x_norm

    rows_here = width // count
    block = (4, rows_here, gate_parts[0].shape[-1])
    if len(spread) > 2:
        up_parts = (inner(added(up_parts)),)
    ffn_held = [
        down_held.reshape((2,) + block),
        tuple(part.reshape(block) for part in gate_parts),
        tuple(part.reshape((2,) + block) for part in up_parts),
    ]
    gain_grads = rows_of(
        *(grad.reshape(devices, -1) for grad in (in_grad, post_grad, q_gain_grad, kv_gain_grad))
    ).astype(bf16)

    def blocks(grad, lead):
        return grad.reshape([2] * lead + [grad.shape[0] // 2**lead, -1])

    small_out, gain_out, q_up_out, kv_up_out, out_out, ffn_cols, peak_all = last_scatter(
        fsdp,
        pair,
        local_peak,
        blocks(down_grads, len(fsdp) + 1),
        gain_grads.reshape([2] * (len(fsdp) + 1) + [8, TILE]),
        blocks(q_up_grad, len(fsdp)),
        blocks(kv_up_grad, len(fsdp)),
        blocks(out_grad, len(fsdp)),
        *ffn_held,
    )
    down_out, gate_out, up_out = (merge(ffn_cols, which) for which in range(3))
    peaks = peak_all[0, :heads]
    limit = clip_limit[0]
    factors = limit / jnp.maximum(peaks, limit)
    root = jnp.sqrt(factors)
    q_cols = jnp.concatenate(
        [
            jnp.broadcast_to(root[:, None], (heads, NOPE)),
            jnp.broadcast_to(factors[:, None], (heads, ROPE)),
        ],
        axis=1,
    ).reshape(heads * (NOPE + ROPE))
    kv_cols = jnp.concatenate(
        [jnp.broadcast_to(root[:, None], (heads, NOPE)), jnp.ones((heads, VD), f32)], axis=1
    ).reshape(heads * (NOPE + VD))
    q_clipped = (q_up.astype(f32) * q_cols[None, :]).astype(bf16)
    kv_clipped = (kv_up.astype(f32) * kv_cols[None, :]).astype(bf16)
    return (
        layer_out,
        input_grad,
        small_out[:, :q_rank],
        small_out[:, q_rank:],
        q_up_out,
        kv_up_out,
        out_out,
        gate_out,
        up_out,
        down_out,
        gain_out[0, : in_gain.shape[0]],
        gain_out[2, : q_gain.shape[0]],
        gain_out[3, : kv_gain.shape[0]],
        gain_out[1, : post_gain.shape[0]],
        q_clipped,
        kv_clipped,
        peaks,
        factors,
    )


def solution(mesh):
    bits = mesh.shape["fsdp"].bit_length() - 1
    fsdp = [f"f{i}" for i in range(bits)]
    fine = Mesh(mesh.devices.reshape((2,) * (bits + 1)), tuple(fsdp) + ("c",))
    split = tuple(fsdp)
    whole = split + ("c",)
    return jax.shard_map(
        functools.partial(shards, fsdp),
        mesh=fine,
        in_specs=(
            P(whole, None),
            P(split, None),
            P(split, None),
            P(),
            P(whole, None),
            P(whole, None),
            P(whole, None),
            P(split, "c"),
            P(split, "c"),
            P(split, "c"),
            P(split, "c"),
            P(split, "c"),
            P(split, "c"),
            P(whole),
            P(whole),
            P(whole),
            P(whole),
        ),
        out_specs=(
            P(whole, None),
            P(whole, None),
            P(whole, None),
            P(whole, None),
            P(split, "c"),
            P(split, "c"),
            P(split, "c"),
            P(split, "c"),
            P(split, "c"),
            P(split, "c"),
            P(whole),
            P(whole),
            P(whole),
            P(whole),
            P(split, "c"),
            P(split, "c"),
            P("c"),
            P("c"),
        ),
        check_vma=False,
    )
```
